256 devices in a mesh: head: 4 (over x), blk: 64 (over y, z, core).
Axes of the slice: x: 4, y: 4, z: 8, core: 2. Of those that a mesh axis runs over, the one named last changes fastest.
Arguments:
- doc_x: bfloat16 [65536, 1024], P('blk'), may hold values from -6 to 6
- doc_seg: int32 [65536], P('blk'), may hold values from 0 to 1023, as said below
- doc_query: int32 [1024], replicated, may hold values from 0 to 7
- doc_var: int32 [65536], P('blk'), may hold values from 0 to 7
- query_len: int32 [8], replicated, may hold values from 256 to 4096, as said below
- block_perm: int32 [64], replicated, may hold values from 0 to 63, each once
- cache_k: bfloat16 [32768, 1024], P('blk', 'head'), may hold values from -164 to 164
- cache_v: bfloat16 [32768, 1024], P('blk', 'head'), may hold values from -6 to 6
- cache_var: int32 [32768], P('blk'), may hold values from 0 to 7
- w_query: bfloat16 [1024, 1024], P(None, 'head'), may hold values from -0.1875 to 0.1875
- w_key: bfloat16 [1024, 1024], P(None, 'head'), may hold values from -0.5 to 0.5
- w_value: bfloat16 [1024, 1024], P(None, 'head'), may hold values from -0.1875 to 0.1875
- w_out: bfloat16 [1024, 1024], P('head'), may hold values from -0.1875 to 0.1875
- var_bias: float32 [2, 16], P(None, 'head'), may hold values from -1 to 1
- norm_gain: float32 [1024], replicated, may hold values from 0.1 to 1.9
- readout: float32 [1024], replicated, may hold values from -1.5 to 1.5
Outputs:
- update: float32 [65536, 1024], P('blk', 'head')
- pooled: float32 [1024], P('blk')
The draws below stay inside these ranges and needn't reach their ends.
Inputs may be any that keep to these rules, and one draw needn't show every extreme that they name: `doc_seg`: index i of blk holds documents i * 16 to (i + 1) * 16 - 1 whole; its 1024 tokens form 8 runs of 128 tokens, run j holding its documents 2j and 2j + 1, both of one query, and the 8 runs of one index belong to 8 different queries. query_len[0] = 4096.
All inputs are finite; a program needn't handle non-finite values.
Results may differ from the reference program's by a relative error of at most 0.012.
The reference program's roundings to bfloat16 on the way (of `query_rot`, `key_rot`, `value_proj` and `attended`) count: a program that leaves them out, or rounds other values in their place, can miss the bound.
Values may be sent and summed in bfloat16 or wider, within the bound.
A program may use at most 128 MiB of HBM per device.

```python
import jax
import jax.numpy as jnp
from jax import lax

D = 1024
H = 16
DH = 64
CROWS = 512
SLOT = 128
QUERIES = 8
VARIATES = 8
BPQ = 8
DOC_DEV = 1024
DOCS_DEV = 16
BLOCKS = 64
CACHE_ROWS = 32768
DOC_TOK = 65536
DOCS = 1024


def document_plan(key):
    plan_key = jax.random.fold_in(key, 101)
    cut_key, order_key = jax.random.split(plan_key)
    device_count = DOC_TOK // DOC_DEV
    cut_points = jax.random.randint(cut_key, (device_count, QUERIES), SLOT // 4, SLOT - SLOT // 4 + 1)
    order_keys = jax.random.split(order_key, device_count)
    slot_orders = jax.vmap(lambda one_key: jax.random.permutation(one_key, QUERIES))(order_keys)
    return (cut_points, slot_orders)


def draw_doc_seg(key, part):
    cut_points, slot_orders = document_plan(key)
    device_count = DOC_TOK // DOC_DEV
    offset = jnp.arange(SLOT, dtype=jnp.int32)
    second = (offset[None, None, :] >= cut_points[:, :, None]).astype(jnp.int32)
    slot_ids = 2 * jnp.arange(QUERIES, dtype=jnp.int32)[None, :, None]
    device_ids = DOCS_DEV * jnp.arange(device_count, dtype=jnp.int32)[:, None, None]
    return (device_ids + slot_ids + second).reshape(DOC_TOK).astype(jnp.int32)


def draw_doc_query(key, part):
    cut_points, slot_orders = document_plan(key)
    return jnp.repeat(slot_orders, 2, axis=1).reshape(DOCS).astype(jnp.int32)


def draw_query_len(key, part):
    drawn = jax.random.randint(key, (QUERIES,), CROWS // 2, BPQ * CROWS + 1)
    return drawn.at[0].set(BPQ * CROWS).astype(jnp.int32)


def draw_cache_k(key, part):
    first_key = jax.random.fold_in(jax.random.fold_in(key, 11), 0)
    values = jnp.clip(jax.random.normal(first_key, (CACHE_ROWS, D), jnp.float32) * 2.5, -15.0, 15.0)
    return values.astype(jnp.bfloat16)


def with_ends(values, own_key, smallest, largest):
    index_at = [jax.random.randint(jax.random.fold_in(own_key, axis), (), 0, length) for axis, length in enumerate(values.shape)]
    main_axis = values.shape.index(max(values.shape))
    neighbour = index_at[:main_axis] + [(index_at[main_axis] + 1) % values.shape[main_axis]] + index_at[main_axis + 1:]
    return values.at[tuple(index_at)].set(smallest).at[tuple(neighbour)].set(largest)


def steps_of(own_key, dims, cuts, low, largest):
    def one(axis_at, shards_of):
        steps = jax.random.uniform(jax.random.fold_in(jax.random.fold_in(own_key, 6), axis_at), (shards_of,), jnp.float32, low / len(cuts), largest / len(cuts))
        return jnp.repeat(jnp.exp(steps), dims[axis_at] // shards_of).reshape((-1,) + (1,) * (len(dims) - axis_at - 1))

    loudness = one(*cuts[0])
    for cut in cuts[1:]:
        loudness = loudness * one(*cut)
    return loudness


def scatter_about(key, shape, spread, reach, pieces=(), kind=jnp.bfloat16):
    level = steps_of(key, shape, pieces, -0.22, 0.18) if pieces else 1.0
    values = jax.random.normal(key, shape, jnp.float32) * spread * level
    return jnp.minimum(jnp.maximum(values, -reach), reach).astype(kind)


def setup_inputs(seed: int = 0) -> dict:
    seeds = jax.random.split(jax.random.key(seed), 17)
    doc_x = scatter_about(seeds[0], (DOC_TOK, D), 1.0, 6.0, ((0, 64),))
    doc_seg = draw_doc_seg(jax.random.fold_in(seeds[16], 71), 0)
    doc_query = draw_doc_query(jax.random.fold_in(seeds[16], 71), 0)
    doc_var = with_ends(jax.random.randint(seeds[3], (DOC_TOK,), 0, VARIATES), jax.random.fold_in(seeds[3], 1), 0, VARIATES - 1).astype(jnp.int32)
    query_len = draw_query_len(jax.random.fold_in(seeds[16], 71), 0)
    block_perm = jax.random.permutation(seeds[5], BLOCKS).astype(jnp.int32)
    cache_k = draw_cache_k(jax.random.fold_in(seeds[16], 71), 0)
    cache_v = scatter_about(seeds[7], (CACHE_ROWS, D), 1.0, 6.0, ((0, 64), (1, 4)))
    cache_var = with_ends(jax.random.randint(seeds[8], (CACHE_ROWS,), 0, VARIATES), jax.random.fold_in(seeds[8], 1), 0, VARIATES - 1).astype(jnp.int32)
    w_query = scatter_about(seeds[9], (D, D), D ** -0.5, 0.1875, ((1, 4),))
    w_key = scatter_about(seeds[10], (D, D), (D // 9) ** -0.5, 0.5, ((1, 4),))
    w_value = scatter_about(seeds[11], (D, D), D ** -0.5, 0.1875, ((1, 4),))
    w_out = scatter_about(seeds[12], (D, D), D ** -0.5, 0.1875, ((0, 4),))
    var_bias = jnp.clip(jax.random.uniform(seeds[13], (2, H), jnp.float32, -1.0, 1.0) * steps_of(seeds[13], (2, H), ((1, 4),), -0.4, 0.0), -1.0, 1.0)
    norm_gain = jnp.clip(1.0 + 0.18 * jax.random.normal(seeds[14], (D,), jnp.float32), 0.1, 1.9)
    readout = scatter_about(seeds[15], (D,), (D // 64) ** -0.5, 1.5, (), jnp.float32)
    return {"doc_x": doc_x, "doc_seg": doc_seg, "doc_query": doc_query, "doc_var": doc_var, "query_len": query_len, "block_perm": block_perm, "cache_k": cache_k, "cache_v": cache_v, "cache_var": cache_var, "w_query": w_query, "w_key": w_key, "w_value": w_value, "w_out": w_out, "var_bias": var_bias, "norm_gain": norm_gain, "readout": readout}


def rotary(projected, positions):
    row_count = projected.shape[0]
    head_count = projected.shape[1] // DH
    half_size = DH // 2
    shaped = projected.reshape(row_count, head_count, DH)
    frequency = 10000.0 ** (-jnp.arange(half_size, dtype=jnp.float32) / half_size)
    angles = positions.astype(jnp.float32)[:, None] * frequency[None, :]
    cosine = jnp.cos(angles)[:, None, :]
    sine_part = jnp.sin(angles)[:, None, :]
    first_half = shaped[:, :, :half_size]
    second_half = shaped[:, :, half_size:]
    turned = jnp.concatenate([first_half * cosine - second_half * sine_part, second_half * cosine + first_half * sine_part], axis=2)
    return turned.reshape(row_count, head_count * DH)

def softmax_part(scores, allowed):
    scores = jnp.where(allowed, scores, -1e+30)
    peak = lax.optimization_barrier(jnp.max(scores, axis=-1))
    weights = jnp.where(allowed, jnp.exp(scores - peak[..., None]), 0.0)
    return (peak, lax.optimization_barrier(jnp.sum(weights, axis=-1)), weights.astype(jnp.bfloat16))

def reference(doc_x, doc_seg, doc_query, doc_var, query_len, block_perm, cache_k, cache_v, cache_var, w_query, w_key, w_value, w_out, var_bias, norm_gain, readout):
    token_count = doc_x.shape[0]
    doc_count = doc_query.shape[0]
    lengths = jax.ops.segment_sum(jnp.ones((token_count,), jnp.int32), doc_seg, num_segments=doc_count).astype(jnp.int32)
    starts = (jnp.cumsum(lengths) - lengths).astype(jnp.int32)
    tok_query = doc_query[doc_seg].astype(jnp.int32)
    positions = (query_len[tok_query] + jnp.arange(token_count, dtype=jnp.int32) - starts[doc_seg]).astype(jnp.int32)
    query_rot = rotary(jnp.dot(doc_x, w_query, preferred_element_type=jnp.float32), positions).astype(jnp.bfloat16)
    key_rot = rotary(jnp.dot(doc_x, w_key, preferred_element_type=jnp.float32), positions).astype(jnp.bfloat16)
    value_proj = jnp.dot(doc_x, w_value, preferred_element_type=jnp.float32).astype(jnp.bfloat16)

    def heads_first(array):
        return array.reshape(array.shape[0], H, DH).transpose(1, 0, 2)
    slot_total = token_count // SLOT
    seg_slots = doc_seg.reshape(slot_total, SLOT)
    var_slots = doc_var.reshape(slot_total, SLOT)
    self_allowed = seg_slots[:, :, None] == seg_slots[:, None, :]
    var_equal = var_slots[:, :, None] == var_slots[:, None, :]

    def self_head(head_inputs):
        head_q, head_k, head_v, bias_pair = head_inputs
        slot_q = head_q.reshape(slot_total, SLOT, DH).astype(jnp.float32)
        slot_k = head_k.reshape(slot_total, SLOT, DH).astype(jnp.float32)
        slot_v = head_v.reshape(slot_total, SLOT, DH).astype(jnp.float32)
        scores = jnp.einsum('gtd,gsd->gts', slot_q, slot_k) * 0.125
        scores = scores + jnp.where(var_equal, bias_pair[0], bias_pair[1])
        peak, total_weight, weights = softmax_part(scores, self_allowed)
        sums = jnp.einsum('gts,gsd->gtd', weights.astype(jnp.float32), slot_v)
        return (peak.reshape(token_count), total_weight.reshape(token_count), sums.reshape(token_count, DH))
    self_peak, self_total, self_sum = lax.map(self_head, (heads_first(query_rot), heads_first(key_rot), heads_first(value_proj), var_bias.T))
    token_order = jnp.argsort(tok_query, stable=True).astype(jnp.int32)
    restore = jnp.argsort(token_order).astype(jnp.int32)
    per_query = token_count // QUERIES
    holder = jnp.argsort(block_perm).astype(jnp.int32)
    query_rows = BPQ * CROWS
    query_keys = cache_k.reshape(BLOCKS, CROWS, D)[holder].reshape(QUERIES, query_rows, H, DH)
    query_values = cache_v.reshape(BLOCKS, CROWS, D)[holder].reshape(QUERIES, query_rows, H, DH)
    query_cvar = cache_var.reshape(BLOCKS, CROWS)[holder].reshape(QUERIES, query_rows)
    row_valid = jnp.arange(query_rows, dtype=jnp.int32)[None, :] < query_len[:, None]
    sorted_q = query_rot[token_order].reshape(QUERIES, per_query, H, DH)
    sorted_var = doc_var[token_order].reshape(QUERIES, per_query)
    block_size = 512 if per_query % 512 == 0 else per_query
    block_count = per_query // block_size

    def one_query(query_inputs):
        keys, values, cvar, valid, tok_q, tok_var = query_inputs

        def one_head(head_inputs):
            head_k, head_v, head_q, bias_pair = head_inputs

            def one_block(block_inputs):
                block_q, block_var = block_inputs
                scores = jnp.dot(block_q, head_k.T, preferred_element_type=jnp.float32) * 0.125
                scores = scores + jnp.where(block_var[:, None] == cvar[None, :], bias_pair[0], bias_pair[1])
                allowed = jnp.broadcast_to(valid[None, :], scores.shape)
                peak, total_weight, weights = softmax_part(scores, allowed)
                return (peak, total_weight, jnp.dot(weights, head_v, preferred_element_type=jnp.float32))
            peaks, totals, sums = lax.map(one_block, (head_q.reshape(block_count, block_size, DH), tok_var.reshape(block_count, block_size)))
            return (peaks.reshape(per_query), totals.reshape(per_query), sums.reshape(per_query, DH))
        return lax.map(one_head, (keys.transpose(1, 0, 2), values.transpose(1, 0, 2), tok_q.transpose(1, 0, 2), var_bias.T))
    cache_peak, cache_total, cache_sum = lax.map(one_query, (query_keys, query_values, query_cvar, row_valid, sorted_q, sorted_var))
    cache_peak = cache_peak.transpose(1, 0, 2).reshape(H, token_count)[:, restore]
    cache_total = cache_total.transpose(1, 0, 2).reshape(H, token_count)[:, restore]
    cache_sum = cache_sum.transpose(1, 0, 2, 3).reshape(H, token_count, DH)[:, restore]
    peak = jnp.maximum(cache_peak, self_peak)
    cache_factor = jnp.exp(cache_peak - peak)
    self_factor = jnp.exp(self_peak - peak)
    numerator = cache_sum * cache_factor[..., None] + self_sum * self_factor[..., None]
    denominator = cache_total * cache_factor + self_total * self_factor
    attended = (numerator / denominator[..., None]).transpose(1, 0, 2).reshape(token_count, H * DH).astype(jnp.bfloat16)
    update_sum = jnp.dot(attended, w_out, preferred_element_type=jnp.float32)
    hidden = doc_x.astype(jnp.float32) + update_sum
    square_sum = lax.optimization_barrier(jnp.sum(hidden * hidden, axis=1))
    weighted = lax.optimization_barrier(jnp.sum(hidden * norm_gain * readout, axis=1))
    token_score = weighted * lax.rsqrt(square_sum / D + 1e-06)
    pooled = jax.ops.segment_sum(token_score, doc_seg, num_segments=doc_count) / lengths.astype(jnp.float32)
    return (update_sum, pooled)
```

```python
import functools

import jax
import jax.numpy as jnp
from jax import lax
from jax.experimental import pallas as pl
from jax.experimental.pallas import tpu as pltpu
from jax.sharding import Mesh, PartitionSpec as P

DH = 64
F32 = jnp.float32
BF16 = jnp.bfloat16
NEG = -1e30
ANY = pl.ANY
BLK = ("y", "z", "c")


def remote(src, dst, send_sem, recv_sem, **device):
    return pltpu.make_async_remote_copy(
        src_ref=src,
        dst_ref=dst,
        send_sem=send_sem,
        recv_sem=recv_sem,
        device_id=device,
        device_id_type=pl.DeviceIdType.MESH,
    )


def each(count, first, step):
    def run(i, carry):
        step(i)
        return carry

    lax.fori_loop(first, count, run, 0)


def local_kernel(order, x_ref, wq_ref, wk_ref, wv_ref, cos_ref, sin_ref, qf_ref, kf_ref,
                 q_out, o_out, st_out, wide):
    x = x_ref[...]
    rows, cols = x.shape[0], wq_ref.shape[1]
    lane = lax.broadcasted_iota(jnp.int32, (rows, cols), 1)
    low = (lane % DH) < DH // 2
    cosine = jnp.concatenate([cos_ref[...]] * (cols // 128), axis=1)
    sine = jnp.concatenate([sin_ref[...]] * (cols // 128), axis=1)

    def turn(w_ref):
        a = jnp.dot(x, w_ref[...], preferred_element_type=F32)
        other = jnp.where(low, pltpu.roll(a, cols - DH // 2, 1), pltpu.roll(a, DH // 2, 1))
        return a * cosine + other * sine

    q = (turn(wq_ref) * 0.125).astype(BF16)
    k = turn(wk_ref).astype(BF16)
    v = jnp.dot(x, wv_ref[...], preferred_element_type=F32).astype(BF16)
    q_out[0] = q
    kf = kf_ref[...]
    half = lax.broadcasted_iota(jnp.int32, (rows, 128), 1)
    stats = jnp.zeros((rows, 128), F32)
    for pair in range(cols // 128):
        tile = slice(pair * 128, pair * 128 + 128)
        outs = []
        for odd in range(2):
            mine = (half >= DH) if odd else (half < DH)
            qa = jnp.where(mine, q[:, tile], qf_ref[:, tile])
            ka = jnp.where(mine, k[:, tile], kf)
            s = lax.dot_general(qa, ka, (((1,), (1,)), ((), ())), preferred_element_type=F32)
            m = jnp.max(s, axis=1, keepdims=True)
            p = jnp.exp(s - m)
            l = jnp.sum(p, axis=1, keepdims=True)
            o = jnp.dot(p.astype(BF16), v[:, tile], preferred_element_type=F32)
            outs.append(o / l)
            head = 2 * pair + odd
            stats = jnp.where(half == head, m, jnp.where(half == 4 + head, l, stats))
        o_out[0, :, tile] = jnp.where(half < DH, outs[0], outs[1])
    wide[...] = stats
    st_out[0] = jnp.transpose(wide[...])[:8]


def cache_kernel(q_ref, qf_ref, k_ref, kf_ref, v_ref, o_ref, st_ref, wide):
    pair, tile, odd = pl.program_id(0), pl.program_id(1), pl.program_id(2)
    rows, keys = q_ref.shape[0], k_ref.shape[0]
    lane_q = lax.broadcasted_iota(jnp.int32, (rows, 128), 1)
    lane_k = lax.broadcasted_iota(jnp.int32, (keys, 128), 1)
    mine_q = (lane_q // DH) == odd
    mine_k = (lane_k // DH) == odd
    qa = jnp.where(mine_q, q_ref[...], qf_ref[...])
    ka = jnp.where(mine_k, k_ref[...], kf_ref[...])
    s = lax.dot_general(qa, ka, (((1,), (1,)), ((), ())), preferred_element_type=F32)
    m = jnp.max(s, axis=1, keepdims=True)
    p = jnp.exp(s - m)
    l = jnp.sum(p, axis=1, keepdims=True)
    o = jnp.dot(p.astype(BF16), v_ref[...], preferred_element_type=F32) / l

    @pl.when(odd == 0)
    def _():
        o_ref[...] = o.astype(BF16)

    @pl.when(odd == 1)
    def _():
        o_ref[...] = jnp.where(mine_q, o, o_ref[...].astype(F32)).astype(BF16)

    head = 2 * pair + odd
    here = pl.ds(pl.multiple_of(tile * rows, rows), rows)
    wide[here, :] = jnp.where(
        lane_q == head, m, jnp.where(lane_q == 4 + head, l, wide[here, :])
    )

    @pl.when((pair == pl.num_programs(0) - 1) & (tile == pl.num_programs(1) - 1) & (odd == 1))
    def _():
        for slot in range(st_ref.shape[0]):
            st_ref[slot] = jnp.transpose(wide[slot * 128:slot * 128 + 128, :])[:8]


def spread_kernel(sizes, inv, ck, cv, q, kv, qh, abuf, bbuf, gbuf,
                  s_a, r_a, s_b, r_b, s_g, r_g, s_q, r_q, s_r, s_l, r_l, r_r, s_fr, s_fl, r_fl, r_fr,
                  s_s, r_s, here):
    X, Y, Z, C = sizes
    y, z, c = lax.axis_index("y"), lax.axis_index("z"), lax.axis_index("c")
    W = Y * C
    w = y * C + c
    bpq = kv.shape[3]
    barrier = pltpu.get_barrier_semaphore()

    def greet_cluster(i):
        other = (w + i) % W
        pl.semaphore_signal(barrier, inc=1, device_id={"y": other // C, "c": other % C},
                            device_id_type=pl.DeviceIdType.MESH)

    def greet_line(i):
        pl.semaphore_signal(barrier, inc=1, device_id={"z": (z + i) % Z},
                            device_id_type=pl.DeviceIdType.MESH)

    each(W, 1, greet_cluster)
    each(Z, 1, greet_line)
    pl.semaphore_wait(barrier, W - 1 + Z - 1)

    def first(kind, step):
        to = (y + step) % Y
        src = (ck, cv)[kind].at[to]
        return to, src

    for step in range(1, Y):
        for kind in range(C):
            to, src = first(kind, step)
            remote(src, abuf.at[w], s_a.at[to * C + kind], r_a.at[w], y=to, c=kind).start()
    for kind in range(C):
        _, src = first(kind, 0)

        @pl.when(kind != c)
        def _():
            remote(src, abuf.at[w], s_a.at[y * C + kind], r_a.at[w], c=kind).start()

        @pl.when(kind == c)
        def _():
            pltpu.make_async_copy(src, abuf.at[w], here.at[0]).start()

    def send_q(i):
        to = (z + i) % Z
        remote(q.at[to], qh.at[z], s_q.at[to], r_q.at[z], z=to).start()

    each(Z, 1, send_q)
    pltpu.make_async_copy(q.at[z], qh.at[z], here.at[1]).start()
    pltpu.make_async_copy(ck.at[y], abuf.at[w], here.at[0]).wait()

    def wait_a(i):
        src = (w + i) % W
        remote(abuf.at[src], abuf.at[src], s_a.at[src], r_a.at[src], y=src // C, c=src % C).wait_recv()

    each(W, 1, wait_a)

    def send_b(i):
        to = (z + i) % Z
        remote(abuf.at[:, to], bbuf.at[pl.ds(z * W, W)], s_b.at[to], r_b.at[z], z=to).start()

    each(Z, 1, send_b)
    own_b = pltpu.make_async_copy(abuf.at[:, z], bbuf.at[pl.ds(z * W, W)], here.at[2])
    own_b.start()
    own_b.wait()

    def wait_b(i):
        src = (z + i) % Z
        part = bbuf.at[pl.ds(src * W, W)]
        remote(part, part, s_b.at[src], r_b.at[src], z=src).wait_recv()

    each(Z, 1, wait_b)

    def pick(i):
        gbuf[i] = bbuf[inv[i]]

    each(Z * bpq, 0, pick)

    def send_g(i):
        to = (z + i) % Z
        remote(gbuf.at[pl.ds(to * bpq, bpq)], kv.at[c, y, z], s_g.at[to], r_g.at[z], z=to).start()

    own_g = pltpu.make_async_copy(gbuf.at[pl.ds(z * bpq, bpq)], kv.at[c, y, z], here.at[3])
    own_g.start()
    each(Z, 1, send_g)
    own_g.wait()

    right, left, far, twin = (y + 1) % Y, (y + Y - 1) % Y, (y + 2) % Y, 1 - c

    def to_twin(piece, at):
        return remote(kv.at[c, piece, at], kv.at[c, piece, at], s_s.at[piece, at], r_s.at[piece, at], c=twin)

    def from_twin(piece, at):
        part = kv.at[twin, piece, at]
        return remote(part, part, s_s.at[piece, at], r_s.at[piece, at], c=twin)

    def to_right(at):
        return remote(kv.at[c, y, at], kv.at[c, y, at], s_r.at[at], r_l.at[at], y=right)

    def to_left(at):
        return remote(kv.at[c, y, at], kv.at[c, y, at], s_l.at[at], r_r.at[at], y=left)

    def from_left(at):
        return remote(kv.at[c, left, at], kv.at[c, left, at], s_r.at[at], r_l.at[at], y=left)

    def from_right(at):
        return remote(kv.at[c, right, at], kv.at[c, right, at], s_l.at[at], r_r.at[at], y=right)

    def pass_right(at):
        return remote(kv.at[c, left, at], kv.at[c, left, at], s_fr.at[at], r_fl.at[at], y=right)

    def pass_left(at):
        return remote(kv.at[c, right, at], kv.at[c, right, at], s_fl.at[at], r_fr.at[at], y=left)

    def far_left(at):
        return remote(kv.at[c, far, at], kv.at[c, far, at], s_fr.at[at], r_fl.at[at], y=left)

    def far_right(at):
        return remote(kv.at[c, far, at], kv.at[c, far, at], s_fl.at[at], r_fr.at[at], y=right)

    def share(at):
        to_right(at).start()
        to_left(at).start()
        to_twin(y, at).start()

    def step1(i):
        at = (z + i) % Z
        remote(kv.at[c, y, at], kv.at[c, y, at], s_g.at[at], r_g.at[at], z=at).wait_recv()
        share(at)

    def step2(i):
        at = (z + i) % Z
        from_left(at).wait_recv()

        @pl.when(at % 2 == 0)
        def _():
            pass_right(at).start()

        to_twin(left, at).start()
        from_right(at).wait_recv()

        @pl.when(at % 2 == 1)
        def _():
            pass_left(at).start()

        to_twin(right, at).start()

    def step3(i):
        at = (z + i) % Z

        @pl.when(at % 2 == 0)
        def _():
            far_left(at).wait_recv()

        @pl.when(at % 2 == 1)
        def _():
            far_right(at).wait_recv()

        to_twin(far, at).start()

    share(z)

    def steps12(i):
        step1(i)
        step2(i - 1)

    each(Z, 1, steps12)
    step2(Z - 1)
    each(Z, 0, step3)

    def twins(i):
        for piece in range(Y):
            from_twin(piece, i).wait_recv()

    each(Z, 0, twins)

    def end_line(i):
        at = (z + i) % Z
        remote(q.at[at], qh.at[at], s_q.at[at], r_q.at[at], z=at).wait_recv()
        remote(q.at[at], qh.at[at], s_q.at[at], r_q.at[at], z=at).wait_send()
        remote(abuf.at[:, at], bbuf.at[pl.ds(at * W, W)], s_b.at[at], r_b.at[at], z=at).wait_send()
        part = gbuf.at[pl.ds(at * bpq, bpq)]
        remote(part, part, s_g.at[at], r_g.at[at], z=at).wait_send()

    each(Z, 1, end_line)
    pltpu.make_async_copy(q.at[z], qh.at[z], here.at[1]).wait()

    def end_cluster(i):
        to = (w + i) % W
        remote(abuf.at[to], abuf.at[to], s_a.at[to], r_a.at[to], y=to // C, c=to % C).wait_send()

    each(W, 1, end_cluster)

    def end_ring(at):
        to_right(at).wait_send()
        to_left(at).wait_send()

        @pl.when(at % 2 == 0)
        def _():
            pass_right(at).wait_send()

        @pl.when(at % 2 == 1)
        def _():
            pass_left(at).wait_send()

        for piece in range(Y):
            to_twin(piece, at).wait_send()

    each(Z, 0, end_ring)


def return_kernel(sizes, oh, sth, os, sts, attg, ro, rst, att,
                  s_o, r_o, s_t, r_t, s_r, s_l, r_l, r_r, s_fr, s_fl, r_fl, r_fr, here, mine):
    X, Y, Z, C = sizes
    x, z = lax.axis_index("x"), lax.axis_index("z")
    right, left, far = (x + 1) % X, (x + X - 1) % X, (x + 2) % X
    rows, cols = ro.shape[1], ro.shape[2]
    half = rows // 2
    barrier = pltpu.get_barrier_semaphore()

    def greet_line(i):
        pl.semaphore_signal(barrier, inc=1, device_id={"z": (z + i) % Z},
                            device_id_type=pl.DeviceIdType.MESH)

    each(Z, 1, greet_line)
    for side in (right, left):
        pl.semaphore_signal(barrier, inc=1, device_id={"x": side}, device_id_type=pl.DeviceIdType.MESH)
    pl.semaphore_wait(barrier, Z - 1 + 2)

    def send(i):
        to = (z + i) % Z
        remote(oh.at[to], ro.at[z], s_o.at[to], r_o.at[z], z=to).start()
        remote(sth.at[to], rst.at[z], s_t.at[to], r_t.at[z], z=to).start()

    own_o = pltpu.make_async_copy(oh.at[z], ro.at[z], here.at[0])
    own_t = pltpu.make_async_copy(sth.at[z], rst.at[z], here.at[1])
    own_o.start()
    own_t.start()
    each(Z, 1, send)
    lane = lax.broadcasted_iota(jnp.int32, (8, cols), 1)
    row = lax.broadcasted_iota(jnp.int32, (8, cols), 0)
    widen = jnp.where(lane // DH == row, 1.0, 0.0).astype(F32)

    def keep(at):
        return pltpu.make_async_copy(att.at[at], attg.at[x, at], mine.at[at])

    def to_right(at):
        return remote(att.at[at], attg.at[x, at], s_r.at[at], r_l.at[at], x=right)

    def to_left(at):
        return remote(att.at[at], attg.at[x, at], s_l.at[at], r_r.at[at], x=left)

    def from_left(at):
        return remote(att.at[at], attg.at[left, at], s_r.at[at], r_l.at[at], x=left)

    def from_right(at):
        return remote(att.at[at], attg.at[right, at], s_l.at[at], r_r.at[at], x=right)

    def part(who, at, side):
        return attg.at[who, at, pl.ds(side * half, half)]

    def pass_right(at):
        return remote(part(left, at, 0), part(left, at, 0), s_fr.at[at], r_fl.at[at], x=right)

    def pass_left(at):
        return remote(part(right, at, 1), part(right, at, 1), s_fl.at[at], r_fr.at[at], x=left)

    def far_left(at):
        return remote(part(far, at, 0), part(far, at, 0), s_fr.at[at], r_fl.at[at], x=left)

    def far_right(at):
        return remote(part(far, at, 1), part(far, at, 1), s_fl.at[at], r_fr.at[at], x=right)

    def join(at):
        far_m, far_l = rst[at][0:4], rst[at][4:8]
        own_m, own_l = sts[at][0:4], sts[at][4:8]
        m = jnp.maximum(far_m, own_m)
        a = far_l * jnp.exp(far_m - m)
        b = own_l * jnp.exp(own_m - m)
        total = a + b
        zero = jnp.zeros_like(total)

        def wide(share):
            return lax.dot_general(
                jnp.concatenate([share, zero], axis=0), widen, (((0,), (0,)), ((), ())),
                preferred_element_type=F32, precision=lax.Precision.HIGHEST)

        value = wide(a / total) * ro[at].astype(F32) + wide(b / total) * os[at]
        att[at] = value.astype(BF16)
        keep(at).start()
        to_right(at).start()
        to_left(at).start()

    def arrive(i):
        at = (z + i) % Z
        remote(oh.at[at], ro.at[at], s_o.at[at], r_o.at[at], z=at).wait_recv()
        remote(sth.at[at], rst.at[at], s_t.at[at], r_t.at[at], z=at).wait_recv()
        join(at)

    def forward(i):
        at = (z + i) % Z
        from_left(at).wait_recv()
        pass_right(at).start()
        from_right(at).wait_recv()
        pass_left(at).start()

    own_o.wait()
    own_t.wait()
    join(z)

    def steps(i):
        arrive(i)
        forward(i - 1)

    each(Z, 1, steps)
    forward(Z - 1)

    def finish(at):
        far_left(at).wait_recv()
        far_right(at).wait_recv()
        keep(at).wait()
        to_right(at).wait_send()
        to_left(at).wait_send()
        pass_right(at).wait_send()
        pass_left(at).wait_send()

    each(Z, 0, finish)

    def end_line(i):
        at = (z + i) % Z
        remote(oh.at[at], ro.at[at], s_o.at[at], r_o.at[at], z=at).wait_send()
        remote(sth.at[at], rst.at[at], s_t.at[at], r_t.at[at], z=at).wait_send()

    each(Z, 1, end_line)


def out_kernel(where, att_ref, w_ref, x_ref, gain_ref, sel_ref, upd_ref, pool_ref, y_ref):
    parts, cols = att_ref.shape[0], att_ref.shape[3]
    y = jnp.dot(att_ref[0, 0], w_ref[0:cols, :], preferred_element_type=F32)
    for p in range(1, parts):
        y += jnp.dot(att_ref[p, 0], w_ref[p * cols:(p + 1) * cols, :], preferred_element_type=F32)
    y_ref[...] = y
    mine = where[where.shape[0] - 1]
    upd_ref[...] = y_ref[:, pl.ds(pl.multiple_of(mine * cols, cols), cols)]
    hidden = x_ref[...].astype(F32) + y
    square = jnp.sum(hidden * hidden, axis=1, keepdims=True)
    weighted = jnp.sum(hidden * gain_ref[...], axis=1, keepdims=True)
    score = weighted * lax.rsqrt(square / y.shape[1] + 1e-06)
    pool_ref[0] = jnp.dot(sel_ref[0], jnp.broadcast_to(score, (score.shape[0], 128)),
                          preferred_element_type=F32, precision=lax.Precision.HIGHEST)


def body(sizes, doc_x, doc_seg, doc_query, doc_var, query_len, block_perm, cache_k, cache_v, cache_var,
         w_query, w_key, w_value, w_out, var_bias, norm_gain, readout):
    X, Y, Z, C = sizes
    W = Y * C
    tokens, cols = doc_x.shape[0], w_query.shape[1]
    features = doc_x.shape[1]
    heads = cols // DH
    slot = tokens // Z
    crows = cache_k.shape[0]
    blocks = Y * Z * C
    bpq = blocks // Z
    keys = bpq * crows
    x_id, z_id, blk = lax.axis_index("x"), lax.axis_index("z"), lax.axis_index(BLK)
    i32 = jnp.int32
    iz = jnp.arange(Z, dtype=i32)

    w_all = lax.all_gather(w_out, "x", axis=0, tiled=True)

    slot_query = lax.dynamic_slice_in_dim(doc_query, blk * 2 * Z, 2 * Z).reshape(Z, 2)[:, 0]
    match = (slot_query[None, :] == iz[:, None]).astype(i32)
    order = jnp.sum(match * iz[None, :], axis=1)
    seg = doc_seg.reshape(Z, slot) - blk * (2 * Z) - 2 * iz[:, None]
    first_len = jnp.sum((seg == 0).astype(i32), axis=1)
    offset = jnp.arange(slot, dtype=i32)[None, :] - seg * first_len[:, None]
    packed = jnp.stack([seg, offset, doc_var.reshape(Z, slot)])
    packed = jnp.sum(jnp.where(match[None, :, :, None] == 1, packed[:, None], 0), axis=2)
    seg_q, off_q, var_q = packed[0], packed[1], packed[2]
    positions = (query_len[:, None] + off_q).reshape(tokens)

    payload = jnp.concatenate([cache_var, var_q.reshape(tokens)])
    everyone = lax.all_gather(payload, BLK)

    lane = jnp.arange(128, dtype=i32)
    half_size = DH // 2
    frequency = 10000.0 ** (-jnp.arange(half_size, dtype=F32) / half_size)
    angles = positions.astype(F32)[:, None] * jnp.tile(frequency, 128 // half_size)[None, :]
    cosine = jnp.cos(angles)
    sine = jnp.where((lane % DH < half_size)[None, :], -jnp.sin(angles), jnp.sin(angles))

    feature = lane % DH
    delta = var_bias[0] - var_bias[1]
    hi = lax.reduce_precision(delta, 8, 7)
    mid = lax.reduce_precision(delta - hi, 8, 7)
    low = lax.reduce_precision(delta - hi - mid, 8, 7)
    parts = jnp.stack([hi, mid, low])
    swapped = parts.reshape(3, heads // 2, 2)[:, :, ::-1].reshape(3, heads)
    col = jnp.arange(cols, dtype=i32)
    col_feature = col % DH
    per_col = jnp.repeat(swapped, DH, axis=1)
    table = jnp.where(col_feature < 8, per_col[0],
                      jnp.where(col_feature < 16, per_col[1], jnp.where(col_feature < 24, per_col[2], 0.0)))

    def query_features(var, segment):
        same = (var[:, None] == (col_feature % 8)[None, :])
        value = jnp.where(same, table[None, :], 0.0)
        value = jnp.where((col_feature == 24)[None, :], 1.0, value)
        if segment is not None:
            value = jnp.where((col_feature[None, :] - 25) == segment[:, None], 1.0, value)
        return value.astype(BF16)

    def key_features(var, valid, segment):
        same = (var[:, None] == (feature % 8)[None, :]) & (feature < 24)[None, :]
        value = jnp.where(same, 1.0, 0.0)
        if valid is not None:
            value = jnp.where((feature == 24)[None, :] & ~valid[:, None], NEG, value)
        if segment is not None:
            f = feature[None, :] - 25
            value = jnp.where(((f == 0) | (f == 1)) & (f != segment[:, None]), NEG, value)
        return value.astype(BF16)

    seg_flat, var_flat = seg_q.reshape(tokens), var_q.reshape(tokens)
    qf = query_features(var_flat, seg_flat)
    kf = key_features(var_flat, None, seg_flat)

    full = lambda *shape: pl.BlockSpec(shape, lambda i, *_: (0,) * len(shape))
    q_rot, own_o, own_st = pl.pallas_call(
        local_kernel,
        grid_spec=pltpu.PrefetchScalarGridSpec(
            num_scalar_prefetch=1,
            grid=(Z,),
            in_specs=[
                pl.BlockSpec((slot, features), lambda i, o: (o[i], 0)),
                full(features, cols), full(features, cols), full(features, cols),
                pl.BlockSpec((slot, 128), lambda i, o: (i, 0)),
                pl.BlockSpec((slot, 128), lambda i, o: (i, 0)),
                pl.BlockSpec((slot, cols), lambda i, o: (i, 0)),
                pl.BlockSpec((slot, 128), lambda i, o: (i, 0)),
            ],
            out_specs=[
                pl.BlockSpec((1, slot, cols), lambda i, o: (i, 0, 0)),
                pl.BlockSpec((1, slot, cols), lambda i, o: (i, 0, 0)),
                pl.BlockSpec((1, 8, slot), lambda i, o: (i, 0, 0)),
            ],
            scratch_shapes=[pltpu.VMEM((slot, 128), F32)],
        ),
        out_shape=[
            jax.ShapeDtypeStruct((Z, slot, cols), BF16),
            jax.ShapeDtypeStruct((Z, slot, cols), F32),
            jax.ShapeDtypeStruct((Z, 8, slot), F32),
        ],
        compiler_params=pltpu.CompilerParams(vmem_limit_bytes=32 << 20),
        name="local_part",
    )(order, doc_x, w_query, w_key, w_value, cosine, sine, qf, kf)

    by_block = jnp.sum(
        jnp.where(block_perm[None, :] == jnp.arange(blocks, dtype=i32)[:, None],
                  jnp.arange(blocks, dtype=i32)[None, :], 0), axis=1)
    inv = (by_block // C % Z) * W + (by_block // (Z * C)) * C + by_block % C

    dma = pltpu.SemaphoreType.DMA
    piece = crows // (Y * Z)
    kv, q_home = pl.pallas_call(
        functools.partial(spread_kernel, sizes),
        in_specs=[pl.BlockSpec(memory_space=pltpu.SMEM)] + [pl.BlockSpec(memory_space=ANY)] * 3,
        out_specs=[pl.BlockSpec(memory_space=ANY)] * 2,
        out_shape=[
            jax.ShapeDtypeStruct((C, Y, Z, bpq, piece, cols), BF16),
            jax.ShapeDtypeStruct((Z, slot, cols), BF16),
        ],
        scratch_shapes=[
            pltpu.VMEM((W, Z, piece, cols), BF16),
            pltpu.VMEM((Z * W, piece, cols), BF16),
            pltpu.VMEM((Z * bpq, piece, cols), BF16),
            dma((W,)), dma((W,)), dma((Z,)), dma((Z,)), dma((Z,)), dma((Z,)), dma((Z,)), dma((Z,)),
            dma((Z,)), dma((Z,)), dma((Z,)), dma((Z,)), dma((Z,)), dma((Z,)), dma((Z,)), dma((Z,)),
            dma((Y, Z)), dma((Y, Z)), dma((4,)),
        ],
        compiler_params=pltpu.CompilerParams(
            collective_id=0, has_side_effects=True, vmem_limit_bytes=16 << 20),
        name="spread",
    )(inv, cache_k.reshape(Y, Z, piece, cols), cache_v.reshape(Y, Z, piece, cols), q_rot)

    mine = lax.dynamic_slice_in_dim(by_block, z_id * bpq, bpq)
    key_var = jnp.take(everyone[:, :crows], mine, axis=0)
    key_var = key_var.reshape(bpq, Y, Z, piece).transpose(1, 2, 0, 3).reshape(keys)
    position = (jnp.arange(bpq, dtype=i32)[None, None, :, None] * crows
                + jnp.arange(Y, dtype=i32)[:, None, None, None] * (Z * piece)
                + jnp.arange(Z, dtype=i32)[None, :, None, None] * piece
                + jnp.arange(piece, dtype=i32)[None, None, None, :]).reshape(keys)
    my_len = lax.dynamic_slice_in_dim(query_len, z_id, 1)[0]
    ckf = key_features(key_var, position < my_len, None)
    home_var = everyone[:, crows:].reshape(Y, Z, C, Z, slot)
    home_var = lax.dynamic_slice(
        home_var, (lax.axis_index("y"), 0, lax.axis_index("c"), z_id, 0), (1, Z, 1, 1, slot)).reshape(tokens)
    hqf = query_features(home_var, None)

    rows = 256
    o_home, st_home = pl.pallas_call(
        cache_kernel,
        grid=(heads // 2, tokens // rows, 2),
        in_specs=[
            pl.BlockSpec((rows, 128), lambda p, t, o: (t, p)),
            pl.BlockSpec((rows, 128), lambda p, t, o: (t, p)),
            pl.BlockSpec((keys, 128), lambda p, t, o: (0, p)),
            pl.BlockSpec((keys, 128), lambda p, t, o: (0, 0)),
            pl.BlockSpec((keys, 128), lambda p, t, o: (0, p)),
        ],
        out_specs=[
            pl.BlockSpec((rows, 128), lambda p, t, o: (t, p)),
            pl.BlockSpec((Z, 8, slot), lambda p, t, o: (0, 0, 0)),
        ],
        out_shape=[
            jax.ShapeDtypeStruct((tokens, cols), BF16),
            jax.ShapeDtypeStruct((Z, 8, slot), F32),
        ],
        scratch_shapes=[pltpu.VMEM((tokens, 128), F32)],
        compiler_params=pltpu.CompilerParams(vmem_limit_bytes=56 << 20),
        name="cache_part",
    )(q_home.reshape(tokens, cols), hqf, kv[0].reshape(keys, cols), ckf, kv[1].reshape(keys, cols))

    attended = pl.pallas_call(
        functools.partial(return_kernel, sizes),
        in_specs=[pl.BlockSpec(memory_space=ANY)] * 2 + [pl.BlockSpec(memory_space=pltpu.VMEM)] * 2,
        out_specs=pl.BlockSpec(memory_space=ANY),
        out_shape=jax.ShapeDtypeStruct((X, Z, slot, cols), BF16),
        scratch_shapes=[
            pltpu.VMEM((Z, slot, cols), BF16),
            pltpu.VMEM((Z, 8, slot), F32),
            pltpu.VMEM((Z, slot, cols), BF16),
        ] + [dma((Z,))] * 12 + [dma((2,)), dma((Z,))],
        compiler_params=pltpu.CompilerParams(
            collective_id=1, has_side_effects=True, vmem_limit_bytes=16 << 20),
        name="give_back",
    )(o_home.reshape(Z, slot, cols), st_home, own_o, own_st)

    sel = jnp.stack([seg == 0, seg == 1], axis=1)
    share = jnp.where(sel, 1.0 / jnp.sum(sel.astype(F32), axis=2, keepdims=True), 0.0)
    share = jnp.concatenate([share, jnp.zeros((Z, 6, slot), F32)], axis=1)
    gain = (norm_gain * readout).reshape(1, features)
    where = jnp.concatenate([slot_query, x_id.reshape(1).astype(i32)])
    update, pooled = pl.pallas_call(
        out_kernel,
        grid_spec=pltpu.PrefetchScalarGridSpec(
            num_scalar_prefetch=1,
            grid=(Z,),
            in_specs=[
                pl.BlockSpec((X, 1, slot, cols), lambda i, w: (0, w[i], 0, 0)),
                full(X * cols, features),
                pl.BlockSpec((slot, features), lambda i, w: (i, 0)),
                full(1, features),
                pl.BlockSpec((1, 8, slot), lambda i, w: (i, 0, 0)),
            ],
            out_specs=[
                pl.BlockSpec((slot, cols), lambda i, w: (i, 0)),
                pl.BlockSpec((1, 8, 128), lambda i, w: (i, 0, 0)),
            ],
            scratch_shapes=[pltpu.VMEM((slot, features), F32)],
        ),
        out_shape=[
            jax.ShapeDtypeStruct((tokens, cols), F32),
            jax.ShapeDtypeStruct((Z, 8, 128), F32),
        ],
        compiler_params=pltpu.CompilerParams(vmem_limit_bytes=32 << 20),
        name="out_part",
    )(where, attended, w_all, doc_x, gain, share)
    return update, pooled[:, :2, 0].reshape(2 * Z)


def solution(mesh):
    heads = mesh.shape["head"]
    cores = 2
    across = 4
    along = mesh.shape["blk"] // (across * cores)
    sizes = (heads, across, along, cores)
    split = Mesh(mesh.devices.reshape(sizes), ("x", "y", "z", "c"))
    return jax.shard_map(
        functools.partial(body, sizes),
        mesh=split,
        in_specs=(
            P(BLK, None), P(BLK), P(), P(BLK), P(), P(),
            P(BLK, "x"), P(BLK, "x"), P(BLK),
            P(None, "x"), P(None, "x"), P(None, "x"), P("x", None), P(None, "x"),
            P(), P(),
        ),
        out_specs=(P(BLK, "x"), P(BLK)),
        check_vma=False,
    )
```

```python
import functools

import jax
import jax.numpy as jnp
import numpy as np
from jax import lax
from jax.experimental import pallas as pl
from jax.experimental.pallas import tpu as pltpu
from jax.sharding import Mesh, PartitionSpec as P

DH = 64
F32 = jnp.float32
BF16 = jnp.bfloat16
NEG = -1e30
ANY = pl.ANY
BLK = ("y", "z", "c")


def remote(src, dst, send_sem, recv_sem, **device):
    return pltpu.make_async_remote_copy(
        src_ref=src,
        dst_ref=dst,
        send_sem=send_sem,
        recv_sem=recv_sem,
        device_id=device,
        device_id_type=pl.DeviceIdType.MESH,
    )


def each(count, first, step):
    def run(i, carry):
        step(i)
        return carry

    lax.fori_loop(first, count, run, 0)


def nth_near(i, Z):
    return lax.rem(jnp.where(i % 2 == 1, (i + 1) // 2, Z - i // 2), Z)


def attention_kernel(
    sizes, inv, dq, qlen, bias, seg_ref, var_ref, tcos_ref, tsin_ref, freq_ref, x_in, wq_in, wk_in, wv_in,
    ck, cv, cvar, attg,
    xv, wq, wk, wv, order, abuf, bbuf, gbuf, va, vb, kv, qrot, qh, dv, hv, cosv, sinv, qtab, ktab,
    os, sts, ka, vx, qa, acc, mx, oh, sth, ro, rst, att,
    s_x, s_a, r_a, s_va, r_va, s_b, r_b, s_vb, r_vb, s_g, r_g, s_q, r_q, s_dv, r_dv,
    s_r, s_l, r_l, r_r, s_fr, s_fl, r_fl, r_fr, s_s, r_s,
    s_o, r_o, s_t, r_t, x_r, x_l, y_l, y_r, x_fr, x_fl, y_fl, y_fr, mine_sem, here,
):
    X, Y, Z, C = sizes
    x, y, z, c = lax.axis_index("x"), lax.axis_index("y"), lax.axis_index("z"), lax.axis_index("c")
    W = Y * C
    w = y * C + c
    bpq = W
    blk = (y * Z + z) * C + c
    slot, cols = qrot.shape[1], qrot.shape[2]
    heads = cols // DH
    pairs = cols // 128
    part_keys = bpq * slot
    barrier = pltpu.get_barrier_semaphore()

    loads = [pltpu.make_async_copy(s, d, s_x.at[n]) for n, (s, d) in
             enumerate(((x_in, xv), (wq_in, wq), (wk_in, wk), (wv_in, wv)))]
    for load in loads:
        load.start()

    def greet(**device):
        pl.semaphore_signal(barrier, inc=1, device_id=device, device_id_type=pl.DeviceIdType.MESH)

    each(W, 1, lambda i: greet(y=(w + i) % W // C, c=(w + i) % W % C))
    each(Z, 1, lambda i: greet(z=(z + i) % Z))
    for side in ((x + 1) % X, (x + X - 1) % X):
        greet(x=side)

    slot_query = [dq[blk * 2 * Z + 2 * j] for j in range(Z)]
    for query in range(Z):
        at = jnp.int32(0)
        for j in range(Z):
            at = jnp.where(slot_query[j] == query, j, at)
        order[query] = at
    lane2 = lax.broadcasted_iota(jnp.int32, (16, cols), 1)
    row2 = lax.broadcasted_iota(jnp.int32, (16, cols), 0)
    feat2 = lane2 % DH
    lane_head = 2 * (lane2 // 128) + (1 - lane2 % 128 // DH)
    delta = jnp.zeros((16, cols), F32)
    for h in range(heads):
        delta = jnp.where(lane_head == h, bias[0, h] - bias[1, h], delta)
    hi = delta.astype(BF16).astype(F32)
    mid = (delta - hi).astype(BF16).astype(F32)
    low = delta - hi - mid
    value = jnp.where(feat2 < 8, hi, jnp.where(feat2 < 16, mid, low))
    value = jnp.where((feat2 < 24) & (feat2 % 8 == row2), value, 0.0)
    qtab[...] = jnp.where((row2 >= 8) & (row2 < 11) & (feat2 == row2 + 16), 1.0, value).astype(BF16)
    lane1, row1 = lane2[:, :128], row2[:, :128]
    feat1 = lane1 % DH
    value = jnp.where((feat1 < 24) & (feat1 % 8 == row1), 1.0, 0.0)
    hit = (((row1 == 8) & (feat1 == 24)) | ((row1 == 9) & (feat1 == 26)) | ((row1 == 10) & (feat1 == 25)))
    ktab[...] = jnp.where(hit, NEG, value).astype(BF16)

    def features(rows, table):
        return lax.dot_general(rows.astype(BF16), table, (((0,), (0,)), ((), ())),
                               preferred_element_type=F32).astype(BF16)

    def marks(var, eight, seg):
        same = jnp.where((row1 < 8) & (var == row1), 1.0, 0.0)
        rows = jnp.where(row1 == 8, eight, same)
        if seg is not None:
            rows = jnp.where(((row1 == 9) & (seg == 0)) | ((row1 == 10) & (seg == 1)), 1.0, rows)
        return rows

    pl.semaphore_wait(barrier, W - 1 + Z - 1 + 2)

    for step in range(1, Y):
        to = (y + step) % Y
        for kind in range(C):
            remote((ck, cv)[kind].at[to], abuf.at[w], s_a.at[to * C + kind], r_a.at[w], y=to, c=kind).start()
            remote(cvar, va.at[w], s_va.at[to * C + kind], r_va.at[w], y=to, c=kind).start()
    for kind in range(C):
        src = (ck, cv)[kind].at[y]

        @pl.when(kind != c)
        def _():
            remote(src, abuf.at[w], s_a.at[y * C + kind], r_a.at[w], c=kind).start()
            remote(cvar, va.at[w], s_va.at[y * C + kind], r_va.at[w], c=kind).start()

        @pl.when(kind == c)
        def _():
            pltpu.make_async_copy(src, abuf.at[w], here.at[0]).start()

    own_var = pltpu.make_async_copy(cvar, va.at[w], here.at[1])
    own_var.start()

    lane = lax.broadcasted_iota(jnp.int32, (slot, cols), 1)
    half = lax.broadcasted_iota(jnp.int32, (slot, 128), 1)
    first_lanes = (lane % DH) < DH // 2
    first_half = (half % DH) < DH // 2
    ones_row = jnp.where(row1 == 10, 1.0, 0.0).astype(BF16)

    def segment(at):
        return seg_ref[at] - (blk * 2 * Z + 2 * at)

    def turn(a, query):
        other = jnp.where(first_lanes, pltpu.roll(a, cols - DH // 2, 1), pltpu.roll(a, DH // 2, 1))
        cosine = jnp.concatenate([cosv[query]] * pairs, axis=1)
        sine = jnp.concatenate([sinv[query]] * pairs, axis=1)
        return a * cosine + other * sine

    loads[0].wait()
    loads[1].wait()

    def project_q(query):
        at = order[query]
        seg = segment(at)
        length = qlen[query].astype(F32)
        count = jnp.sum(jnp.where(seg == 0, 1.0, 0.0), axis=1, keepdims=True)
        base0 = freq_ref[...] * length
        base1 = freq_ref[...] * (length - count)
        second = features(marks(var_ref[at], 1.0, seg), ones_row).astype(F32) > 0.5
        cos_a = jnp.where(second, jnp.cos(base1), jnp.cos(base0))
        sin_a = jnp.where(second, jnp.sin(base1), jnp.sin(base0))
        cosv[query] = cos_a * tcos_ref[...] - sin_a * tsin_ref[...]
        sine = sin_a * tcos_ref[...] + cos_a * tsin_ref[...]
        sinv[query] = jnp.where(first_half, -sine, sine)
        a = jnp.dot(xv[at], wq[...], preferred_element_type=F32)
        qrot[query] = (turn(a, query) * 0.125).astype(BF16)
        dv[query] = var_ref[at]

    each(Z, 0, project_q)

    pltpu.make_async_copy(ck.at[y], abuf.at[w], here.at[0]).wait()
    own_var.wait()

    def wait_a(i):
        src = (w + i) % W
        remote(abuf.at[src], abuf.at[src], s_a.at[src], r_a.at[src], y=src // C, c=src % C).wait_recv()
        remote(va.at[src], va.at[src], s_va.at[src], r_va.at[src], y=src // C, c=src % C).wait_recv()

    each(W, 1, wait_a)

    def line_b(to, at):
        return (remote(abuf.at[:, to], bbuf.at[pl.ds(at * W, W)], s_b.at[to], r_b.at[at], z=to),
                remote(va, vb.at[pl.ds(at * W, W)], s_vb.at[to], r_vb.at[at], z=to))

    def send_b(i):
        for copy in line_b((z + nth_near(i, Z)) % Z, z):
            copy.start()

    each(Z, 1, send_b)
    own_b = pltpu.make_async_copy(abuf.at[:, z], bbuf.at[pl.ds(z * W, W)], here.at[2])
    own_vb = pltpu.make_async_copy(va, vb.at[pl.ds(z * W, W)], here.at[3])
    own_b.start()
    own_vb.start()

    loads[2].wait()
    loads[3].wait()
    wide8 = lax.broadcasted_iota(jnp.int32, (8, cols), 1)
    deep8 = lax.broadcasted_iota(jnp.int32, (8, cols), 0)
    widen = jnp.where(wide8 // DH == deep8, 1.0, 0.0).astype(F32)

    def own_part(query):
        at = order[query]
        xs = xv[at]
        k = turn(jnp.dot(xs, wk[...], preferred_element_type=F32), query).astype(BF16)
        v = jnp.dot(xs, wv[...], preferred_element_type=F32).astype(BF16)
        seg = segment(at)
        qf = features(marks(var_ref[at], 1.0, seg), qtab[...])
        kf = features(marks(var_ref[at], 0.0, seg), ktab[...])
        q = qrot[query]
        stats = jnp.zeros((slot, 128), F32)
        for pair in range(pairs):
            tile = slice(pair * 128, pair * 128 + 128)
            outs = []
            for odd in range(2):
                mine = (half >= DH) if odd else (half < DH)
                qs = jnp.where(mine, q[:, tile], qf[:, tile])
                ks = jnp.where(mine, k[:, tile], kf)
                s = lax.dot_general(qs, ks, (((1,), (1,)), ((), ())), preferred_element_type=F32)
                m = jnp.max(s, axis=1, keepdims=True)
                p = jnp.exp(s - m)
                l = jnp.sum(p, axis=1, keepdims=True)
                outs.append(jnp.dot(p.astype(BF16), v[:, tile], preferred_element_type=F32) / l)
                head = 2 * pair + odd
                stats = jnp.where(half == head, m, jnp.where(half == 4 + head, l, stats))
            os[query, :, tile] = jnp.where(half < DH, outs[0], outs[1])
        sts[query] = jnp.transpose(stats)[:8]

    each(Z, 0, own_part)

    own_b.wait()
    own_vb.wait()

    def wait_b(i):
        src = (z + i) % Z
        part = bbuf.at[pl.ds(src * W, W)]
        remote(part, part, s_b.at[src], r_b.at[src], z=src).wait_recv()
        part = vb.at[pl.ds(src * W, W)]
        remote(part, part, s_vb.at[src], r_vb.at[src], z=src).wait_recv()

    each(Z, 1, wait_b)

    def pick(i):
        gbuf[i] = bbuf[inv[i]]

    each(Z * bpq, 0, pick)

    def line_g(to, at):
        return remote(gbuf.at[pl.ds(to * bpq, bpq)], kv.at[c, y, :, at], s_g.at[to], r_g.at[at], z=to)

    own_g = pltpu.make_async_copy(gbuf.at[pl.ds(z * bpq, bpq)], kv.at[c, y, :, z], here.at[2])
    own_g.start()
    each(Z, 1, lambda i: line_g((z + nth_near(i, Z)) % Z, z).start())

    def line_q(to, at):
        return (remote(qrot.at[to], qh.at[at], s_q.at[to], r_q.at[at], z=to),
                remote(dv.at[to], hv.at[at], s_dv.at[to], r_dv.at[at], z=to))

    def send_q(i):
        for copy in line_q((z + nth_near(i, Z)) % Z, z):
            copy.start()

    each(Z, 1, send_q)
    own_q = pltpu.make_async_copy(qrot.at[z], qh.at[z], here.at[0])
    own_dv = pltpu.make_async_copy(dv.at[z], hv.at[z], here.at[1])
    own_q.start()
    own_dv.start()
    own_g.wait()

    right, left, far, twin = (y + 1) % Y, (y + Y - 1) % Y, (y + 2) % Y, 1 - c

    def ring(kind, piece, at, send, recv, **device):
        part = kv.at[kind, piece, :, at]
        return remote(part, part, send.at[at], recv.at[at], **device)

    def to_twin(piece, at):
        return ring(c, piece, at, s_s.at[piece], r_s.at[piece], c=twin)

    def from_twin(piece, at):
        return ring(twin, piece, at, s_s.at[piece], r_s.at[piece], c=twin)

    to_right = lambda at: ring(c, y, at, s_r, r_l, y=right)
    to_left = lambda at: ring(c, y, at, s_l, r_r, y=left)
    from_left = lambda at: ring(c, left, at, s_r, r_l, y=left)
    from_right = lambda at: ring(c, right, at, s_l, r_r, y=right)
    pass_right = lambda at: ring(c, left, at, s_fr, r_fl, y=right)
    pass_left = lambda at: ring(c, right, at, s_fl, r_fr, y=left)
    far_left = lambda at: ring(c, far, at, s_fr, r_fl, y=left)
    far_right = lambda at: ring(c, far, at, s_fl, r_fr, y=right)

    def share(at):
        to_right(at).start()
        to_left(at).start()
        to_twin(y, at).start()

    def step1(i):
        at = (z + nth_near(i, Z)) % Z
        part = kv.at[c, y, :, at]
        remote(part, part, s_g.at[at], r_g.at[at], z=at).wait_recv()
        share(at)

    def step2(i):
        at = (z + nth_near(i, Z)) % Z
        from_left(at).wait_recv()

        @pl.when(at % 2 == 0)
        def _():
            pass_right(at).start()

        to_twin(left, at).start()
        from_right(at).wait_recv()

        @pl.when(at % 2 == 1)
        def _():
            pass_left(at).start()

        to_twin(right, at).start()

    def step3(i):
        at = (z + nth_near(i, Z)) % Z

        @pl.when(at % 2 == 0)
        def _():
            far_left(at).wait_recv()

        @pl.when(at % 2 == 1)
        def _():
            far_right(at).wait_recv()

        to_twin(far, at).start()

    share(z)
    each(Z, 1, step1)

    my_len = qlen[z]

    def build(n, piece):
        def one(j):
            var = vb[inv[z * bpq + j], piece]
            place = lane1 + (j * Y * slot + piece * slot)
            kf = features(marks(var, jnp.where(place >= my_len, 1.0, 0.0), None), ktab[...])
            k = kv[0, piece, j].reshape(slot, cols)
            v = kv[1, piece, j].reshape(slot, cols)
            rows = pl.ds(pl.multiple_of(j * slot, slot), slot)
            for pair in range(pairs):
                tile = slice(pair * 128, pair * 128 + 128)
                for odd in range(2):
                    mine = (half >= DH) if odd else (half < DH)
                    ka[2 * pair + odd, n, rows, :] = jnp.where(mine, k[:, tile], kf)
                    vx[2 * pair + odd, n, rows, :] = jnp.where(mine, v[:, tile], jnp.ones_like(kf))

        each(bpq, 0, one)

    def take_q(i):
        at = (z + nth_near(i, Z)) % Z
        qf = features(marks(hv[at], 1.0, None), qtab[...])
        q = qh[at]
        rows = pl.ds(pl.multiple_of(i * slot, slot), slot)
        for pair in range(pairs):
            tile = slice(pair * 128, pair * 128 + 128)
            for odd in range(2):
                mine = (half >= DH) if odd else (half < DH)
                qa[2 * pair + odd, rows, :] = jnp.where(mine, q[:, tile], qf[:, tile])

    def wait_q(i):
        at = (z + nth_near(i, Z)) % Z
        for copy in line_q(at, at):
            copy.wait_recv()
        take_q(i)

    side = Z // 2 * slot
    chunk = 256

    def attend(n, group, start):
        rows = slice(group * side, group * side + side)

        def one(h):
            q = qa[h, rows, :]
            if start:
                m = jnp.full((side, 128), -3e38, F32)[:, :1]
                total = None
            else:
                m = mx[h, rows, :][:, :1]
                total = acc[h, rows, :]
            for first in range(0, part_keys, chunk):
                s = lax.dot_general(q, ka[h, n, first:first + chunk, :], (((1,), (1,)), ((), ())),
                                    preferred_element_type=F32)
                new = jnp.maximum(m, jnp.max(s, axis=1, keepdims=True))
                p = jnp.exp(s - new).astype(BF16)
                o = jnp.dot(p, vx[h, n, first:first + chunk, :], preferred_element_type=F32)
                total = o if total is None else total * jnp.exp(m - new) + o
                m = new
            acc[h, rows, :] = total
            mx[h, rows, :] = jnp.broadcast_to(m, (side, 128))

        each(heads, 0, one)

    def twins(piece):
        each(Z, 0, lambda at: from_twin(piece, at).wait_recv())

    twins(y)
    build(0, y)
    own_q.wait()
    own_dv.wait()
    take_q(0)
    each(Z // 2, 1, wait_q)
    attend(0, 0, True)
    each(Z, 0, step2)
    each(Z, Z // 2, wait_q)
    attend(0, 1, True)
    each(Z, 0, step3)
    twins(left)
    build(1, left)
    twins(right)
    build(2, right)
    twins(far)
    build(3, far)

    def line_o(to, at):
        return (remote(oh.at[to], ro.at[at], s_o.at[to], r_o.at[at], z=to),
                remote(sth.at[to], rst.at[at], s_t.at[to], r_t.at[at], z=to))

    def settle(i):
        at = (z + nth_near(i, Z)) % Z
        rows = pl.ds(pl.multiple_of(i * slot, slot), slot)
        stats = jnp.zeros((slot, 128), F32)
        for pair in range(pairs):
            outs = []
            for odd in range(2):
                mine = (half >= DH) if odd else (half < DH)
                head = 2 * pair + odd
                total = acc[head, rows, :]
                turned = pltpu.roll(total, DH, 1)
                l = jnp.where(mine, turned, total)
                outs.append(total / l)
                stats = jnp.where(half == head, mx[head, rows, :], jnp.where(half == 4 + head, l, stats))
            oh[at, :, pair * 128:pair * 128 + 128] = jnp.where(half < DH, outs[0], outs[1]).astype(BF16)
        sth[at] = jnp.transpose(stats)[:8]

    def settle_send(i):
        settle(i)
        at = (z + nth_near(i, Z)) % Z
        for copy in line_o(at, z):
            copy.start()

    xright, xleft, xfar = (x + 1) % X, (x + X - 1) % X, (x + 2) % X
    mid_row = slot // 2
    keep = lambda at: pltpu.make_async_copy(att.at[at], attg.at[x, at], mine_sem.at[at])

    def xring(src, who, at, send, recv, dev):
        return remote(src, attg.at[who, at], send.at[at], recv.at[at], x=dev)

    def xpass(who, at, piece, send, recv, dev):
        part = attg.at[who, at, pl.ds(piece * mid_row, mid_row)]
        return remote(part, part, send.at[at], recv.at[at], x=dev)

    xto_right = lambda at: xring(att.at[at], x, at, x_r, y_l, xright)
    xto_left = lambda at: xring(att.at[at], x, at, x_l, y_r, xleft)
    xfrom_left = lambda at: xring(att.at[at], xleft, at, x_r, y_l, xleft)
    xfrom_right = lambda at: xring(att.at[at], xright, at, x_l, y_r, xright)
    xpass_right = lambda at: xpass(xleft, at, 0, x_fr, y_fl, xright)
    xpass_left = lambda at: xpass(xright, at, 1, x_fl, y_fr, xleft)
    xfar_left = lambda at: xpass(xfar, at, 0, x_fr, y_fl, xleft)
    xfar_right = lambda at: xpass(xfar, at, 1, x_fl, y_fr, xright)

    def join(at):
        far_m, far_l = rst[at][0:4], rst[at][4:8]
        own_m, own_l = sts[at][0:4], sts[at][4:8]
        m = jnp.maximum(far_m, own_m)
        a = far_l * jnp.exp(far_m - m)
        b = own_l * jnp.exp(own_m - m)
        total = a + b
        zero = jnp.zeros_like(total)

        def wide(share):
            return lax.dot_general(
                jnp.concatenate([share, zero], axis=0), widen, (((0,), (0,)), ((), ())),
                preferred_element_type=F32, precision=lax.Precision.HIGHEST)

        value = wide(a / total) * ro[at].astype(F32) + wide(b / total) * os[at]
        att[at] = value.astype(BF16)
        keep(at).start()
        xto_right(at).start()
        xto_left(at).start()

    def home(i):
        return (z + Z - nth_near(i, Z)) % Z

    def arrive(i):
        at = home(i)
        for copy in line_o(at, at):
            copy.wait_recv()
        join(at)

    def forward(i):
        at = home(i)
        xfrom_left(at).wait_recv()
        xpass_right(at).start()
        xfrom_right(at).wait_recv()
        xpass_left(at).start()

    for n in range(1, Y):
        attend(n, 0, False)
    settle(0)
    own_o = pltpu.make_async_copy(oh.at[z], ro.at[z], here.at[0])
    own_t = pltpu.make_async_copy(sth.at[z], rst.at[z], here.at[1])
    own_o.start()
    own_t.start()
    each(Z // 2, 1, settle_send)
    attend(1, 1, False)
    own_o.wait()
    own_t.wait()
    join(z)
    attend(2, 1, False)
    each(Z // 2, 1, arrive)
    attend(3, 1, False)
    each(Z, Z // 2, settle_send)
    each(Z // 2, 0, forward)

    def late(i):
        arrive(i)

        @pl.when(i > Z // 2)
        def _():
            forward(i - 1)

    each(Z, Z // 2, late)
    forward(Z - 1)

    def finish(at):
        xfar_left(at).wait_recv()
        xfar_right(at).wait_recv()
        keep(at).wait()
        for copy in (xto_right(at), xto_left(at), xpass_right(at), xpass_left(at), to_right(at), to_left(at)):
            copy.wait_send()

        @pl.when(at % 2 == 0)
        def _():
            pass_right(at).wait_send()

        @pl.when(at % 2 == 1)
        def _():
            pass_left(at).wait_send()

        for piece in range(Y):
            to_twin(piece, at).wait_send()

    each(Z, 0, finish)

    def end_line(i):
        at = (z + i) % Z
        for copy in line_b(at, at) + line_q(at, at) + line_o(at, at) + (line_g(at, at),):
            copy.wait_send()

    each(Z, 1, end_line)

    def end_cluster(i):
        to = (w + i) % W
        remote(abuf.at[to], abuf.at[to], s_a.at[to], r_a.at[to], y=to // C, c=to % C).wait_send()
        remote(cvar, va.at[to], s_va.at[to], r_va.at[to], y=to // C, c=to % C).wait_send()

    each(W, 1, end_cluster)


def out_kernel(dq, ids, att_ref, w_ref, x_ref, seg_ref, gain_ref, read_ref, upd_ref, pool_ref, y_ref):
    step = pl.program_id(0)
    parts, cols = att_ref.shape[0], att_ref.shape[3]
    y = jnp.dot(att_ref[0, 0], w_ref[0:cols, :], preferred_element_type=F32)
    for p in range(1, parts):
        y += jnp.dot(att_ref[p, 0], w_ref[p * cols:(p + 1) * cols, :], preferred_element_type=F32)
    y_ref[...] = y
    upd_ref[...] = y_ref[:, pl.ds(pl.multiple_of(ids[1] * cols, cols), cols)]
    hidden = x_ref[...].astype(F32) + y
    square = jnp.sum(hidden * hidden, axis=1, keepdims=True)
    weighted = jnp.sum(hidden * (gain_ref[...] * read_ref[...]), axis=1, keepdims=True)
    score = weighted * lax.rsqrt(square / y.shape[1] + 1e-06)
    first = (ids[0] * pl.num_programs(0) + step) * 2
    row = lax.broadcasted_iota(jnp.int32, (8, score.shape[0]), 0)
    member = jnp.where((row < 2) & (seg_ref[0] - first == row), 1.0, 0.0)
    sums = jnp.dot(member, jnp.broadcast_to(score, (score.shape[0], 128)),
                   preferred_element_type=F32, precision=lax.Precision.HIGHEST)
    count = jnp.maximum(jnp.sum(member, axis=1, keepdims=True), 1.0)
    pool_ref[0] = sums / count


def body(sizes, doc_x, doc_seg, doc_query, doc_var, query_len, block_perm, cache_k, cache_v, cache_var,
         w_query, w_key, w_value, w_out, var_bias, norm_gain, readout):
    X, Y, Z, C = sizes
    W = Y * C
    tokens, cols = doc_x.shape[0], w_query.shape[1]
    features = doc_x.shape[1]
    heads = cols // DH
    slot = tokens // Z
    crows = cache_k.shape[0]
    blocks = Y * Z * C
    bpq = blocks // Z
    piece = crows // (Y * Z)
    part_keys = bpq * slot
    i32 = jnp.int32
    dma = pltpu.SemaphoreType.DMA

    w_all = lax.all_gather(w_out, "x", axis=0, tiled=True)

    at = jnp.arange(blocks, dtype=i32)
    place = (at // C % Z) * W + (at // (Z * C)) * C + at % C
    inv = jnp.sum(jnp.where(block_perm[None, :] == at[:, None], place[None, :], 0), axis=1)

    half_size = DH // 2
    frequency = 10000.0 ** (-np.arange(half_size) / half_size)
    frequency = np.tile(frequency.astype(np.float32), 128 // half_size)
    turns = np.arange(slot)[:, None] * frequency.astype(np.float64)[None, :]
    seg = doc_seg.reshape(Z, 1, slot)

    vm = lambda *shape: pltpu.VMEM(shape, BF16)
    vf = lambda *shape: pltpu.VMEM(shape, F32)
    vi = lambda *shape: pltpu.VMEM(shape, i32)
    smem = pl.BlockSpec(memory_space=pltpu.SMEM)
    vmem = pl.BlockSpec(memory_space=pltpu.VMEM)
    hbm = pl.BlockSpec(memory_space=ANY)
    attended = pl.pallas_call(
        functools.partial(attention_kernel, sizes),
        in_specs=[smem] * 4 + [vmem] * 5 + [hbm] * 7,
        out_specs=hbm,
        out_shape=jax.ShapeDtypeStruct((X, Z, slot, cols), BF16),
        scratch_shapes=[
            vm(Z, slot, features), vm(features, cols), vm(features, cols), vm(features, cols),
            pltpu.SMEM((Z,), i32),
            vm(W, Z, piece, cols), vm(Z * W, piece, cols), vm(Z * bpq, piece, cols),
            vi(W, Y, 1, slot), vi(Z * W, Y, 1, slot),
            vm(C, Y, bpq, Z, piece, cols),
            vm(Z, slot, cols), vm(Z, slot, cols), vi(Z, 1, slot), vi(Z, 1, slot),
            vf(Z, slot, 128), vf(Z, slot, 128), vm(16, cols), vm(16, 128),
            vf(Z, slot, cols), vf(Z, 8, slot),
            vm(heads, Y, part_keys, 128), vm(heads, Y, part_keys, 128), vm(heads, tokens, 128),
            vf(heads, tokens, 128), vf(heads, tokens, 128),
            vm(Z, slot, cols), vf(Z, 8, slot), vm(Z, slot, cols), vf(Z, 8, slot), vm(Z, slot, cols),
            dma((4,)),
        ] + [dma((W,))] * 4 + [dma((Z,))] * 10 + [dma((Z,))] * 8 + [dma((Y, Z))] * 2
        + [dma((Z,))] * 4 + [dma((Z,))] * 9 + [dma((4,))],
        compiler_params=pltpu.CompilerParams(
            collective_id=0, has_side_effects=True, vmem_limit_bytes=56 << 20),
        name="attention",
    )(inv, doc_query, query_len, var_bias, seg, doc_var.reshape(Z, 1, slot),
      jnp.asarray(np.cos(turns), F32), jnp.asarray(np.sin(turns), F32), jnp.asarray(frequency)[None, :],
      doc_x.reshape(Z, slot, features), w_query, w_key, w_value,
      cache_k.reshape(Y, Z, piece, cols), cache_v.reshape(Y, Z, piece, cols), cache_var.reshape(Y, 1, slot))

    full = lambda *shape: pl.BlockSpec(shape, lambda i, *_: (0,) * len(shape))
    ids = jnp.stack([lax.axis_index(BLK), lax.axis_index("x")]).astype(i32)
    update, pooled = pl.pallas_call(
        out_kernel,
        grid_spec=pltpu.PrefetchScalarGridSpec(
            num_scalar_prefetch=2,
            grid=(Z,),
            in_specs=[
                pl.BlockSpec((X, 1, slot, cols), lambda i, d, n: (0, d[n[0] * 2 * Z + 2 * i], 0, 0)),
                full(X * cols, features),
                pl.BlockSpec((slot, features), lambda i, d, n: (i, 0)),
                pl.BlockSpec((1, 1, slot), lambda i, d, n: (i, 0, 0)),
                full(1, features),
                full(1, features),
            ],
            out_specs=[
                pl.BlockSpec((slot, cols), lambda i, d, n: (i, 0)),
                pl.BlockSpec((1, 8, 128), lambda i, d, n: (i, 0, 0)),
            ],
            scratch_shapes=[pltpu.VMEM((slot, features), F32)],
        ),
        out_shape=[
            jax.ShapeDtypeStruct((tokens, cols), F32),
            jax.ShapeDtypeStruct((Z, 8, 128), F32),
        ],
        compiler_params=pltpu.CompilerParams(vmem_limit_bytes=32 << 20),
        name="out_part",
    )(doc_query, ids, attended, w_all, doc_x, seg, norm_gain.reshape(1, features), readout.reshape(1, features))
    return update, pooled[:, :2, 0].reshape(2 * Z)


def solution(mesh):
    heads = mesh.shape["head"]
    cores = 2
    across = 4
    along = mesh.shape["blk"] // (across * cores)
    sizes = (heads, across, along, cores)
    split = Mesh(mesh.devices.reshape(sizes), ("x", "y", "z", "c"))
    return jax.shard_map(
        functools.partial(body, sizes),
        mesh=split,
        in_specs=(
            P(BLK, None), P(BLK), P(), P(BLK), P(), P(),
            P(BLK, "x"), P(BLK, "x"), P(BLK),
            P(None, "x"), P(None, "x"), P(None, "x"), P("x", None), P(None, "x"),
            P(), P(),
        ),
        out_specs=(P(BLK, "x"), P(BLK)),
        check_vma=False,
    )
```

```python
import functools

import jax
import jax.numpy as jnp
import numpy as np
from jax import lax
from jax.experimental import pallas as pl
from jax.experimental.pallas import tpu as pltpu
from jax.sharding import Mesh, PartitionSpec as P

DH = 64
F32 = jnp.float32
BF16 = jnp.bfloat16
NEG = -1e30
ANY = pl.ANY
BLK = ("y", "z", "c")


def remote(src, dst, send_sem, recv_sem, **device):
    return pltpu.make_async_remote_copy(
        src_ref=src,
        dst_ref=dst,
        send_sem=send_sem,
        recv_sem=recv_sem,
        device_id=device,
        device_id_type=pl.DeviceIdType.MESH,
    )


def each(count, first, step):
    def run(i, carry):
        step(i)
        return carry

    lax.fori_loop(first, count, run, 0)


def nth_near(i, Z):
    return lax.rem(jnp.where(i % 2 == 1, (i + 1) // 2, Z - i // 2), Z)


def attention_kernel(
    sizes, inv, dq, qlen, bias, seg_ref, var_ref, tcos_ref, tsin_ref, freq_ref, x_in, wq_in, wk_in, wv_in,
    ck, cv, cvar, w_in, attg, w_all,
    xv, wq, wk, wv, order, abuf, bbuf, gbuf, va, vb, kv, qrot, qh, dv, hv, cosv, sinv, qtab, ktab,
    os, sts, ka, vx, qa, acc, mx, oh, sth, ro, rst, att,
    s_x, s_a, r_a, s_va, r_va, s_b, r_b, s_vb, r_vb, s_g, r_g, s_q, r_q, s_dv, r_dv,
    s_r, s_l, r_l, r_r, s_fr, s_fl, r_fl, r_fr, s_s, r_s,
    s_o, r_o, s_t, r_t, x_r, x_l, y_l, y_r, x_fr, x_fl, y_fl, y_fr, mine_sem, here, w_sem,
):
    X, Y, Z, C = sizes
    x, y, z, c = lax.axis_index("x"), lax.axis_index("y"), lax.axis_index("z"), lax.axis_index("c")
    W = Y * C
    w = y * C + c
    bpq = W
    blk = (y * Z + z) * C + c
    slot, cols = qrot.shape[1], qrot.shape[2]
    heads = cols // DH
    pairs = cols // 128
    part_keys = bpq * slot
    barrier = pltpu.get_barrier_semaphore()

    loads = [pltpu.make_async_copy(s, d, s_x.at[n]) for n, (s, d) in
             enumerate(((x_in, xv), (wq_in, wq), (wk_in, wk), (wv_in, wv)))]
    for load in loads:
        load.start()

    def greet(**device):
        pl.semaphore_signal(barrier, inc=1, device_id=device, device_id_type=pl.DeviceIdType.MESH)

    each(W, 1, lambda i: greet(y=(w + i) % W // C, c=(w + i) % W % C))
    each(Z, 1, lambda i: greet(z=(z + i) % Z))
    for side in ((x + 1) % X, (x + X - 1) % X):
        greet(x=side)

    slot_query = [dq[blk * 2 * Z + 2 * j] for j in range(Z)]
    for query in range(Z):
        at = jnp.int32(0)
        for j in range(Z):
            at = jnp.where(slot_query[j] == query, j, at)
        order[query] = at
    lane2 = lax.broadcasted_iota(jnp.int32, (16, cols), 1)
    row2 = lax.broadcasted_iota(jnp.int32, (16, cols), 0)
    feat2 = lane2 % DH
    lane_head = 2 * (lane2 // 128) + (1 - lane2 % 128 // DH)
    delta = jnp.zeros((16, cols), F32)
    for h in range(heads):
        delta = jnp.where(lane_head == h, bias[0, h] - bias[1, h], delta)
    hi = delta.astype(BF16).astype(F32)
    mid = (delta - hi).astype(BF16).astype(F32)
    low = delta - hi - mid
    value = jnp.where(feat2 < 8, hi, jnp.where(feat2 < 16, mid, low))
    value = jnp.where((feat2 < 24) & (feat2 % 8 == row2), value, 0.0)
    qtab[...] = jnp.where((row2 >= 8) & (row2 < 11) & (feat2 == row2 + 16), 1.0, value).astype(BF16)
    lane1, row1 = lane2[:, :128], row2[:, :128]
    feat1 = lane1 % DH
    value = jnp.where((feat1 < 24) & (feat1 % 8 == row1), 1.0, 0.0)
    hit = (((row1 == 8) & (feat1 == 24)) | ((row1 == 9) & (feat1 == 26)) | ((row1 == 10) & (feat1 == 25)))
    ktab[...] = jnp.where(hit, NEG, value).astype(BF16)

    def features(rows, table):
        return lax.dot_general(rows.astype(BF16), table, (((0,), (0,)), ((), ())),
                               preferred_element_type=F32).astype(BF16)

    def marks(var, eight, seg):
        same = jnp.where((row1 < 8) & (var == row1), 1.0, 0.0)
        rows = jnp.where(row1 == 8, eight, same)
        if seg is not None:
            rows = jnp.where(((row1 == 9) & (seg == 0)) | ((row1 == 10) & (seg == 1)), 1.0, rows)
        return rows

    pl.semaphore_wait(barrier, W - 1 + Z - 1 + 2)

    for step in range(1, Y):
        to = (y + step) % Y
        for kind in range(C):
            remote((ck, cv)[kind].at[to], abuf.at[w], s_a.at[to * C + kind], r_a.at[w], y=to, c=kind).start()
            remote(cvar, va.at[w], s_va.at[to * C + kind], r_va.at[w], y=to, c=kind).start()
    for kind in range(C):
        src = (ck, cv)[kind].at[y]

        @pl.when(kind != c)
        def _():
            remote(src, abuf.at[w], s_a.at[y * C + kind], r_a.at[w], c=kind).start()
            remote(cvar, va.at[w], s_va.at[y * C + kind], r_va.at[w], c=kind).start()

        @pl.when(kind == c)
        def _():
            pltpu.make_async_copy(src, abuf.at[w], here.at[0]).start()

    own_var = pltpu.make_async_copy(cvar, va.at[w], here.at[1])
    own_var.start()

    xright, xleft, xfar = (x + 1) % X, (x + X - 1) % X, (x + 2) % X
    w_half = w_in.shape[0] // 2
    w_keep = pltpu.make_async_copy(w_in, w_all.at[x], w_sem.at[8])

    def w_whole(who, send, recv, dev):
        return remote(w_in, w_all.at[who], w_sem.at[send], w_sem.at[recv], x=dev)

    def w_pass(who, piece, send, recv, dev):
        part = w_all.at[who, pl.ds(piece * w_half, w_half)]
        return remote(part, part, w_sem.at[send], w_sem.at[recv], x=dev)

    w_keep.start()
    w_whole(x, 0, 2, xright).start()
    w_whole(x, 1, 3, xleft).start()

    lane = lax.broadcasted_iota(jnp.int32, (slot, cols), 1)
    half = lax.broadcasted_iota(jnp.int32, (slot, 128), 1)
    first_lanes = (lane % DH) < DH // 2
    first_half = (half % DH) < DH // 2
    ones_row = jnp.where(row1 == 10, 1.0, 0.0).astype(BF16)

    def segment(at):
        return seg_ref[at] - (blk * 2 * Z + 2 * at)

    def turn(a, query):
        other = jnp.where(first_lanes, pltpu.roll(a, cols - DH // 2, 1), pltpu.roll(a, DH // 2, 1))
        cosine = jnp.concatenate([cosv[query]] * pairs, axis=1)
        sine = jnp.concatenate([sinv[query]] * pairs, axis=1)
        return a * cosine + other * sine

    loads[0].wait()
    loads[1].wait()

    def project_q(query):
        at = order[query]
        seg = segment(at)
        length = qlen[query].astype(F32)
        count = jnp.sum(jnp.where(seg == 0, 1.0, 0.0), axis=1, keepdims=True)
        base0 = freq_ref[...] * length
        base1 = freq_ref[...] * (length - count)
        second = features(marks(var_ref[at], 1.0, seg), ones_row).astype(F32) > 0.5
        cos_a = jnp.where(second, jnp.cos(base1), jnp.cos(base0))
        sin_a = jnp.where(second, jnp.sin(base1), jnp.sin(base0))
        cosv[query] = cos_a * tcos_ref[...] - sin_a * tsin_ref[...]
        sine = sin_a * tcos_ref[...] + cos_a * tsin_ref[...]
        sinv[query] = jnp.where(first_half, -sine, sine)
        a = jnp.dot(xv[at], wq[...], preferred_element_type=F32)
        qrot[query] = (turn(a, query) * 0.125).astype(BF16)
        dv[query] = var_ref[at]

    each(Z, 0, project_q)

    pltpu.make_async_copy(ck.at[y], abuf.at[w], here.at[0]).wait()
    own_var.wait()

    def wait_a(i):
        src = (w + i) % W
        remote(abuf.at[src], abuf.at[src], s_a.at[src], r_a.at[src], y=src // C, c=src % C).wait_recv()
        remote(va.at[src], va.at[src], s_va.at[src], r_va.at[src], y=src // C, c=src % C).wait_recv()

    each(W, 1, wait_a)

    def line_b(to, at):
        return (remote(abuf.at[:, to], bbuf.at[pl.ds(at * W, W)], s_b.at[to], r_b.at[at], z=to),
                remote(va, vb.at[pl.ds(at * W, W)], s_vb.at[to], r_vb.at[at], z=to))

    def send_b(i):
        for copy in line_b((z + nth_near(i, Z)) % Z, z):
            copy.start()

    each(Z, 1, send_b)
    own_b = pltpu.make_async_copy(abuf.at[:, z], bbuf.at[pl.ds(z * W, W)], here.at[2])
    own_vb = pltpu.make_async_copy(va, vb.at[pl.ds(z * W, W)], here.at[3])
    own_b.start()
    own_vb.start()

    loads[2].wait()
    loads[3].wait()
    wide8 = lax.broadcasted_iota(jnp.int32, (8, cols), 1)
    deep8 = lax.broadcasted_iota(jnp.int32, (8, cols), 0)
    widen = jnp.where(wide8 // DH == deep8, 1.0, 0.0).astype(F32)

    def own_part(query):
        at = order[query]
        xs = xv[at]
        k = turn(jnp.dot(xs, wk[...], preferred_element_type=F32), query).astype(BF16)
        v = jnp.dot(xs, wv[...], preferred_element_type=F32).astype(BF16)
        seg = segment(at)
        qf = features(marks(var_ref[at], 1.0, seg), qtab[...])
        kf = features(marks(var_ref[at], 0.0, seg), ktab[...])
        q = qrot[query]
        stats = jnp.zeros((slot, 128), F32)
        for pair in range(pairs):
            tile = slice(pair * 128, pair * 128 + 128)
            outs = []
            for odd in range(2):
                mine = (half >= DH) if odd else (half < DH)
                qs = jnp.where(mine, q[:, tile], qf[:, tile])
                ks = jnp.where(mine, k[:, tile], kf)
                s = lax.dot_general(qs, ks, (((1,), (1,)), ((), ())), preferred_element_type=F32)
                m = jnp.max(s, axis=1, keepdims=True)
                p = jnp.exp(s - m)
                l = jnp.sum(p, axis=1, keepdims=True)
                outs.append(jnp.dot(p.astype(BF16), v[:, tile], preferred_element_type=F32) / l)
                head = 2 * pair + odd
                stats = jnp.where(half == head, m, jnp.where(half == 4 + head, l, stats))
            os[query, :, tile] = jnp.where(half < DH, outs[0], outs[1])
        sts[query] = jnp.transpose(stats)[:8]

    each(Z, 0, own_part)
    w_whole(xleft, 0, 2, xleft).wait_recv()
    w_pass(xleft, 0, 4, 6, xright).start()
    w_whole(xright, 1, 3, xright).wait_recv()
    w_pass(xright, 1, 5, 7, xleft).start()

    own_b.wait()
    own_vb.wait()

    def wait_b(i):
        src = (z + i) % Z
        part = bbuf.at[pl.ds(src * W, W)]
        remote(part, part, s_b.at[src], r_b.at[src], z=src).wait_recv()
        part = vb.at[pl.ds(src * W, W)]
        remote(part, part, s_vb.at[src], r_vb.at[src], z=src).wait_recv()

    each(Z, 1, wait_b)

    def pick(i):
        gbuf[i] = bbuf[inv[i]]

    each(Z * bpq, 0, pick)

    def line_g(to, at):
        return remote(gbuf.at[pl.ds(to * bpq, bpq)], kv.at[c, y, :, at], s_g.at[to], r_g.at[at], z=to)

    own_g = pltpu.make_async_copy(gbuf.at[pl.ds(z * bpq, bpq)], kv.at[c, y, :, z], here.at[2])
    own_g.start()
    each(Z, 1, lambda i: line_g((z + nth_near(i, Z)) % Z, z).start())

    def line_q(to, at):
        return (remote(qrot.at[to], qh.at[at], s_q.at[to], r_q.at[at], z=to),
                remote(dv.at[to], hv.at[at], s_dv.at[to], r_dv.at[at], z=to))

    def send_q(i):
        for copy in line_q((z + nth_near(i, Z)) % Z, z):
            copy.start()

    each(Z, 1, send_q)
    own_q = pltpu.make_async_copy(qrot.at[z], qh.at[z], here.at[0])
    own_dv = pltpu.make_async_copy(dv.at[z], hv.at[z], here.at[1])
    own_q.start()
    own_dv.start()
    own_g.wait()

    right, left, far, twin = (y + 1) % Y, (y + Y - 1) % Y, (y + 2) % Y, 1 - c

    def ring(kind, piece, at, send, recv, **device):
        part = kv.at[kind, piece, :, at]
        return remote(part, part, send.at[at], recv.at[at], **device)

    def to_twin(piece, at):
        return ring(c, piece, at, s_s.at[piece], r_s.at[piece], c=twin)

    def from_twin(piece, at):
        return ring(twin, piece, at, s_s.at[piece], r_s.at[piece], c=twin)

    to_right = lambda at: ring(c, y, at, s_r, r_l, y=right)
    to_left = lambda at: ring(c, y, at, s_l, r_r, y=left)
    from_left = lambda at: ring(c, left, at, s_r, r_l, y=left)
    from_right = lambda at: ring(c, right, at, s_l, r_r, y=right)
    pass_right = lambda at: ring(c, left, at, s_fr, r_fl, y=right)
    pass_left = lambda at: ring(c, right, at, s_fl, r_fr, y=left)
    far_left = lambda at: ring(c, far, at, s_fr, r_fl, y=left)
    far_right = lambda at: ring(c, far, at, s_fl, r_fr, y=right)

    def share(at):
        to_right(at).start()
        to_left(at).start()
        to_twin(y, at).start()

    def step1(i):
        at = (z + nth_near(i, Z)) % Z
        part = kv.at[c, y, :, at]
        remote(part, part, s_g.at[at], r_g.at[at], z=at).wait_recv()
        share(at)

    def step2(i):
        at = (z + nth_near(i, Z)) % Z
        from_left(at).wait_recv()

        @pl.when(at % 2 == 0)
        def _():
            pass_right(at).start()

        to_twin(left, at).start()
        from_right(at).wait_recv()

        @pl.when(at % 2 == 1)
        def _():
            pass_left(at).start()

        to_twin(right, at).start()

    def step3(i):
        at = (z + nth_near(i, Z)) % Z

        @pl.when(at % 2 == 0)
        def _():
            far_left(at).wait_recv()

        @pl.when(at % 2 == 1)
        def _():
            far_right(at).wait_recv()

        to_twin(far, at).start()

    share(z)

    def steps12(i):
        step1(i)

        @pl.when(i > 2)
        def _():
            step2(i - 3)

    each(Z, 1, steps12)
    each(Z, Z - 3, step2)

    my_len = qlen[z]

    def build(n, piece):
        def one(j):
            var = vb[inv[z * bpq + j], piece]
            place = lane1 + (j * Y * slot + piece * slot)
            kf = features(marks(var, jnp.where(place >= my_len, 1.0, 0.0), None), ktab[...])
            k = kv[0, piece, j].reshape(slot, cols)
            v = kv[1, piece, j].reshape(slot, cols)
            rows = pl.ds(pl.multiple_of(j * slot, slot), slot)
            for pair in range(pairs):
                tile = slice(pair * 128, pair * 128 + 128)
                for odd in range(2):
                    mine = (half >= DH) if odd else (half < DH)
                    ka[2 * pair + odd, n, rows, :] = jnp.where(mine, k[:, tile], kf)
                    vx[2 * pair + odd, n, rows, :] = jnp.where(mine, v[:, tile], jnp.ones_like(kf))

        each(bpq, 0, one)

    def take_q(i):
        at = (z + nth_near(i, Z)) % Z
        qf = features(marks(hv[at], 1.0, None), qtab[...])
        q = qh[at]
        rows = pl.ds(pl.multiple_of(i * slot, slot), slot)
        for pair in range(pairs):
            tile = slice(pair * 128, pair * 128 + 128)
            for odd in range(2):
                mine = (half >= DH) if odd else (half < DH)
                qa[2 * pair + odd, rows, :] = jnp.where(mine, q[:, tile], qf[:, tile])

    def wait_q(i):
        at = (z + nth_near(i, Z)) % Z

        @pl.when(i == 0)
        def _():
            own_q.wait()
            own_dv.wait()

        @pl.when(i > 0)
        def _():
            for copy in line_q(at, at):
                copy.wait_recv()

        take_q(i)

    side = Z // 2 * slot

    def attend(n, group):
        rows = pl.ds(pl.multiple_of(group * side, side), side)

        def score(h):
            return lax.dot_general(qa[h, rows, :], ka[h, n], (((1,), (1,)), ((), ())), preferred_element_type=F32)

        def weigh(h, s):
            old = mx[h, rows, :][:, :1]
            m = jnp.maximum(old, jnp.max(s, axis=1, keepdims=True))
            o = jnp.dot(jnp.exp(s - m).astype(BF16), vx[h, n], preferred_element_type=F32)
            acc[h, rows, :] = acc[h, rows, :] * jnp.exp(old - m) + o
            mx[h, rows, :] = jnp.broadcast_to(m, (side, 128))

        s = score(0)
        for h in range(heads):
            later = score(h + 1) if h + 1 < heads else None
            weigh(h, s)
            s = later

    def twins(piece):
        each(Z, 0, lambda at: from_twin(piece, at).wait_recv())

    def line_o(to, at):
        return (remote(oh.at[to], ro.at[at], s_o.at[to], r_o.at[at], z=to),
                remote(sth.at[to], rst.at[at], s_t.at[to], r_t.at[at], z=to))

    def settle(i):
        at = (z + nth_near(i, Z)) % Z
        rows = pl.ds(pl.multiple_of(i * slot, slot), slot)
        stats = jnp.zeros((slot, 128), F32)
        for pair in range(pairs):
            outs = []
            for odd in range(2):
                mine = (half >= DH) if odd else (half < DH)
                head = 2 * pair + odd
                total = acc[head, rows, :]
                turned = pltpu.roll(total, DH, 1)
                l = jnp.where(mine, turned, total)
                outs.append(total / l)
                stats = jnp.where(half == head, mx[head, rows, :], jnp.where(half == 4 + head, l, stats))
            oh[at, :, pair * 128:pair * 128 + 128] = jnp.where(half < DH, outs[0], outs[1]).astype(BF16)
        sth[at] = jnp.transpose(stats)[:8]

    own_o = pltpu.make_async_copy(oh.at[z], ro.at[z], here.at[2])
    own_t = pltpu.make_async_copy(sth.at[z], rst.at[z], here.at[3])

    def settle_send(i):
        settle(i)
        at = (z + nth_near(i, Z)) % Z

        @pl.when(i == 0)
        def _():
            own_o.start()
            own_t.start()

        @pl.when(i > 0)
        def _():
            for copy in line_o(at, z):
                copy.start()

    mid_row = slot // 2
    keep = lambda at: pltpu.make_async_copy(att.at[at], attg.at[x, at], mine_sem.at[at])

    def xring(src, who, at, send, recv, dev):
        return remote(src, attg.at[who, at], send.at[at], recv.at[at], x=dev)

    def xpass(who, at, piece, send, recv, dev):
        part = attg.at[who, at, pl.ds(piece * mid_row, mid_row)]
        return remote(part, part, send.at[at], recv.at[at], x=dev)

    xto_right = lambda at: xring(att.at[at], x, at, x_r, y_l, xright)
    xto_left = lambda at: xring(att.at[at], x, at, x_l, y_r, xleft)
    xfrom_left = lambda at: xring(att.at[at], xleft, at, x_r, y_l, xleft)
    xfrom_right = lambda at: xring(att.at[at], xright, at, x_l, y_r, xright)
    xpass_right = lambda at: xpass(xleft, at, 0, x_fr, y_fl, xright)
    xpass_left = lambda at: xpass(xright, at, 1, x_fl, y_fr, xleft)
    xfar_left = lambda at: xpass(xfar, at, 0, x_fr, y_fl, xleft)
    xfar_right = lambda at: xpass(xfar, at, 1, x_fl, y_fr, xright)

    def join(at):
        far_m, far_l = rst[at][0:4], rst[at][4:8]
        own_m, own_l = sts[at][0:4], sts[at][4:8]
        m = jnp.maximum(far_m, own_m)
        a = far_l * jnp.exp(far_m - m)
        b = own_l * jnp.exp(own_m - m)
        total = a + b
        zero = jnp.zeros_like(total)

        def wide(share):
            return lax.dot_general(
                jnp.concatenate([share, zero], axis=0), widen, (((0,), (0,)), ((), ())),
                preferred_element_type=F32, precision=lax.Precision.HIGHEST)

        value = wide(a / total) * ro[at].astype(F32) + wide(b / total) * os[at]
        att[at] = value.astype(BF16)
        keep(at).start()
        xto_right(at).start()
        xto_left(at).start()

    def home(i):
        return (z + Z - nth_near(i, Z)) % Z

    def arrive(i):
        at = home(i)

        @pl.when(i == 0)
        def _():
            own_o.wait()
            own_t.wait()

        @pl.when(i > 0)
        def _():
            for copy in line_o(at, at):
                copy.wait_recv()

        join(at)

    def forward(i):
        at = home(i)
        xfrom_left(at).wait_recv()
        xpass_right(at).start()
        xfrom_right(at).wait_recv()
        xpass_left(at).start()

    hz = Z // 2

    def main(t):
        group, n = t // Y, t % Y
        piece = jnp.where(n == 0, y, jnp.where(n == 1, left, jnp.where(n == 2, right, far)))

        @pl.when(n == 0)
        def _():
            rows = pl.ds(pl.multiple_of(group * side, side), side)
            for h in range(heads):
                acc[h, rows, :] = jnp.zeros((side, 128), F32)
                mx[h, rows, :] = jnp.full((side, 128), -3e38, F32)
            each(hz, 0, lambda i: wait_q(group * hz + i))

        @pl.when(t == 2)
        def _():
            each(Z, 0, step3)

        @pl.when(t < Y)
        def _():
            twins(piece)
            build(n, piece)

        attend(n, group)

        @pl.when(t == Y - 1)
        def _():
            each(hz, 0, settle_send)

        @pl.when(t == Y)
        def _():
            arrive(0)

        @pl.when(t == Y + 1)
        def _():
            each(hz, 1, arrive)

        @pl.when(t == Y + 2)
        def _():
            forward(0)

    each(2 * Y, 0, main)
    each(Z, hz, settle_send)
    each(hz, 1, forward)

    def late(i):
        arrive(i)

        @pl.when(i > Z // 2)
        def _():
            forward(i - 1)

    each(Z, Z // 2, late)
    forward(Z - 1)

    def finish(at):
        xfar_left(at).wait_recv()
        xfar_right(at).wait_recv()
        keep(at).wait()
        for copy in (xto_right(at), xto_left(at), xpass_right(at), xpass_left(at), to_right(at), to_left(at)):
            copy.wait_send()

        @pl.when(at % 2 == 0)
        def _():
            pass_right(at).wait_send()

        @pl.when(at % 2 == 1)
        def _():
            pass_left(at).wait_send()

        for piece in range(Y):
            to_twin(piece, at).wait_send()

    each(Z, 0, finish)
    w_keep.wait()
    w_pass(xfar, 0, 4, 6, xleft).wait_recv()
    w_pass(xfar, 1, 5, 7, xright).wait_recv()
    for copy in (w_whole(x, 0, 2, xright), w_whole(x, 1, 3, xleft),
                 w_pass(xleft, 0, 4, 6, xright), w_pass(xright, 1, 5, 7, xleft)):
        copy.wait_send()

    def end_line(i):
        at = (z + i) % Z
        for copy in line_b(at, at) + line_q(at, at) + line_o(at, at) + (line_g(at, at),):
            copy.wait_send()

    each(Z, 1, end_line)

    def end_cluster(i):
        to = (w + i) % W
        remote(abuf.at[to], abuf.at[to], s_a.at[to], r_a.at[to], y=to // C, c=to % C).wait_send()
        remote(cvar, va.at[to], s_va.at[to], r_va.at[to], y=to // C, c=to % C).wait_send()

    each(W, 1, end_cluster)


def out_kernel(dq, ids, att_ref, next_ref, w_ref, x_ref, seg_ref, gain_ref, read_ref, upd_ref, pool_ref, y_ref):
    step = pl.program_id(0)
    parts, slot, cols = att_ref.shape[0], att_ref.shape[2], att_ref.shape[3]
    y = None
    for p in range(parts):
        rows = jnp.concatenate([att_ref[p, 0], next_ref[p, 0]], axis=0)
        part = jnp.dot(rows, w_ref[p], preferred_element_type=F32)
        y = part if y is None else y + part
    y_ref[...] = y
    upd_ref[...] = y_ref[:, pl.ds(pl.multiple_of(ids[1] * cols, cols), cols)]
    hidden = x_ref[...].astype(F32) + y
    square = jnp.sum(hidden * hidden, axis=1, keepdims=True)
    weighted = jnp.sum(hidden * (gain_ref[...] * read_ref[...]), axis=1, keepdims=True)
    score = weighted * lax.rsqrt(square / y.shape[1] + 1e-06)
    row = lax.broadcasted_iota(jnp.int32, (8, slot), 0)
    for n in range(2):
        first = (ids[0] * pl.num_programs(0) * 2 + step * 2 + n) * 2
        member = jnp.where((row < 2) & (seg_ref[n] - first == row), 1.0, 0.0)
        own = jnp.broadcast_to(score[n * slot:n * slot + slot], (slot, 128))
        sums = jnp.dot(member, own, preferred_element_type=F32, precision=lax.Precision.HIGHEST)
        count = jnp.maximum(jnp.sum(member, axis=1, keepdims=True), 1.0)
        pool_ref[n] = sums / count


def body(sizes, doc_x, doc_seg, doc_query, doc_var, query_len, block_perm, cache_k, cache_v, cache_var,
         w_query, w_key, w_value, w_out, var_bias, norm_gain, readout):
    X, Y, Z, C = sizes
    W = Y * C
    tokens, cols = doc_x.shape[0], w_query.shape[1]
    features = doc_x.shape[1]
    heads = cols // DH
    slot = tokens // Z
    crows = cache_k.shape[0]
    blocks = Y * Z * C
    bpq = blocks // Z
    piece = crows // (Y * Z)
    part_keys = bpq * slot
    i32 = jnp.int32
    dma = pltpu.SemaphoreType.DMA

    at = jnp.arange(blocks, dtype=i32)
    place = (at // C % Z) * W + (at // (Z * C)) * C + at % C
    inv = jnp.sum(jnp.where(block_perm[None, :] == at[:, None], place[None, :], 0), axis=1)

    half_size = DH // 2
    frequency = 10000.0 ** (-np.arange(half_size) / half_size)
    frequency = np.tile(frequency.astype(np.float32), 128 // half_size)
    turns = np.arange(slot)[:, None] * frequency.astype(np.float64)[None, :]
    seg = doc_seg.reshape(Z, 1, slot)

    vm = lambda *shape: pltpu.VMEM(shape, BF16)
    vf = lambda *shape: pltpu.VMEM(shape, F32)
    vi = lambda *shape: pltpu.VMEM(shape, i32)
    smem = pl.BlockSpec(memory_space=pltpu.SMEM)
    vmem = pl.BlockSpec(memory_space=pltpu.VMEM)
    hbm = pl.BlockSpec(memory_space=ANY)
    attended, w_all = pl.pallas_call(
        functools.partial(attention_kernel, sizes),
        in_specs=[smem] * 4 + [vmem] * 5 + [hbm] * 8,
        out_specs=[hbm] * 2,
        out_shape=[
            jax.ShapeDtypeStruct((X, Z, slot, cols), BF16),
            jax.ShapeDtypeStruct((X, cols, features), BF16),
        ],
        scratch_shapes=[
            vm(Z, slot, features), vm(features, cols), vm(features, cols), vm(features, cols),
            pltpu.SMEM((Z,), i32),
            vm(W, Z, piece, cols), vm(Z * W, piece, cols), vm(Z * bpq, piece, cols),
            vi(W, Y, 1, slot), vi(Z * W, Y, 1, slot),
            vm(C, Y, bpq, Z, piece, cols),
            vm(Z, slot, cols), vm(Z, slot, cols), vi(Z, 1, slot), vi(Z, 1, slot),
            vf(Z, slot, 128), vf(Z, slot, 128), vm(16, cols), vm(16, 128),
            vf(Z, slot, cols), vf(Z, 8, slot),
            vm(heads, Y, part_keys, 128), vm(heads, Y, part_keys, 128), vm(heads, tokens, 128),
            vf(heads, tokens, 128), vf(heads, tokens, 128),
            vm(Z, slot, cols), vf(Z, 8, slot), vm(Z, slot, cols), vf(Z, 8, slot), vm(Z, slot, cols),
            dma((4,)),
        ] + [dma((W,))] * 4 + [dma((Z,))] * 10 + [dma((Z,))] * 8 + [dma((Y, Z))] * 2
        + [dma((Z,))] * 4 + [dma((Z,))] * 9 + [dma((4,)), dma((9,))],
        compiler_params=pltpu.CompilerParams(
            collective_id=0, has_side_effects=True, vmem_limit_bytes=56 << 20),
        name="attention",
    )(inv, doc_query, query_len, var_bias, seg, doc_var.reshape(Z, 1, slot),
      jnp.asarray(np.cos(turns), F32), jnp.asarray(np.sin(turns), F32), jnp.asarray(frequency)[None, :],
      doc_x.reshape(Z, slot, features), w_query, w_key, w_value,
      cache_k.reshape(Y, Z, piece, cols), cache_v.reshape(Y, Z, piece, cols), cache_var.reshape(Y, 1, slot), w_out)

    full = lambda *shape: pl.BlockSpec(shape, lambda i, *_: (0,) * len(shape))
    ids = jnp.stack([lax.axis_index(BLK), lax.axis_index("x")]).astype(i32)
    update, pooled = pl.pallas_call(
        out_kernel,
        grid_spec=pltpu.PrefetchScalarGridSpec(
            num_scalar_prefetch=2,
            grid=(Z // 2,),
            in_specs=[
                pl.BlockSpec((X, 1, slot, cols), lambda i, d, n: (0, d[n[0] * 2 * Z + 4 * i], 0, 0)),
                pl.BlockSpec((X, 1, slot, cols), lambda i, d, n: (0, d[n[0] * 2 * Z + 4 * i + 2], 0, 0)),
                full(X, cols, features),
                pl.BlockSpec((2 * slot, features), lambda i, d, n: (i, 0)),
                pl.BlockSpec((2, 1, slot), lambda i, d, n: (i, 0, 0)),
                full(1, features),
                full(1, features),
            ],
            out_specs=[
                pl.BlockSpec((2 * slot, cols), lambda i, d, n: (i, 0)),
                pl.BlockSpec((2, 8, 128), lambda i, d, n: (i, 0, 0)),
            ],
            scratch_shapes=[pltpu.VMEM((2 * slot, features), F32)],
        ),
        out_shape=[
            jax.ShapeDtypeStruct((tokens, cols), F32),
            jax.ShapeDtypeStruct((Z, 8, 128), F32),
        ],
        compiler_params=pltpu.CompilerParams(vmem_limit_bytes=60 << 20),
        name="out_part",
    )(doc_query, ids, attended, attended, w_all, doc_x, seg, norm_gain.reshape(1, features),
      readout.reshape(1, features))
    return update, pooled[:, :2, 0].reshape(2 * Z)


def solution(mesh):
    heads = mesh.shape["head"]
    cores = 2
    across = 4
    along = mesh.shape["blk"] // (across * cores)
    sizes = (heads, across, along, cores)
    split = Mesh(mesh.devices.reshape(sizes), ("x", "y", "z", "c"))
    return jax.shard_map(
        functools.partial(body, sizes),
        mesh=split,
        in_specs=(
            P(BLK, None), P(BLK), P(), P(BLK), P(), P(),
            P(BLK, "x"), P(BLK, "x"), P(BLK),
            P(None, "x"), P(None, "x"), P(None, "x"), P("x", None), P(None, "x"),
            P(), P(),
        ),
        out_specs=(P(BLK, "x"), P(BLK)),
        check_vma=False,
    )
```

```python
import functools

import jax
import jax.numpy as jnp
import numpy as np
from jax import lax
from jax.experimental import pallas as pl
from jax.experimental.pallas import tpu as pltpu
from jax.sharding import Mesh, PartitionSpec as P

DH = 64
F32 = jnp.float32
BF16 = jnp.bfloat16
NEG = -1e30
ANY = pl.ANY
BLK = ("y", "z", "c")


def remote(src, dst, send_sem, recv_sem, **device):
    return pltpu.make_async_remote_copy(
        src_ref=src,
        dst_ref=dst,
        send_sem=send_sem,
        recv_sem=recv_sem,
        device_id=device,
        device_id_type=pl.DeviceIdType.MESH,
    )


def each(count, first, step):
    def run(i, carry):
        step(i)
        return carry

    lax.fori_loop(first, count, run, 0)


def nth_near(i, Z):
    return lax.rem(jnp.where(i % 2 == 1, (i + 1) // 2, Z - i // 2), Z)


def attention_kernel(
    sizes, inv, dq, qlen, bias, seg_ref, var_ref, tcos_ref, tsin_ref, freq_ref, x_in, wq_in, wk_in, wv_in,
    ck, cv, cvar, w_in, attg, w_all,
    xv, wq, wk, wv, order, abuf, bbuf, gbuf, va, vb, kv, qrot, qh, dv, hv, cosv, sinv, qtab, ktab,
    os, sts, kfs, qfs, ka, vx, qa, acc, mx, oh, sth, ro, rst, att,
    s_x, s_a, r_a, s_va, r_va, s_b, r_b, s_vb, r_vb, s_g, r_g, s_q, r_q, s_dv, r_dv,
    s_r, s_l, r_l, r_r, s_fr, s_fl, r_fl, r_fr, s_s, r_s,
    s_o, r_o, s_t, r_t, x_r, x_l, y_l, y_r, x_fr, x_fl, y_fl, y_fr, mine_sem, here, w_sem,
):
    X, Y, Z, C = sizes
    x, y, z, c = lax.axis_index("x"), lax.axis_index("y"), lax.axis_index("z"), lax.axis_index("c")
    W = Y * C
    w = y * C + c
    bpq = W
    blk = (y * Z + z) * C + c
    slot, cols = qrot.shape[1], qrot.shape[2]
    heads = cols // DH
    pairs = cols // 128
    part_keys = bpq * slot
    barrier = pltpu.get_barrier_semaphore()

    loads = [pltpu.make_async_copy(s, d, s_x.at[n]) for n, (s, d) in
             enumerate(((x_in, xv), (wq_in, wq), (wk_in, wk), (wv_in, wv)))]
    for load in loads:
        load.start()

    def greet(**device):
        pl.semaphore_signal(barrier, inc=1, device_id=device, device_id_type=pl.DeviceIdType.MESH)

    each(W, 1, lambda i: greet(y=(w + i) % W // C, c=(w + i) % W % C))
    each(Z, 1, lambda i: greet(z=(z + i) % Z))
    for side in ((x + 1) % X, (x + X - 1) % X):
        greet(x=side)

    slot_query = [dq[blk * 2 * Z + 2 * j] for j in range(Z)]
    for query in range(Z):
        at = jnp.int32(0)
        for j in range(Z):
            at = jnp.where(slot_query[j] == query, j, at)
        order[query] = at
    lane2 = lax.broadcasted_iota(jnp.int32, (16, cols), 1)
    row2 = lax.broadcasted_iota(jnp.int32, (16, cols), 0)
    feat2 = lane2 % DH
    lane_head = 2 * (lane2 // 128) + (1 - lane2 % 128 // DH)
    delta = jnp.zeros((16, cols), F32)
    for h in range(heads):
        delta = jnp.where(lane_head == h, bias[0, h] - bias[1, h], delta)
    hi = delta.astype(BF16).astype(F32)
    mid = (delta - hi).astype(BF16).astype(F32)
    low = delta - hi - mid
    value = jnp.where(feat2 < 8, hi, jnp.where(feat2 < 16, mid, low))
    value = jnp.where((feat2 < 24) & (feat2 % 8 == row2), value, 0.0)
    qtab[...] = jnp.where((row2 >= 8) & (row2 < 11) & (feat2 == row2 + 16), 1.0, value).astype(BF16)
    lane1, row1 = lane2[:, :128], row2[:, :128]
    feat1 = lane1 % DH
    value = jnp.where((feat1 < 24) & (feat1 % 8 == row1), 1.0, 0.0)
    hit = (((row1 == 8) & (feat1 == 24)) | ((row1 == 9) & (feat1 == 26)) | ((row1 == 10) & (feat1 == 25)))
    ktab[...] = jnp.where(hit, NEG, value).astype(BF16)

    def features(rows, table):
        return lax.dot_general(rows.astype(BF16), table, (((0,), (0,)), ((), ())),
                               preferred_element_type=F32).astype(BF16)

    def marks(var, eight, seg):
        same = jnp.where((row1 < 8) & (var == row1), 1.0, 0.0)
        rows = jnp.where(row1 == 8, eight, same)
        if seg is not None:
            rows = jnp.where(((row1 == 9) & (seg == 0)) | ((row1 == 10) & (seg == 1)), 1.0, rows)
        return rows

    pl.semaphore_wait(barrier, W - 1 + Z - 1 + 2)

    for step in range(1, Y):
        to = (y + step) % Y
        for kind in range(C):
            remote((ck, cv)[kind].at[to], abuf.at[w], s_a.at[to * C + kind], r_a.at[w], y=to, c=kind).start()
            remote(cvar, va.at[w], s_va.at[to * C + kind], r_va.at[w], y=to, c=kind).start()
    for kind in range(C):
        src = (ck, cv)[kind].at[y]

        @pl.when(kind != c)
        def _():
            remote(src, abuf.at[w], s_a.at[y * C + kind], r_a.at[w], c=kind).start()
            remote(cvar, va.at[w], s_va.at[y * C + kind], r_va.at[w], c=kind).start()

        @pl.when(kind == c)
        def _():
            pltpu.make_async_copy(src, abuf.at[w], here.at[0]).start()

    own_var = pltpu.make_async_copy(cvar, va.at[w], here.at[1])
    own_var.start()

    xright, xleft, xfar = (x + 1) % X, (x + X - 1) % X, (x + 2) % X
    w_half = w_in.shape[0] // 2
    w_keep = pltpu.make_async_copy(w_in, w_all.at[x], w_sem.at[8])

    def w_whole(who, send, recv, dev):
        return remote(w_in, w_all.at[who], w_sem.at[send], w_sem.at[recv], x=dev)

    def w_pass(who, piece, send, recv, dev):
        part = w_all.at[who, pl.ds(piece * w_half, w_half)]
        return remote(part, part, w_sem.at[send], w_sem.at[recv], x=dev)

    w_keep.start()
    w_whole(x, 0, 2, xright).start()
    w_whole(x, 1, 3, xleft).start()

    lane = lax.broadcasted_iota(jnp.int32, (slot, cols), 1)
    half = lax.broadcasted_iota(jnp.int32, (slot, 128), 1)
    first_lanes = (lane % DH) < DH // 2
    first_half = (half % DH) < DH // 2
    ones_row = jnp.where(row1 == 10, 1.0, 0.0).astype(BF16)

    def segment(at):
        return seg_ref[at] - (blk * 2 * Z + 2 * at)

    def turn(a, query):
        other = jnp.where(first_lanes, pltpu.roll(a, cols - DH // 2, 1), pltpu.roll(a, DH // 2, 1))
        cosine = jnp.concatenate([cosv[query]] * pairs, axis=1)
        sine = jnp.concatenate([sinv[query]] * pairs, axis=1)
        return a * cosine + other * sine

    loads[0].wait()
    loads[1].wait()

    def project_q(query):
        at = order[query]
        seg = segment(at)
        length = qlen[query].astype(F32)
        count = jnp.sum(jnp.where(seg == 0, 1.0, 0.0), axis=1, keepdims=True)
        base0 = freq_ref[...] * length
        base1 = freq_ref[...] * (length - count)
        second = features(marks(var_ref[at], 1.0, seg), ones_row).astype(F32) > 0.5
        cos_a = jnp.where(second, jnp.cos(base1), jnp.cos(base0))
        sin_a = jnp.where(second, jnp.sin(base1), jnp.sin(base0))
        cosv[query] = cos_a * tcos_ref[...] - sin_a * tsin_ref[...]
        sine = sin_a * tcos_ref[...] + cos_a * tsin_ref[...]
        sinv[query] = jnp.where(first_half, -sine, sine)
        a = jnp.dot(xv[at], wq[...], preferred_element_type=F32)
        qrot[query] = (turn(a, query) * 0.125).astype(BF16)
        dv[query] = var_ref[at]

    each(Z, 0, project_q)

    pltpu.make_async_copy(ck.at[y], abuf.at[w], here.at[0]).wait()
    own_var.wait()

    def wait_a(i):
        src = (w + i) % W
        remote(abuf.at[src], abuf.at[src], s_a.at[src], r_a.at[src], y=src // C, c=src % C).wait_recv()
        remote(va.at[src], va.at[src], s_va.at[src], r_va.at[src], y=src // C, c=src % C).wait_recv()

    each(W, 1, wait_a)

    def line_b(to, at):
        return (remote(abuf.at[:, to], bbuf.at[pl.ds(at * W, W)], s_b.at[to], r_b.at[at], z=to),
                remote(va, vb.at[pl.ds(at * W, W)], s_vb.at[to], r_vb.at[at], z=to),
                remote(dv.at[to], hv.at[at], s_dv.at[to], r_dv.at[at], z=to))

    def send_b(i):
        for copy in line_b((z + nth_near(i, Z)) % Z, z):
            copy.start()

    each(Z, 1, send_b)
    own_b = pltpu.make_async_copy(abuf.at[:, z], bbuf.at[pl.ds(z * W, W)], here.at[2])
    own_vb = pltpu.make_async_copy(va, vb.at[pl.ds(z * W, W)], here.at[3])
    own_dv = pltpu.make_async_copy(dv.at[z], hv.at[z], here.at[1])
    own_b.start()
    own_vb.start()
    own_dv.start()

    loads[2].wait()
    loads[3].wait()
    wide8 = lax.broadcasted_iota(jnp.int32, (8, cols), 1)
    deep8 = lax.broadcasted_iota(jnp.int32, (8, cols), 0)
    widen = jnp.where(wide8 // DH == deep8, 1.0, 0.0).astype(F32)

    def own_part(query):
        at = order[query]
        xs = xv[at]
        k = turn(jnp.dot(xs, wk[...], preferred_element_type=F32), query).astype(BF16)
        v = jnp.dot(xs, wv[...], preferred_element_type=F32).astype(BF16)
        seg = segment(at)
        qf = features(marks(var_ref[at], 1.0, seg), qtab[...])
        kf = features(marks(var_ref[at], 0.0, seg), ktab[...])
        q = qrot[query]
        stats = jnp.zeros((slot, 128), F32)
        for pair in range(pairs):
            tile = slice(pair * 128, pair * 128 + 128)
            outs = []
            for odd in range(2):
                mine = (half >= DH) if odd else (half < DH)
                qs = jnp.where(mine, q[:, tile], qf[:, tile])
                ks = jnp.where(mine, k[:, tile], kf)
                s = lax.dot_general(qs, ks, (((1,), (1,)), ((), ())), preferred_element_type=F32)
                m = jnp.max(s, axis=1, keepdims=True)
                p = jnp.exp(s - m)
                l = jnp.sum(p, axis=1, keepdims=True)
                outs.append(jnp.dot(p.astype(BF16), v[:, tile], preferred_element_type=F32) / l)
                head = 2 * pair + odd
                stats = jnp.where(half == head, m, jnp.where(half == 4 + head, l, stats))
            os[query, :, tile] = jnp.where(half < DH, outs[0], outs[1])
        sts[query] = jnp.transpose(stats)[:8]

    early = Z - 2
    each(early, 0, own_part)
    w_whole(xleft, 0, 2, xleft).wait_recv()
    w_pass(xleft, 0, 4, 6, xright).start()
    w_whole(xright, 1, 3, xright).wait_recv()
    w_pass(xright, 1, 5, 7, xleft).start()

    own_b.wait()
    own_vb.wait()
    own_dv.wait()

    def wait_b(i):
        src = (z + i) % Z
        part = bbuf.at[pl.ds(src * W, W)]
        remote(part, part, s_b.at[src], r_b.at[src], z=src).wait_recv()
        part = vb.at[pl.ds(src * W, W)]
        remote(part, part, s_vb.at[src], r_vb.at[src], z=src).wait_recv()
        remote(hv.at[src], hv.at[src], s_dv.at[src], r_dv.at[src], z=src).wait_recv()

    each(Z, 1, wait_b)

    def pick(i):
        gbuf[i] = bbuf[inv[i]]

    each(Z * bpq, 0, pick)

    def line_g(to, at):
        return remote(gbuf.at[pl.ds(to * bpq, bpq)], kv.at[c, y, :, at], s_g.at[to], r_g.at[at], z=to)

    own_g = pltpu.make_async_copy(gbuf.at[pl.ds(z * bpq, bpq)], kv.at[c, y, :, z], here.at[2])
    own_g.start()
    each(Z, 1, lambda i: line_g((z + nth_near(i, Z)) % Z, z).start())

    def line_q(to, at):
        return remote(qrot.at[to], qh.at[at], s_q.at[to], r_q.at[at], z=to)

    each(Z, 1, lambda i: line_q((z + nth_near(i, Z)) % Z, z).start())
    own_q = pltpu.make_async_copy(qrot.at[z], qh.at[z], here.at[0])
    own_q.start()
    own_g.wait()

    right, left, far, twin = (y + 1) % Y, (y + Y - 1) % Y, (y + 2) % Y, 1 - c

    def ring(kind, piece, at, send, recv, **device):
        part = kv.at[kind, piece, :, at]
        return remote(part, part, send.at[at], recv.at[at], **device)

    def to_twin(piece, at):
        return ring(c, piece, at, s_s.at[piece], r_s.at[piece], c=twin)

    def from_twin(piece, at):
        return ring(twin, piece, at, s_s.at[piece], r_s.at[piece], c=twin)

    to_right = lambda at: ring(c, y, at, s_r, r_l, y=right)
    to_left = lambda at: ring(c, y, at, s_l, r_r, y=left)
    from_left = lambda at: ring(c, left, at, s_r, r_l, y=left)
    from_right = lambda at: ring(c, right, at, s_l, r_r, y=right)
    pass_right = lambda at: ring(c, left, at, s_fr, r_fl, y=right)
    pass_left = lambda at: ring(c, right, at, s_fl, r_fr, y=left)
    far_left = lambda at: ring(c, far, at, s_fr, r_fl, y=left)
    far_right = lambda at: ring(c, far, at, s_fl, r_fr, y=right)

    def share(at):
        to_right(at).start()
        to_left(at).start()
        to_twin(y, at).start()

    def step1(i):
        at = (z + nth_near(i, Z)) % Z
        part = kv.at[c, y, :, at]
        remote(part, part, s_g.at[at], r_g.at[at], z=at).wait_recv()
        share(at)

    def step2(i):
        at = (z + nth_near(i, Z)) % Z
        from_left(at).wait_recv()

        @pl.when(at % 2 == 0)
        def _():
            pass_right(at).start()

        to_twin(left, at).start()
        from_right(at).wait_recv()

        @pl.when(at % 2 == 1)
        def _():
            pass_left(at).start()

        to_twin(right, at).start()

    def step3(i):
        at = (z + nth_near(i, Z)) % Z

        @pl.when(at % 2 == 0)
        def _():
            far_left(at).wait_recv()

        @pl.when(at % 2 == 1)
        def _():
            far_right(at).wait_recv()

        to_twin(far, at).start()

    share(z)
    my_len = qlen[z]

    def key_marks(i):
        piece, j = i // bpq, i % bpq
        var = vb[inv[z * bpq + j], piece]
        place = lane1 + (j * Y * slot + piece * slot)
        rows = pl.ds(pl.multiple_of(j * slot, slot), slot)
        kfs[piece, rows, :] = features(marks(var, jnp.where(place >= my_len, 1.0, 0.0), None), ktab[...])

    def query_marks(at):
        qfs[at] = features(marks(hv[at], 1.0, None), qtab[...])

    def steps12(i):
        step1(i)

        @pl.when(i < 5)
        def _():
            each(bpq * i, bpq * (i - 1), key_marks)

        @pl.when(i == 5)
        def _():
            each(Z, 0, query_marks)

        @pl.when(i > 5)
        def _():
            own_part(early + i - 6)

        @pl.when(i > 2)
        def _():
            step2(i - 3)

    each(Z, 1, steps12)

    def build(n, piece):
        def one(j):
            k = kv[0, piece, j].reshape(slot, cols)
            v = kv[1, piece, j].reshape(slot, cols)
            rows = pl.ds(pl.multiple_of(j * slot, slot), slot)
            kf = kfs[piece, rows, :]
            for pair in range(pairs):
                tile = slice(pair * 128, pair * 128 + 128)
                for odd in range(2):
                    mine = (half >= DH) if odd else (half < DH)
                    ka[2 * pair + odd, n, rows, :] = jnp.where(mine, k[:, tile], kf)
                    vx[2 * pair + odd, n, rows, :] = jnp.where(mine, v[:, tile], jnp.ones_like(kf))

        each(bpq, 0, one)

    def take_q(i):
        at = (z + nth_near(i, Z)) % Z
        qf = qfs[at]
        q = qh[at]
        rows = pl.ds(pl.multiple_of(i * slot, slot), slot)
        for pair in range(pairs):
            tile = slice(pair * 128, pair * 128 + 128)
            for odd in range(2):
                mine = (half >= DH) if odd else (half < DH)
                qa[2 * pair + odd, rows, :] = jnp.where(mine, q[:, tile], qf[:, tile])

    def wait_q(i):
        at = (z + nth_near(i, Z)) % Z

        @pl.when(i == 0)
        def _():
            own_q.wait()

        @pl.when(i > 0)
        def _():
            line_q(at, at).wait_recv()

        take_q(i)

    side = Z // 2 * slot

    def attend(n, group):
        rows = pl.ds(pl.multiple_of(group * side, side), side)

        def score(h):
            return lax.dot_general(qa[h, rows, :], ka[h, n], (((1,), (1,)), ((), ())), preferred_element_type=F32)

        def weigh(h, s):
            old = mx[h, rows, :][:, :1]
            m = jnp.maximum(old, jnp.max(s, axis=1, keepdims=True))
            o = jnp.dot(jnp.exp(s - m).astype(BF16), vx[h, n], preferred_element_type=F32)
            acc[h, rows, :] = acc[h, rows, :] * jnp.exp(old - m) + o
            mx[h, rows, :] = jnp.broadcast_to(m, (side, 128))

        s = score(0)
        for h in range(heads):
            later = score(h + 1) if h + 1 < heads else None
            weigh(h, s)
            s = later

    def twins(piece):
        each(Z, 0, lambda at: from_twin(piece, at).wait_recv())

    def line_o(to, at):
        return (remote(oh.at[to], ro.at[at], s_o.at[to], r_o.at[at], z=to),
                remote(sth.at[to], rst.at[at], s_t.at[to], r_t.at[at], z=to))

    def settle(i):
        at = (z + nth_near(i, Z)) % Z
        rows = pl.ds(pl.multiple_of(i * slot, slot), slot)
        stats = jnp.zeros((slot, 128), F32)
        for pair in range(pairs):
            outs = []
            for odd in range(2):
                mine = (half >= DH) if odd else (half < DH)
                head = 2 * pair + odd
                total = acc[head, rows, :]
                turned = pltpu.roll(total, DH, 1)
                l = jnp.where(mine, turned, total)
                outs.append(total / l)
                stats = jnp.where(half == head, mx[head, rows, :], jnp.where(half == 4 + head, l, stats))
            oh[at, :, pair * 128:pair * 128 + 128] = jnp.where(half < DH, outs[0], outs[1]).astype(BF16)
        sth[at] = jnp.transpose(stats)[:8]

    own_o = pltpu.make_async_copy(oh.at[z], ro.at[z], here.at[2])
    own_t = pltpu.make_async_copy(sth.at[z], rst.at[z], here.at[3])

    def settle_send(i):
        settle(i)
        at = (z + nth_near(i, Z)) % Z

        @pl.when(i == 0)
        def _():
            own_o.start()
            own_t.start()

        @pl.when(i > 0)
        def _():
            for copy in line_o(at, z):
                copy.start()

    mid_row = slot // 2
    keep = lambda at: pltpu.make_async_copy(att.at[at], attg.at[x, at], mine_sem.at[at])

    def xring(src, who, at, send, recv, dev):
        return remote(src, attg.at[who, at], send.at[at], recv.at[at], x=dev)

    def xpass(who, at, piece, send, recv, dev):
        part = attg.at[who, at, pl.ds(piece * mid_row, mid_row)]
        return remote(part, part, send.at[at], recv.at[at], x=dev)

    xto_right = lambda at: xring(att.at[at], x, at, x_r, y_l, xright)
    xto_left = lambda at: xring(att.at[at], x, at, x_l, y_r, xleft)
    xfrom_left = lambda at: xring(att.at[at], xleft, at, x_r, y_l, xleft)
    xfrom_right = lambda at: xring(att.at[at], xright, at, x_l, y_r, xright)
    xpass_right = lambda at: xpass(xleft, at, 0, x_fr, y_fl, xright)
    xpass_left = lambda at: xpass(xright, at, 1, x_fl, y_fr, xleft)
    xfar_left = lambda at: xpass(xfar, at, 0, x_fr, y_fl, xleft)
    xfar_right = lambda at: xpass(xfar, at, 1, x_fl, y_fr, xright)

    def join(at):
        far_m, far_l = rst[at][0:4], rst[at][4:8]
        own_m, own_l = sts[at][0:4], sts[at][4:8]
        m = jnp.maximum(far_m, own_m)
        a = far_l * jnp.exp(far_m - m)
        b = own_l * jnp.exp(own_m - m)
        total = a + b
        zero = jnp.zeros_like(total)

        def wide(share):
            return lax.dot_general(
                jnp.concatenate([share, zero], axis=0), widen, (((0,), (0,)), ((), ())),
                preferred_element_type=F32, precision=lax.Precision.HIGHEST)

        value = wide(a / total) * ro[at].astype(F32) + wide(b / total) * os[at]
        att[at] = value.astype(BF16)
        keep(at).start()
        xto_right(at).start()
        xto_left(at).start()

    def home(i):
        return (z + Z - nth_near(i, Z)) % Z

    def arrive(i):
        at = home(i)

        @pl.when(i == 0)
        def _():
            own_o.wait()
            own_t.wait()

        @pl.when(i > 0)
        def _():
            for copy in line_o(at, at):
                copy.wait_recv()

        join(at)

    def forward(i):
        at = home(i)
        xfrom_left(at).wait_recv()
        xpass_right(at).start()
        xfrom_right(at).wait_recv()
        xpass_left(at).start()

    hz = Z // 2

    def main(t):
        group, n = t // Y, t % Y
        piece = jnp.where(n == 0, y, jnp.where(n == 1, left, jnp.where(n == 2, right, far)))

        @pl.when(n == 0)
        def _():
            rows = pl.ds(pl.multiple_of(group * side, side), side)
            for h in range(heads):
                acc[h, rows, :] = jnp.zeros((side, 128), F32)
                mx[h, rows, :] = jnp.full((side, 128), -3e38, F32)
            each(hz, 0, lambda i: wait_q(group * hz + i))

        @pl.when(t == Y - 1)
        def _():
            each(Z, 0, step3)

        @pl.when(t < Y)
        def _():
            twins(piece)
            build(n, piece)

        attend(n, group)

        @pl.when(t == 0)
        def _():
            each(Z, Z - 3, step2)

        @pl.when(t == Y - 1)
        def _():
            each(hz, 0, settle_send)

        @pl.when(t == Y)
        def _():
            arrive(0)

        @pl.when(t == Y + 1)
        def _():
            each(hz, 1, arrive)

        @pl.when(t == Y + 2)
        def _():
            forward(0)

    each(2 * Y, 0, main)
    each(Z, hz, settle_send)
    each(hz, 1, forward)

    def late(i):
        arrive(i)

        @pl.when(i > Z // 2)
        def _():
            forward(i - 1)

    each(Z, Z // 2, late)
    forward(Z - 1)

    def finish(at):
        xfar_left(at).wait_recv()
        xfar_right(at).wait_recv()
        keep(at).wait()
        for copy in (xto_right(at), xto_left(at), xpass_right(at), xpass_left(at), to_right(at), to_left(at)):
            copy.wait_send()

        @pl.when(at % 2 == 0)
        def _():
            pass_right(at).wait_send()

        @pl.when(at % 2 == 1)
        def _():
            pass_left(at).wait_send()

        for piece in range(Y):
            to_twin(piece, at).wait_send()

    each(Z, 0, finish)
    w_keep.wait()
    w_pass(xfar, 0, 4, 6, xleft).wait_recv()
    w_pass(xfar, 1, 5, 7, xright).wait_recv()
    for copy in (w_whole(x, 0, 2, xright), w_whole(x, 1, 3, xleft),
                 w_pass(xleft, 0, 4, 6, xright), w_pass(xright, 1, 5, 7, xleft)):
        copy.wait_send()

    def end_line(i):
        at = (z + i) % Z
        for copy in line_b(at, at) + line_o(at, at) + (line_q(at, at), line_g(at, at)):
            copy.wait_send()

    each(Z, 1, end_line)

    def end_cluster(i):
        to = (w + i) % W
        remote(abuf.at[to], abuf.at[to], s_a.at[to], r_a.at[to], y=to // C, c=to % C).wait_send()
        remote(cvar, va.at[to], s_va.at[to], r_va.at[to], y=to // C, c=to % C).wait_send()

    each(W, 1, end_cluster)


def out_kernel(dq, ids, att_ref, next_ref, w_ref, x_ref, seg_ref, gain_ref, read_ref, upd_ref, pool_ref, y_ref):
    step = pl.program_id(0)
    parts, slot, cols = att_ref.shape[0], att_ref.shape[2], att_ref.shape[3]
    y = None
    for p in range(parts):
        rows = jnp.concatenate([att_ref[p, 0], next_ref[p, 0]], axis=0)
        part = jnp.dot(rows, w_ref[p], preferred_element_type=F32)
        y = part if y is None else y + part
    y_ref[...] = y
    upd_ref[...] = y_ref[:, pl.ds(pl.multiple_of(ids[1] * cols, cols), cols)]
    hidden = x_ref[...].astype(F32) + y
    square = jnp.sum(hidden * hidden, axis=1, keepdims=True)
    weighted = jnp.sum(hidden * (gain_ref[...] * read_ref[...]), axis=1, keepdims=True)
    score = weighted * lax.rsqrt(square / y.shape[1] + 1e-06)
    row = lax.broadcasted_iota(jnp.int32, (8, slot), 0)
    for n in range(2):
        first = (ids[0] * pl.num_programs(0) * 2 + step * 2 + n) * 2
        member = jnp.where((row < 2) & (seg_ref[n] - first == row), 1.0, 0.0)
        own = jnp.broadcast_to(score[n * slot:n * slot + slot], (slot, 128))
        sums = jnp.dot(member, own, preferred_element_type=F32, precision=lax.Precision.HIGHEST)
        count = jnp.maximum(jnp.sum(member, axis=1, keepdims=True), 1.0)
        mean = sums / count
        for k in range(2):
            pool_ref[step * 4 + n * 2 + k] = mean[k, 0]


def body(sizes, doc_x, doc_seg, doc_query, doc_var, query_len, block_perm, cache_k, cache_v, cache_var,
         w_query, w_key, w_value, w_out, var_bias, norm_gain, readout):
    X, Y, Z, C = sizes
    W = Y * C
    tokens, cols = doc_x.shape[0], w_query.shape[1]
    features = doc_x.shape[1]
    heads = cols // DH
    slot = tokens // Z
    crows = cache_k.shape[0]
    blocks = Y * Z * C
    bpq = blocks // Z
    piece = crows // (Y * Z)
    part_keys = bpq * slot
    i32 = jnp.int32
    dma = pltpu.SemaphoreType.DMA

    at = jnp.arange(blocks, dtype=i32)
    place = (at // C % Z) * W + (at // (Z * C)) * C + at % C
    inv = jnp.sum(jnp.where(block_perm[None, :] == at[:, None], place[None, :], 0), axis=1)

    half_size = DH // 2
    frequency = 10000.0 ** (-np.arange(half_size) / half_size)
    frequency = np.tile(frequency.astype(np.float32), 128 // half_size)
    turns = np.arange(slot)[:, None] * frequency.astype(np.float64)[None, :]
    seg = doc_seg.reshape(Z, 1, slot)

    vm = lambda *shape: pltpu.VMEM(shape, BF16)
    vf = lambda *shape: pltpu.VMEM(shape, F32)
    vi = lambda *shape: pltpu.VMEM(shape, i32)
    smem = pl.BlockSpec(memory_space=pltpu.SMEM)
    vmem = pl.BlockSpec(memory_space=pltpu.VMEM)
    hbm = pl.BlockSpec(memory_space=ANY)
    attended, w_all = pl.pallas_call(
        functools.partial(attention_kernel, sizes),
        in_specs=[smem] * 4 + [vmem] * 5 + [hbm] * 8,
        out_specs=[hbm] * 2,
        out_shape=[
            jax.ShapeDtypeStruct((X, Z, slot, cols), BF16),
            jax.ShapeDtypeStruct((X, cols, features), BF16),
        ],
        scratch_shapes=[
            vm(Z, slot, features), vm(features, cols), vm(features, cols), vm(features, cols),
            pltpu.SMEM((Z,), i32),
            vm(W, Z, piece, cols), vm(Z * W, piece, cols), vm(Z * bpq, piece, cols),
            vi(W, Y, 1, slot), vi(Z * W, Y, 1, slot),
            vm(C, Y, bpq, Z, piece, cols),
            vm(Z, slot, cols), vm(Z, slot, cols), vi(Z, 1, slot), vi(Z, 1, slot),
            vf(Z, slot, 128), vf(Z, slot, 128), vm(16, cols), vm(16, 128),
            vf(Z, slot, cols), vf(Z, 8, slot), vm(Y, part_keys, 128), vm(Z, slot, cols),
            vm(heads, Y, part_keys, 128), vm(heads, Y, part_keys, 128), vm(heads, tokens, 128),
            vf(heads, tokens, 128), vf(heads, tokens, 128),
            vm(Z, slot, cols), vf(Z, 8, slot), vm(Z, slot, cols), vf(Z, 8, slot), vm(Z, slot, cols),
            dma((4,)),
        ] + [dma((W,))] * 4 + [dma((Z,))] * 10 + [dma((Z,))] * 8 + [dma((Y, Z))] * 2
        + [dma((Z,))] * 4 + [dma((Z,))] * 9 + [dma((4,)), dma((9,))],
        compiler_params=pltpu.CompilerParams(
            collective_id=0, has_side_effects=True, vmem_limit_bytes=56 << 20),
        name="attention",
    )(inv, doc_query, query_len, var_bias, seg, doc_var.reshape(Z, 1, slot),
      jnp.asarray(np.cos(turns), F32), jnp.asarray(np.sin(turns), F32), jnp.asarray(frequency)[None, :],
      doc_x.reshape(Z, slot, features), w_query, w_key, w_value,
      cache_k.reshape(Y, Z, piece, cols), cache_v.reshape(Y, Z, piece, cols), cache_var.reshape(Y, 1, slot), w_out)

    full = lambda *shape: pl.BlockSpec(shape, lambda i, *_: (0,) * len(shape))
    ids = jnp.stack([lax.axis_index(BLK), lax.axis_index("x")]).astype(i32)
    update, pooled = pl.pallas_call(
        out_kernel,
        grid_spec=pltpu.PrefetchScalarGridSpec(
            num_scalar_prefetch=2,
            grid=(Z // 2,),
            in_specs=[
                pl.BlockSpec((X, 1, slot, cols), lambda i, d, n: (0, d[n[0] * 2 * Z + 4 * i], 0, 0)),
                pl.BlockSpec((X, 1, slot, cols), lambda i, d, n: (0, d[n[0] * 2 * Z + 4 * i + 2], 0, 0)),
                full(X, cols, features),
                pl.BlockSpec((2 * slot, features), lambda i, d, n: (i, 0)),
                pl.BlockSpec((2, 1, slot), lambda i, d, n: (i, 0, 0)),
                full(1, features),
                full(1, features),
            ],
            out_specs=[
                pl.BlockSpec((2 * slot, cols), lambda i, d, n: (i, 0)),
                smem,
            ],
            scratch_shapes=[pltpu.VMEM((2 * slot, features), F32)],
        ),
        out_shape=[
            jax.ShapeDtypeStruct((tokens, cols), F32),
            jax.ShapeDtypeStruct((2 * Z,), F32),
        ],
        compiler_params=pltpu.CompilerParams(vmem_limit_bytes=60 << 20),
        name="out_part",
    )(doc_query, ids, attended, attended, w_all, doc_x, seg, norm_gain.reshape(1, features),
      readout.reshape(1, features))
    return update, pooled


def solution(mesh):
    heads = mesh.shape["head"]
    cores = 2
    across = 4
    along = mesh.shape["blk"] // (across * cores)
    sizes = (heads, across, along, cores)
    split = Mesh(mesh.devices.reshape(sizes), ("x", "y", "z", "c"))
    return jax.shard_map(
        functools.partial(body, sizes),
        mesh=split,
        in_specs=(
            P(BLK, None), P(BLK), P(), P(BLK), P(), P(),
            P(BLK, "x"), P(BLK, "x"), P(BLK),
            P(None, "x"), P(None, "x"), P(None, "x"), P("x", None), P(None, "x"),
            P(), P(),
        ),
        out_specs=(P(BLK, "x"), P(BLK)),
        check_vma=False,
    )
```

```python
import functools

import jax
import jax.numpy as jnp
import numpy as np
from jax import lax
from jax.experimental import pallas as pl
from jax.experimental.pallas import tpu as pltpu
from jax.sharding import Mesh, PartitionSpec as P

DH = 64
F32 = jnp.float32
BF16 = jnp.bfloat16
NEG = -1e30
ANY = pl.ANY
BLK = ("y", "z", "c")


def remote(src, dst, send_sem, recv_sem, **device):
    return pltpu.make_async_remote_copy(
        src_ref=src,
        dst_ref=dst,
        send_sem=send_sem,
        recv_sem=recv_sem,
        device_id=device,
        device_id_type=pl.DeviceIdType.MESH,
    )


def each(count, first, step):
    def run(i, carry):
        step(i)
        return carry

    lax.fori_loop(first, count, run, 0)


def nth_near(i, Z):
    return lax.rem(jnp.where(i % 2 == 1, (i + 1) // 2, Z - i // 2), Z)


def attention_kernel(
    sizes, perm, dq, qlen, bias, seg_ref, var_ref, tcos_ref, tsin_ref, freq_ref, x_in, wq_in, wk_in, wv_in,
    ck, cv, cvar, w_in, attg, w_all, ids,
    inv, xv, wq, wk, wv, order, abuf, bbuf, gbuf, va, vb, kv, qrot, qh, dv, hv, cosv, sinv, qtab, ktab,
    os, sts, kfs, qfs, ka, vx, qa, acc, mx, oh, sth, ro, rst, att,
    s_x, s_a, r_a, s_va, r_va, s_b, r_b, s_vb, r_vb, s_g, r_g, s_q, r_q, s_dv, r_dv,
    s_r, s_l, r_l, r_r, s_fr, s_fl, r_fl, r_fr, s_s, r_s,
    s_o, r_o, s_t, r_t, x_r, x_l, y_l, y_r, x_fr, x_fl, y_fl, y_fr, mine_sem, here, w_sem,
):
    X, Y, Z, C = sizes
    x, y, z, c = lax.axis_index("x"), lax.axis_index("y"), lax.axis_index("z"), lax.axis_index("c")
    W = Y * C
    w = y * C + c
    bpq = W
    blk = (y * Z + z) * C + c
    slot, cols = qrot.shape[1], qrot.shape[2]
    heads = cols // DH
    pairs = cols // 128
    part_keys = bpq * slot
    barrier = pltpu.get_barrier_semaphore()

    loads = [pltpu.make_async_copy(s, d, s_x.at[n]) for n, (s, d) in
             enumerate(((x_in, xv), (wq_in, wq), (wk_in, wk), (wv_in, wv)))]
    for load in loads:
        load.start()

    def greet(**device):
        pl.semaphore_signal(barrier, inc=1, device_id=device, device_id_type=pl.DeviceIdType.MESH)

    each(W, 1, lambda i: greet(y=(w + i) % W // C, c=(w + i) % W % C))
    each(Z, 1, lambda i: greet(z=(z + i) % Z))
    for side in ((x + 1) % X, (x + X - 1) % X):
        greet(x=side)

    slot_query = [dq[blk * 2 * Z + 2 * j] for j in range(Z)]
    for query in range(Z):
        at = jnp.int32(0)
        for j in range(Z):
            at = jnp.where(slot_query[j] == query, j, at)
        order[query] = at
    lane2 = lax.broadcasted_iota(jnp.int32, (16, cols), 1)
    row2 = lax.broadcasted_iota(jnp.int32, (16, cols), 0)
    feat2 = lane2 % DH
    lane_head = 2 * (lane2 // 128) + (1 - lane2 % 128 // DH)
    delta = jnp.zeros((16, cols), F32)
    for h in range(heads):
        delta = jnp.where(lane_head == h, bias[0, h] - bias[1, h], delta)
    hi = delta.astype(BF16).astype(F32)
    mid = (delta - hi).astype(BF16).astype(F32)
    low = delta - hi - mid
    value = jnp.where(feat2 < 8, hi, jnp.where(feat2 < 16, mid, low))
    value = jnp.where((feat2 < 24) & (feat2 % 8 == row2), value, 0.0)
    qtab[...] = jnp.where((row2 >= 8) & (row2 < 11) & (feat2 == row2 + 16), 1.0, value).astype(BF16)
    lane1, row1 = lane2[:, :128], row2[:, :128]
    feat1 = lane1 % DH
    value = jnp.where((feat1 < 24) & (feat1 % 8 == row1), 1.0, 0.0)
    hit = (((row1 == 8) & (feat1 == 24)) | ((row1 == 9) & (feat1 == 26)) | ((row1 == 10) & (feat1 == 25)))
    ktab[...] = jnp.where(hit, NEG, value).astype(BF16)

    def features(rows, table):
        return lax.dot_general(rows.astype(BF16), table, (((0,), (0,)), ((), ())),
                               preferred_element_type=F32).astype(BF16)

    def marks(var, eight, seg):
        same = jnp.where((row1 < 8) & (var == row1), 1.0, 0.0)
        rows = jnp.where(row1 == 8, eight, same)
        if seg is not None:
            rows = jnp.where(((row1 == 9) & (seg == 0)) | ((row1 == 10) & (seg == 1)), 1.0, rows)
        return rows

    pl.semaphore_wait(barrier, W - 1 + Z - 1 + 2)

    for step in range(1, Y):
        to = (y + step) % Y
        for kind in range(C):
            remote((ck, cv)[kind].at[to], abuf.at[w], s_a.at[to * C + kind], r_a.at[w], y=to, c=kind).start()
            remote(cvar, va.at[w], s_va.at[to * C + kind], r_va.at[w], y=to, c=kind).start()
    for kind in range(C):
        src = (ck, cv)[kind].at[y]

        @pl.when(kind != c)
        def _():
            remote(src, abuf.at[w], s_a.at[y * C + kind], r_a.at[w], c=kind).start()
            remote(cvar, va.at[w], s_va.at[y * C + kind], r_va.at[w], c=kind).start()

        @pl.when(kind == c)
        def _():
            pltpu.make_async_copy(src, abuf.at[w], here.at[0]).start()

    own_var = pltpu.make_async_copy(cvar, va.at[w], here.at[1])
    own_var.start()

    xright, xleft, xfar = (x + 1) % X, (x + X - 1) % X, (x + 2) % X
    w_half = w_in.shape[0] // 2
    w_keep = pltpu.make_async_copy(w_in, w_all.at[x], w_sem.at[8])

    def w_whole(who, send, recv, dev):
        return remote(w_in, w_all.at[who], w_sem.at[send], w_sem.at[recv], x=dev)

    def w_pass(who, piece, send, recv, dev):
        part = w_all.at[who, pl.ds(piece * w_half, w_half)]
        return remote(part, part, w_sem.at[send], w_sem.at[recv], x=dev)

    w_keep.start()
    w_whole(x, 0, 2, xright).start()
    w_whole(x, 1, 3, xleft).start()

    lane = lax.broadcasted_iota(jnp.int32, (slot, cols), 1)
    half = lax.broadcasted_iota(jnp.int32, (slot, 128), 1)
    first_lanes = (lane % DH) < DH // 2
    first_half = (half % DH) < DH // 2
    ones_row = jnp.where(row1 == 10, 1.0, 0.0).astype(BF16)

    def segment(at):
        return seg_ref[at] - (blk * 2 * Z + 2 * at)

    def turn(a, query):
        other = jnp.where(first_lanes, pltpu.roll(a, cols - DH // 2, 1), pltpu.roll(a, DH // 2, 1))
        cosine = jnp.concatenate([cosv[query]] * pairs, axis=1)
        sine = jnp.concatenate([sinv[query]] * pairs, axis=1)
        return a * cosine + other * sine

    loads[0].wait()
    loads[1].wait()

    def project_q(query):
        at = order[query]
        seg = segment(at)
        length = qlen[query].astype(F32)
        count = jnp.sum(jnp.where(seg == 0, 1.0, 0.0), axis=1, keepdims=True)
        base0 = freq_ref[...] * length
        base1 = freq_ref[...] * (length - count)
        second = features(marks(var_ref[at], 1.0, seg), ones_row).astype(F32) > 0.5
        cos_a = jnp.where(second, jnp.cos(base1), jnp.cos(base0))
        sin_a = jnp.where(second, jnp.sin(base1), jnp.sin(base0))
        cosv[query] = cos_a * tcos_ref[...] - sin_a * tsin_ref[...]
        sine = sin_a * tcos_ref[...] + cos_a * tsin_ref[...]
        sinv[query] = jnp.where(first_half, -sine, sine)
        a = jnp.dot(xv[at], wq[...], preferred_element_type=F32)
        qrot[query] = (turn(a, query) * 0.125).astype(BF16)
        dv[query] = var_ref[at]

    each(Z, 0, project_q)

    def line_q(to, at):
        return remote(qrot.at[to], qh.at[at], s_q.at[to], r_q.at[at], z=to)

    def send_q(i):
        line_q((z + nth_near(i, Z)) % Z, z).start()

    each(Z // 2, 1, send_q)
    own_q = pltpu.make_async_copy(qrot.at[z], qh.at[z], here.at[4])
    own_q.start()

    pltpu.make_async_copy(ck.at[y], abuf.at[w], here.at[0]).wait()
    own_var.wait()

    def wait_a(i):
        src = (w + i) % W
        remote(abuf.at[src], abuf.at[src], s_a.at[src], r_a.at[src], y=src // C, c=src % C).wait_recv()
        remote(va.at[src], va.at[src], s_va.at[src], r_va.at[src], y=src // C, c=src % C).wait_recv()

    each(W, 1, wait_a)

    def line_b(to, at):
        return (remote(abuf.at[:, to], bbuf.at[pl.ds(at * W, W)], s_b.at[to], r_b.at[at], z=to),
                remote(va, vb.at[pl.ds(at * W, W)], s_vb.at[to], r_vb.at[at], z=to),
                remote(dv.at[to], hv.at[at], s_dv.at[to], r_dv.at[at], z=to))

    def send_b(i):
        for copy in line_b((z + nth_near(i, Z)) % Z, z):
            copy.start()

    each(Z, 1, send_b)
    own_b = pltpu.make_async_copy(abuf.at[:, z], bbuf.at[pl.ds(z * W, W)], here.at[2])
    own_vb = pltpu.make_async_copy(va, vb.at[pl.ds(z * W, W)], here.at[3])
    own_dv = pltpu.make_async_copy(dv.at[z], hv.at[z], here.at[1])
    own_b.start()
    own_vb.start()
    own_dv.start()

    loads[2].wait()
    loads[3].wait()
    wide8 = lax.broadcasted_iota(jnp.int32, (8, cols), 1)
    deep8 = lax.broadcasted_iota(jnp.int32, (8, cols), 0)
    widen = jnp.where(wide8 // DH == deep8, 1.0, 0.0).astype(F32)

    def own_part(query):
        at = order[query]
        xs = xv[at]
        k = turn(jnp.dot(xs, wk[...], preferred_element_type=F32), query).astype(BF16)
        v = jnp.dot(xs, wv[...], preferred_element_type=F32).astype(BF16)
        seg = segment(at)
        qf = features(marks(var_ref[at], 1.0, seg), qtab[...])
        kf = features(marks(var_ref[at], 0.0, seg), ktab[...])
        q = qrot[query]
        stats = jnp.zeros((slot, 128), F32)
        for pair in range(pairs):
            tile = slice(pair * 128, pair * 128 + 128)
            outs = []
            for odd in range(2):
                mine = (half >= DH) if odd else (half < DH)
                qs = jnp.where(mine, q[:, tile], qf[:, tile])
                ks = jnp.where(mine, k[:, tile], kf)
                s = lax.dot_general(qs, ks, (((1,), (1,)), ((), ())), preferred_element_type=F32)
                m = jnp.max(s, axis=1, keepdims=True)
                p = jnp.exp(s - m)
                l = jnp.sum(p, axis=1, keepdims=True)
                outs.append(jnp.dot(p.astype(BF16), v[:, tile], preferred_element_type=F32) / l)
                head = 2 * pair + odd
                stats = jnp.where(half == head, m, jnp.where(half == 4 + head, l, stats))
            os[query, :, tile] = jnp.where(half < DH, outs[0], outs[1])
        sts[query] = jnp.transpose(stats)[:8]

    early = Z // 2 - 1
    each(early, 0, own_part)

    def find(k):
        at = jnp.int32(0)
        for e in range(Z * W):
            at = jnp.where(perm[e] == k, e // C % Z * W + e // (Z * C) * C + e % C, at)
        inv[k] = at

    each(Z * W, 0, find)
    ids[0] = blk
    ids[1] = x
    w_whole(xleft, 0, 2, xleft).wait_recv()
    w_pass(xleft, 0, 4, 6, xright).start()
    w_whole(xright, 1, 3, xright).wait_recv()
    w_pass(xright, 1, 5, 7, xleft).start()

    own_b.wait()
    own_vb.wait()
    own_dv.wait()

    def wait_b(i):
        src = (z + i) % Z
        part = bbuf.at[pl.ds(src * W, W)]
        remote(part, part, s_b.at[src], r_b.at[src], z=src).wait_recv()
        part = vb.at[pl.ds(src * W, W)]
        remote(part, part, s_vb.at[src], r_vb.at[src], z=src).wait_recv()
        remote(hv.at[src], hv.at[src], s_dv.at[src], r_dv.at[src], z=src).wait_recv()

    each(Z, 1, wait_b)

    def pick(i):
        gbuf[i] = bbuf[inv[i]]

    each(Z * bpq, 0, pick)

    def line_g(to, at):
        return remote(gbuf.at[pl.ds(to * bpq, bpq)], kv.at[c, y, :, at], s_g.at[to], r_g.at[at], z=to)

    own_g = pltpu.make_async_copy(gbuf.at[pl.ds(z * bpq, bpq)], kv.at[c, y, :, z], here.at[2])
    own_g.start()
    each(Z, 1, lambda i: line_g((z + nth_near(i, Z)) % Z, z).start())

    each(Z, Z // 2, send_q)
    own_g.wait()

    right, left, far, twin = (y + 1) % Y, (y + Y - 1) % Y, (y + 2) % Y, 1 - c

    def ring(kind, piece, at, send, recv, **device):
        part = kv.at[kind, piece, :, at]
        return remote(part, part, send.at[at], recv.at[at], **device)

    def to_twin(piece, at):
        return ring(c, piece, at, s_s.at[piece], r_s.at[piece], c=twin)

    def from_twin(piece, at):
        return ring(twin, piece, at, s_s.at[piece], r_s.at[piece], c=twin)

    to_right = lambda at: ring(c, y, at, s_r, r_l, y=right)
    to_left = lambda at: ring(c, y, at, s_l, r_r, y=left)
    from_left = lambda at: ring(c, left, at, s_r, r_l, y=left)
    from_right = lambda at: ring(c, right, at, s_l, r_r, y=right)
    pass_right = lambda at: ring(c, left, at, s_fr, r_fl, y=right)
    pass_left = lambda at: ring(c, right, at, s_fl, r_fr, y=left)
    far_left = lambda at: ring(c, far, at, s_fr, r_fl, y=left)
    far_right = lambda at: ring(c, far, at, s_fl, r_fr, y=right)

    def share(at):
        to_right(at).start()
        to_left(at).start()
        to_twin(y, at).start()

    def step1(i):
        at = (z + nth_near(i, Z)) % Z
        part = kv.at[c, y, :, at]
        remote(part, part, s_g.at[at], r_g.at[at], z=at).wait_recv()
        share(at)

    def step2(i):
        at = (z + nth_near(i, Z)) % Z
        from_left(at).wait_recv()

        @pl.when(at % 2 == 0)
        def _():
            pass_right(at).start()

        to_twin(left, at).start()
        from_right(at).wait_recv()

        @pl.when(at % 2 == 1)
        def _():
            pass_left(at).start()

        to_twin(right, at).start()

    def step3(i):
        at = (z + nth_near(i, Z)) % Z

        @pl.when(at % 2 == 0)
        def _():
            far_left(at).wait_recv()

        @pl.when(at % 2 == 1)
        def _():
            far_right(at).wait_recv()

        to_twin(far, at).start()

    share(z)
    my_len = qlen[z]

    def key_marks(i):
        piece, j = i // bpq, i % bpq
        var = vb[inv[z * bpq + j], piece]
        place = lane1 + (j * Y * slot + piece * slot)
        rows = pl.ds(pl.multiple_of(j * slot, slot), slot)
        kfs[piece, rows, :] = features(marks(var, jnp.where(place >= my_len, 1.0, 0.0), None), ktab[...])

    def query_marks(at):
        qfs[at] = features(marks(hv[at], 1.0, None), qtab[...])

    def steps12(i):
        step1(i)

        @pl.when(i < 3)
        def _():
            each(2 * bpq * i, 2 * bpq * (i - 1), key_marks)
            each(Z // 2 * i, Z // 2 * (i - 1), query_marks)

        @pl.when(i > 2)
        def _():
            own_part(early + i - 3)

        @pl.when(i > 2)
        def _():
            step2(i - 3)

    each(Z, 1, steps12)

    def build(n, piece):
        def one(j):
            k = kv[0, piece, j].reshape(slot, cols)
            v = kv[1, piece, j].reshape(slot, cols)
            rows = pl.ds(pl.multiple_of(j * slot, slot), slot)
            kf = kfs[piece, rows, :]
            for pair in range(pairs):
                tile = slice(pair * 128, pair * 128 + 128)
                for odd in range(2):
                    mine = (half >= DH) if odd else (half < DH)
                    ka[2 * pair + odd, n, rows, :] = jnp.where(mine, k[:, tile], kf)
                    vx[2 * pair + odd, n, rows, :] = jnp.where(mine, v[:, tile], jnp.ones_like(kf))

        each(bpq, 0, one)

    def take_q(i):
        at = (z + nth_near(i, Z)) % Z
        qf = qfs[at]
        q = qh[at]
        rows = pl.ds(pl.multiple_of(i * slot, slot), slot)
        for pair in range(pairs):
            tile = slice(pair * 128, pair * 128 + 128)
            for odd in range(2):
                mine = (half >= DH) if odd else (half < DH)
                qa[2 * pair + odd, rows, :] = jnp.where(mine, q[:, tile], qf[:, tile])

    def wait_q(i):
        at = (z + nth_near(i, Z)) % Z

        @pl.when(i == 0)
        def _():
            own_q.wait()

        @pl.when(i > 0)
        def _():
            line_q(at, at).wait_recv()

        take_q(i)

    side = Z // 2 * slot

    def attend(n, group):
        rows = pl.ds(pl.multiple_of(group * side, side), side)

        def score(h):
            return lax.dot_general(qa[h, rows, :], ka[h, n], (((1,), (1,)), ((), ())), preferred_element_type=F32)

        def weigh(h, s):
            old = mx[h, rows, :][:, :1]
            m = jnp.maximum(old, jnp.max(s, axis=1, keepdims=True))
            o = jnp.dot(jnp.exp(s - m).astype(BF16), vx[h, n], preferred_element_type=F32)
            acc[h, rows, :] = acc[h, rows, :] * jnp.exp(old - m) + o
            mx[h, rows, :] = jnp.broadcast_to(m, (side, 128))

        s = score(0)
        for h in range(heads):
            later = score(h + 1) if h + 1 < heads else None
            weigh(h, s)
            s = later

    def twins(piece):
        each(Z, 0, lambda at: from_twin(piece, at).wait_recv())

    def line_o(to, at):
        return (remote(oh.at[to], ro.at[at], s_o.at[to], r_o.at[at], z=to),
                remote(sth.at[to], rst.at[at], s_t.at[to], r_t.at[at], z=to))

    def settle(i):
        at = (z + nth_near(i, Z)) % Z
        rows = pl.ds(pl.multiple_of(i * slot, slot), slot)
        stats = jnp.zeros((slot, 128), F32)
        for pair in range(pairs):
            outs = []
            for odd in range(2):
                mine = (half >= DH) if odd else (half < DH)
                head = 2 * pair + odd
                total = acc[head, rows, :]
                turned = pltpu.roll(total, DH, 1)
                l = jnp.where(mine, turned, total)
                outs.append(total / l)
                stats = jnp.where(half == head, mx[head, rows, :], jnp.where(half == 4 + head, l, stats))
            oh[at, :, pair * 128:pair * 128 + 128] = jnp.where(half < DH, outs[0], outs[1]).astype(BF16)
        sth[at] = jnp.transpose(stats)[:8]

    own_o = pltpu.make_async_copy(oh.at[z], ro.at[z], here.at[2])
    own_t = pltpu.make_async_copy(sth.at[z], rst.at[z], here.at[3])

    def settle_send(i):
        settle(i)
        at = (z + nth_near(i, Z)) % Z

        @pl.when(i == 0)
        def _():
            own_o.start()
            own_t.start()

        @pl.when(i > 0)
        def _():
            for copy in line_o(at, z):
                copy.start()

    mid_row = slot // 2
    keep = lambda at: pltpu.make_async_copy(att.at[at], attg.at[x, at], mine_sem.at[at])

    def xring(src, who, at, send, recv, dev):
        return remote(src, attg.at[who, at], send.at[at], recv.at[at], x=dev)

    def xpass(who, at, piece, send, recv, dev):
        part = attg.at[who, at, pl.ds(piece * mid_row, mid_row)]
        return remote(part, part, send.at[at], recv.at[at], x=dev)

    xto_right = lambda at: xring(att.at[at], x, at, x_r, y_l, xright)
    xto_left = lambda at: xring(att.at[at], x, at, x_l, y_r, xleft)
    xfrom_left = lambda at: xring(att.at[at], xleft, at, x_r, y_l, xleft)
    xfrom_right = lambda at: xring(att.at[at], xright, at, x_l, y_r, xright)
    xpass_right = lambda at: xpass(xleft, at, 0, x_fr, y_fl, xright)
    xpass_left = lambda at: xpass(xright, at, 1, x_fl, y_fr, xleft)
    xfar_left = lambda at: xpass(xfar, at, 0, x_fr, y_fl, xleft)
    xfar_right = lambda at: xpass(xfar, at, 1, x_fl, y_fr, xright)

    def join(at):
        far_m, far_l = rst[at][0:4], rst[at][4:8]
        own_m, own_l = sts[at][0:4], sts[at][4:8]
        m = jnp.maximum(far_m, own_m)
        a = far_l * jnp.exp(far_m - m)
        b = own_l * jnp.exp(own_m - m)
        share = a / (a + b)
        wide = lax.dot_general(
            jnp.concatenate([share, jnp.zeros_like(share)], axis=0), widen, (((0,), (0,)), ((), ())),
            preferred_element_type=F32, precision=lax.Precision.HIGHEST)
        value = os[at] + wide * (ro[at].astype(F32) - os[at])
        att[at] = value.astype(BF16)
        keep(at).start()
        xto_right(at).start()
        xto_left(at).start()

    def home(i):
        return (z + Z - nth_near(i, Z)) % Z

    def arrive(i):
        at = home(i)

        @pl.when(i == 0)
        def _():
            own_o.wait()
            own_t.wait()

        @pl.when(i > 0)
        def _():
            for copy in line_o(at, at):
                copy.wait_recv()

        join(at)

    def forward(i):
        at = home(i)
        xfrom_left(at).wait_recv()
        xpass_right(at).start()
        xfrom_right(at).wait_recv()
        xpass_left(at).start()

    hz = Z // 2

    def main(t):
        group, n = t // Y, t % Y
        piece = jnp.where(n == 0, y, jnp.where(n == 1, left, jnp.where(n == 2, right, far)))

        @pl.when(n == 0)
        def _():
            rows = pl.ds(pl.multiple_of(group * side, side), side)
            for h in range(heads):
                acc[h, rows, :] = jnp.zeros((side, 128), F32)
                mx[h, rows, :] = jnp.full((side, 128), -3e38, F32)
            each(hz, 0, lambda i: wait_q(group * hz + i))

        @pl.when(t == Y - 1)
        def _():
            each(Z, 0, step3)

        @pl.when(t < Y)
        def _():
            twins(piece)
            build(n, piece)

        attend(n, group)

        @pl.when(t == 0)
        def _():
            each(Z, Z - 3, step2)

        @pl.when(t == Y - 1)
        def _():
            each(hz, 0, settle_send)

        @pl.when(t == Y)
        def _():
            arrive(0)

        @pl.when(t == Y + 1)
        def _():
            each(hz, 1, arrive)

        @pl.when(t == Y + 2)
        def _():
            forward(0)

    each(2 * Y, 0, main)
    each(Z, hz, settle_send)
    each(hz, 1, forward)

    def late(i):
        arrive(i)

        @pl.when(i > Z // 2)
        def _():
            forward(i - 1)

    each(Z, Z // 2, late)
    forward(Z - 1)

    def finish(at):
        xfar_left(at).wait_recv()
        xfar_right(at).wait_recv()
        keep(at).wait()
        for copy in (xto_right(at), xto_left(at), xpass_right(at), xpass_left(at), to_right(at), to_left(at)):
            copy.wait_send()

        @pl.when(at % 2 == 0)
        def _():
            pass_right(at).wait_send()

        @pl.when(at % 2 == 1)
        def _():
            pass_left(at).wait_send()

        for piece in range(Y):
            to_twin(piece, at).wait_send()

    each(Z, 0, finish)
    w_keep.wait()
    w_pass(xfar, 0, 4, 6, xleft).wait_recv()
    w_pass(xfar, 1, 5, 7, xright).wait_recv()
    for copy in (w_whole(x, 0, 2, xright), w_whole(x, 1, 3, xleft),
                 w_pass(xleft, 0, 4, 6, xright), w_pass(xright, 1, 5, 7, xleft)):
        copy.wait_send()

    def end_line(i):
        at = (z + i) % Z
        for copy in line_b(at, at) + line_o(at, at) + (line_q(at, at), line_g(at, at)):
            copy.wait_send()

    each(Z, 1, end_line)

    def end_cluster(i):
        to = (w + i) % W
        remote(abuf.at[to], abuf.at[to], s_a.at[to], r_a.at[to], y=to // C, c=to % C).wait_send()
        remote(cvar, va.at[to], s_va.at[to], r_va.at[to], y=to // C, c=to % C).wait_send()

    each(W, 1, end_cluster)


def out_kernel(dq, ids, att_ref, next_ref, w_ref, x_ref, seg_ref, gain_ref, read_ref, upd_ref, pool_ref, y_ref):
    step = pl.program_id(0)
    parts, slot, cols = att_ref.shape[0], att_ref.shape[2], att_ref.shape[3]
    y = None
    for p in range(parts):
        rows = jnp.concatenate([att_ref[p, 0], next_ref[p, 0]], axis=0)
        part = jnp.dot(rows, w_ref[p], preferred_element_type=F32)
        y = part if y is None else y + part
    y_ref[...] = y
    upd_ref[...] = y_ref[:, pl.ds(pl.multiple_of(ids[1] * cols, cols), cols)]
    hidden = x_ref[...].astype(F32) + y
    square = jnp.sum(hidden * hidden, axis=1, keepdims=True)
    weighted = jnp.sum(hidden * (gain_ref[...] * read_ref[...]), axis=1, keepdims=True)
    score = weighted * lax.rsqrt(square / y.shape[1] + 1e-06)
    row = lax.broadcasted_iota(jnp.int32, (8, slot), 0)
    for n in range(2):
        first = (ids[0] * pl.num_programs(0) * 2 + step * 2 + n) * 2
        member = jnp.where((row < 2) & (seg_ref[n] - first == row), 1.0, 0.0)
        own = jnp.broadcast_to(score[n * slot:n * slot + slot], (slot, 128))
        sums = jnp.dot(member, own, preferred_element_type=F32, precision=lax.Precision.HIGHEST)
        count = jnp.maximum(jnp.sum(member, axis=1, keepdims=True), 1.0)
        mean = sums / count
        for k in range(2):
            pool_ref[step * 4 + n * 2 + k] = mean[k, 0]


def body(sizes, doc_x, doc_seg, doc_query, doc_var, query_len, block_perm, cache_k, cache_v, cache_var,
         w_query, w_key, w_value, w_out, var_bias, norm_gain, readout):
    X, Y, Z, C = sizes
    W = Y * C
    tokens, cols = doc_x.shape[0], w_query.shape[1]
    features = doc_x.shape[1]
    heads = cols // DH
    slot = tokens // Z
    crows = cache_k.shape[0]
    blocks = Y * Z * C
    bpq = blocks // Z
    piece = crows // (Y * Z)
    part_keys = bpq * slot
    i32 = jnp.int32
    dma = pltpu.SemaphoreType.DMA

    half_size = DH // 2
    frequency = 10000.0 ** (-np.arange(half_size) / half_size)
    frequency = np.tile(frequency.astype(np.float32), 128 // half_size)
    turns = np.arange(slot)[:, None] * frequency.astype(np.float64)[None, :]
    seg = doc_seg.reshape(Z, 1, slot)

    vm = lambda *shape: pltpu.VMEM(shape, BF16)
    vf = lambda *shape: pltpu.VMEM(shape, F32)
    vi = lambda *shape: pltpu.VMEM(shape, i32)
    smem = pl.BlockSpec(memory_space=pltpu.SMEM)
    vmem = pl.BlockSpec(memory_space=pltpu.VMEM)
    hbm = pl.BlockSpec(memory_space=ANY)
    attended, w_all, ids = pl.pallas_call(
        functools.partial(attention_kernel, sizes),
        in_specs=[smem] * 4 + [vmem] * 5 + [hbm] * 8,
        out_specs=[hbm] * 2 + [smem],
        out_shape=[
            jax.ShapeDtypeStruct((X, Z, slot, cols), BF16),
            jax.ShapeDtypeStruct((X, cols, features), BF16),
            jax.ShapeDtypeStruct((2,), i32),
        ],
        scratch_shapes=[
            pltpu.SMEM((blocks,), i32), vm(Z, slot, features), vm(features, cols), vm(features, cols), vm(features, cols),
            pltpu.SMEM((Z,), i32),
            vm(W, Z, piece, cols), vm(Z * W, piece, cols), vm(Z * bpq, piece, cols),
            vi(W, Y, 1, slot), vi(Z * W, Y, 1, slot),
            vm(C, Y, bpq, Z, piece, cols),
            vm(Z, slot, cols), vm(Z, slot, cols), vi(Z, 1, slot), vi(Z, 1, slot),
            vf(Z, slot, 128), vf(Z, slot, 128), vm(16, cols), vm(16, 128),
            vf(Z, slot, cols), vf(Z, 8, slot), vm(Y, part_keys, 128), vm(Z, slot, cols),
            vm(heads, Y, part_keys, 128), vm(heads, Y, part_keys, 128), vm(heads, tokens, 128),
            vf(heads, tokens, 128), vf(heads, tokens, 128),
            vm(Z, slot, cols), vf(Z, 8, slot), vm(Z, slot, cols), vf(Z, 8, slot), vm(Z, slot, cols),
            dma((4,)),
        ] + [dma((W,))] * 4 + [dma((Z,))] * 10 + [dma((Z,))] * 8 + [dma((Y, Z))] * 2
        + [dma((Z,))] * 4 + [dma((Z,))] * 9 + [dma((5,)), dma((9,))],
        compiler_params=pltpu.CompilerParams(
            collective_id=0, has_side_effects=True, vmem_limit_bytes=56 << 20),
        name="attention",
    )(block_perm, doc_query, query_len, var_bias, seg, doc_var.reshape(Z, 1, slot),
      jnp.asarray(np.cos(turns), F32), jnp.asarray(np.sin(turns), F32), jnp.asarray(frequency)[None, :],
      doc_x.reshape(Z, slot, features), w_query, w_key, w_value,
      cache_k.reshape(Y, Z, piece, cols), cache_v.reshape(Y, Z, piece, cols), cache_var.reshape(Y, 1, slot), w_out)

    full = lambda *shape: pl.BlockSpec(shape, lambda i, *_: (0,) * len(shape))
    update, pooled = pl.pallas_call(
        out_kernel,
        grid_spec=pltpu.PrefetchScalarGridSpec(
            num_scalar_prefetch=2,
            grid=(Z // 2,),
            in_specs=[
                pl.BlockSpec((X, 1, slot, cols), lambda i, d, n: (0, d[n[0] * 2 * Z + 4 * i], 0, 0)),
                pl.BlockSpec((X, 1, slot, cols), lambda i, d, n: (0, d[n[0] * 2 * Z + 4 * i + 2], 0, 0)),
                full(X, cols, features),
                pl.BlockSpec((2 * slot, features), lambda i, d, n: (i, 0)),
                pl.BlockSpec((2, 1, slot), lambda i, d, n: (i, 0, 0)),
                full(1, features),
                full(1, features),
            ],
            out_specs=[
                pl.BlockSpec((2 * slot, cols), lambda i, d, n: (i, 0)),
                smem,
            ],
            scratch_shapes=[pltpu.VMEM((2 * slot, features), F32)],
        ),
        out_shape=[
            jax.ShapeDtypeStruct((tokens, cols), F32),
            jax.ShapeDtypeStruct((2 * Z,), F32),
        ],
        compiler_params=pltpu.CompilerParams(vmem_limit_bytes=60 << 20),
        name="out_part",
    )(doc_query, ids, attended, attended, w_all, doc_x, seg, norm_gain.reshape(1, features),
      readout.reshape(1, features))
    return update, pooled


def solution(mesh):
    heads = mesh.shape["head"]
    cores = 2
    across = 4
    along = mesh.shape["blk"] // (across * cores)
    sizes = (heads, across, along, cores)
    split = Mesh(mesh.devices.reshape(sizes), ("x", "y", "z", "c"))
    return jax.shard_map(
        functools.partial(body, sizes),
        mesh=split,
        in_specs=(
            P(BLK, None), P(BLK), P(), P(BLK), P(), P(),
            P(BLK, "x"), P(BLK, "x"), P(BLK),
            P(None, "x"), P(None, "x"), P(None, "x"), P("x", None), P(None, "x"),
            P(), P(),
        ),
        out_specs=(P(BLK, "x"), P(BLK)),
        check_vma=False,
    )
```

```python
import functools

import jax
import jax.numpy as jnp
import numpy as np
from jax import lax
from jax.experimental import pallas as pl
from jax.experimental.pallas import tpu as pltpu
from jax.sharding import Mesh, PartitionSpec as P

DH = 64
F32 = jnp.float32
BF16 = jnp.bfloat16
NEG = -1e30
ANY = pl.ANY
BLK = ("y", "z", "c")


def remote(src, dst, send_sem, recv_sem, **device):
    return pltpu.make_async_remote_copy(
        src_ref=src,
        dst_ref=dst,
        send_sem=send_sem,
        recv_sem=recv_sem,
        device_id=device,
        device_id_type=pl.DeviceIdType.MESH,
    )


def each(count, first, step):
    def run(i, carry):
        step(i)
        return carry

    lax.fori_loop(first, count, run, 0)


def nth_near(i, Z):
    return lax.rem(jnp.where(i % 2 == 1, (i + 1) // 2, Z - i // 2), Z)


def attention_kernel(
    sizes, perm, dq, qlen, bias, seg_ref, var_ref, tcos_ref, tsin_ref, freq_ref, x_in, wq_in, wk_in, wv_in,
    ck, cv, cvar, w_in, attg, w_all, ids,
    inv, xv, wq, wk, wv, order, abuf, bbuf, gbuf, va, vb, kv, qrot, qh, dv, hv, cosv, sinv, qtab, ktab,
    os, sts, kfs, qfs, ka, vx, qa, acc, mx, oh, sth, ro, rst, att,
    s_x, s_a, r_a, s_va, r_va, s_b, r_b, s_vb, r_vb, s_g, r_g, s_q, r_q, s_dv, r_dv,
    s_r, s_l, r_l, r_r, s_fr, s_fl, r_fl, r_fr, s_s, r_s,
    s_o, r_o, s_t, r_t, x_r, x_l, y_l, y_r, x_fr, x_fl, y_fl, y_fr, mine_sem, here, w_sem,
):
    X, Y, Z, C = sizes
    x, y, z, c = lax.axis_index("x"), lax.axis_index("y"), lax.axis_index("z"), lax.axis_index("c")
    W = Y * C
    w = y * C + c
    bpq = W
    blk = (y * Z + z) * C + c
    slot, cols = qrot.shape[1], qrot.shape[2]
    heads = cols // DH
    pairs = cols // 128
    part_keys = bpq * slot
    barrier = pltpu.get_barrier_semaphore()

    loads = [pltpu.make_async_copy(s, d, s_x.at[n]) for n, (s, d) in
             enumerate(((x_in, xv), (wq_in, wq), (wk_in, wk), (wv_in, wv)))]
    for load in loads:
        load.start()

    def greet(**device):
        pl.semaphore_signal(barrier, inc=1, device_id=device, device_id_type=pl.DeviceIdType.MESH)

    each(W, 1, lambda i: greet(y=(w + i) % W // C, c=(w + i) % W % C))
    each(Z, 1, lambda i: greet(z=(z + i) % Z))
    for side in ((x + 1) % X, (x + X - 1) % X):
        greet(x=side)

    slot_query = [dq[blk * 2 * Z + 2 * j] for j in range(Z)]
    for query in range(Z):
        at = jnp.int32(0)
        for j in range(Z):
            at = jnp.where(slot_query[j] == query, j, at)
        order[query] = at
    lane2 = lax.broadcasted_iota(jnp.int32, (16, cols), 1)
    row2 = lax.broadcasted_iota(jnp.int32, (16, cols), 0)
    feat2 = lane2 % DH
    lane_head = 2 * (lane2 // 128) + (1 - lane2 % 128 // DH)
    delta = jnp.zeros((16, cols), F32)
    for h in range(heads):
        delta = jnp.where(lane_head == h, bias[0, h] - bias[1, h], delta)
    hi = delta.astype(BF16).astype(F32)
    mid = (delta - hi).astype(BF16).astype(F32)
    low = delta - hi - mid
    value = jnp.where(feat2 < 8, hi, jnp.where(feat2 < 16, mid, low))
    value = jnp.where((feat2 < 24) & (feat2 % 8 == row2), value, 0.0)
    qtab[...] = jnp.where((row2 >= 8) & (row2 < 11) & (feat2 == row2 + 16), 1.0, value).astype(BF16)
    lane1, row1 = lane2[:, :128], row2[:, :128]
    feat1 = lane1 % DH
    value = jnp.where((feat1 < 24) & (feat1 % 8 == row1), 1.0, 0.0)
    hit = (((row1 == 8) & (feat1 == 24)) | ((row1 == 9) & (feat1 == 26)) | ((row1 == 10) & (feat1 == 25)))
    ktab[...] = jnp.where(hit, NEG, value).astype(BF16)

    def features(rows, table):
        return lax.dot_general(rows.astype(BF16), table, (((0,), (0,)), ((), ())),
                               preferred_element_type=F32).astype(BF16)

    def marks(var, eight, seg):
        same = jnp.where((row1 < 8) & (var == row1), 1.0, 0.0)
        rows = jnp.where(row1 == 8, eight, same)
        if seg is not None:
            rows = jnp.where(((row1 == 9) & (seg == 0)) | ((row1 == 10) & (seg == 1)), 1.0, rows)
        return rows

    pl.semaphore_wait(barrier, W - 1 + Z - 1 + 2)

    for step in range(1, Y):
        to = (y + step) % Y
        for kind in range(C):
            remote((ck, cv)[kind].at[to], abuf.at[w], s_a.at[to * C + kind], r_a.at[w], y=to, c=kind).start()
            remote(cvar, va.at[w], s_va.at[to * C + kind], r_va.at[w], y=to, c=kind).start()
    for kind in range(C):
        src = (ck, cv)[kind].at[y]

        @pl.when(kind != c)
        def _():
            remote(src, abuf.at[w], s_a.at[y * C + kind], r_a.at[w], c=kind).start()
            remote(cvar, va.at[w], s_va.at[y * C + kind], r_va.at[w], c=kind).start()

        @pl.when(kind == c)
        def _():
            pltpu.make_async_copy(src, abuf.at[w], here.at[0]).start()

    own_var = pltpu.make_async_copy(cvar, va.at[w], here.at[1])
    own_var.start()

    xright, xleft, xfar = (x + 1) % X, (x + X - 1) % X, (x + 2) % X
    w_half = w_in.shape[0] // 2
    w_keep = pltpu.make_async_copy(w_in, w_all.at[x], w_sem.at[8])

    def w_whole(who, send, recv, dev):
        return remote(w_in, w_all.at[who], w_sem.at[send], w_sem.at[recv], x=dev)

    def w_pass(who, piece, send, recv, dev):
        part = w_all.at[who, pl.ds(piece * w_half, w_half)]
        return remote(part, part, w_sem.at[send], w_sem.at[recv], x=dev)

    w_keep.start()
    w_whole(x, 0, 2, xright).start()
    w_whole(x, 1, 3, xleft).start()

    lane = lax.broadcasted_iota(jnp.int32, (slot, cols), 1)
    half = lax.broadcasted_iota(jnp.int32, (slot, 128), 1)
    first_lanes = (lane % DH) < DH // 2
    first_half = (half % DH) < DH // 2
    ones_row = jnp.where(row1 == 10, 1.0, 0.0).astype(BF16)

    def segment(at):
        return seg_ref[at] - (blk * 2 * Z + 2 * at)

    def turn(a, query):
        other = jnp.where(first_lanes, pltpu.roll(a, cols - DH // 2, 1), pltpu.roll(a, DH // 2, 1))
        cosine = jnp.concatenate([cosv[query]] * pairs, axis=1)
        sine = jnp.concatenate([sinv[query]] * pairs, axis=1)
        return a * cosine + other * sine

    loads[0].wait()
    loads[1].wait()

    def project_q(query):
        at = order[query]
        seg = segment(at)
        length = qlen[query].astype(F32)
        count = jnp.sum(jnp.where(seg == 0, 1.0, 0.0), axis=1, keepdims=True)
        base0 = freq_ref[...] * length
        base1 = freq_ref[...] * (length - count)
        second = features(marks(var_ref[at], 1.0, seg), ones_row).astype(F32) > 0.5
        cos_a = jnp.where(second, jnp.cos(base1), jnp.cos(base0))
        sin_a = jnp.where(second, jnp.sin(base1), jnp.sin(base0))
        cosv[query] = cos_a * tcos_ref[...] - sin_a * tsin_ref[...]
        sine = sin_a * tcos_ref[...] + cos_a * tsin_ref[...]
        sinv[query] = jnp.where(first_half, -sine, sine)
        a = jnp.dot(xv[at], wq[...], preferred_element_type=F32)
        qrot[query] = (turn(a, query) * 0.125).astype(BF16)
        dv[query] = var_ref[at]

    each(Z, 0, project_q)

    def line_q(to, at):
        return remote(qrot.at[to], qh.at[at], s_q.at[to], r_q.at[at], z=to)

    def send_q(i):
        line_q((z + nth_near(i, Z)) % Z, z).start()

    each(Z // 2, 1, send_q)
    own_q = pltpu.make_async_copy(qrot.at[z], qh.at[z], here.at[4])
    own_q.start()

    pltpu.make_async_copy(ck.at[y], abuf.at[w], here.at[0]).wait()
    own_var.wait()

    def wait_a(i):
        src = (w + i) % W
        remote(abuf.at[src], abuf.at[src], s_a.at[src], r_a.at[src], y=src // C, c=src % C).wait_recv()
        remote(va.at[src], va.at[src], s_va.at[src], r_va.at[src], y=src // C, c=src % C).wait_recv()

    each(W, 1, wait_a)

    def line_b(to, at):
        return (remote(abuf.at[:, to], bbuf.at[pl.ds(at * W, W)], s_b.at[to], r_b.at[at], z=to),
                remote(va, vb.at[pl.ds(at * W, W)], s_vb.at[to], r_vb.at[at], z=to),
                remote(dv.at[to], hv.at[at], s_dv.at[to], r_dv.at[at], z=to))

    def send_b(i):
        for copy in line_b((z + nth_near(i, Z)) % Z, z):
            copy.start()

    each(Z, 1, send_b)
    own_b = pltpu.make_async_copy(abuf.at[:, z], bbuf.at[pl.ds(z * W, W)], here.at[2])
    own_vb = pltpu.make_async_copy(va, vb.at[pl.ds(z * W, W)], here.at[3])
    own_dv = pltpu.make_async_copy(dv.at[z], hv.at[z], here.at[1])
    own_b.start()
    own_vb.start()
    own_dv.start()

    loads[2].wait()
    loads[3].wait()
    wide8 = lax.broadcasted_iota(jnp.int32, (8, cols), 1)
    deep8 = lax.broadcasted_iota(jnp.int32, (8, cols), 0)
    widen = jnp.where(wide8 // DH == deep8, 1.0, 0.0).astype(F32)

    def own_part(query):
        at = order[query]
        xs = xv[at]
        k = turn(jnp.dot(xs, wk[...], preferred_element_type=F32), query).astype(BF16)
        v = jnp.dot(xs, wv[...], preferred_element_type=F32).astype(BF16)
        seg = segment(at)
        qf = features(marks(var_ref[at], 1.0, seg), qtab[...])
        kf = features(marks(var_ref[at], 0.0, seg), ktab[...])
        q = qrot[query]
        stats = jnp.zeros((slot, 128), F32)
        for pair in range(pairs):
            tile = slice(pair * 128, pair * 128 + 128)
            outs = []
            for odd in range(2):
                mine = (half >= DH) if odd else (half < DH)
                qs = jnp.where(mine, q[:, tile], qf[:, tile])
                ks = jnp.where(mine, k[:, tile], kf)
                s = lax.dot_general(qs, ks, (((1,), (1,)), ((), ())), preferred_element_type=F32)
                m = jnp.max(s, axis=1, keepdims=True)
                p = jnp.exp(s - m)
                l = jnp.sum(p, axis=1, keepdims=True)
                outs.append(jnp.dot(p.astype(BF16), v[:, tile], preferred_element_type=F32) / l)
                head = 2 * pair + odd
                stats = jnp.where(half == head, m, jnp.where(half == 4 + head, l, stats))
            os[query, :, tile] = jnp.where(half < DH, outs[0], outs[1])
        sts[query] = jnp.transpose(stats)[:8]

    early = Z // 2 - 1
    each(early, 0, own_part)

    def find(k):
        at = jnp.int32(0)
        for e in range(Z * W):
            at = jnp.where(perm[e] == k, e // C % Z * W + e // (Z * C) * C + e % C, at)
        inv[k] = at

    each(Z * W, 0, find)
    ids[0] = blk
    ids[1] = x
    w_whole(xleft, 0, 2, xleft).wait_recv()
    w_pass(xleft, 0, 4, 6, xright).start()
    w_whole(xright, 1, 3, xright).wait_recv()
    w_pass(xright, 1, 5, 7, xleft).start()

    own_b.wait()
    own_vb.wait()
    own_dv.wait()

    def wait_b(i):
        src = (z + i) % Z
        part = bbuf.at[pl.ds(src * W, W)]
        remote(part, part, s_b.at[src], r_b.at[src], z=src).wait_recv()
        part = vb.at[pl.ds(src * W, W)]
        remote(part, part, s_vb.at[src], r_vb.at[src], z=src).wait_recv()
        remote(hv.at[src], hv.at[src], s_dv.at[src], r_dv.at[src], z=src).wait_recv()

    each(Z, 1, wait_b)

    def pick(i):
        gbuf[i] = bbuf[inv[i]]

    each(Z * bpq, 0, pick)

    def line_g(to, at):
        return remote(gbuf.at[pl.ds(to * bpq, bpq)], kv.at[c, y, :, at], s_g.at[to], r_g.at[at], z=to)

    own_g = pltpu.make_async_copy(gbuf.at[pl.ds(z * bpq, bpq)], kv.at[c, y, :, z], here.at[2])
    own_g.start()
    each(Z, 1, lambda i: line_g((z + nth_near(i, Z)) % Z, z).start())

    each(Z, Z // 2, send_q)
    own_g.wait()

    right, left, far, twin = (y + 1) % Y, (y + Y - 1) % Y, (y + 2) % Y, 1 - c

    def ring(kind, piece, at, send, recv, **device):
        part = kv.at[kind, piece, :, at]
        return remote(part, part, send.at[at], recv.at[at], **device)

    def to_twin(piece, at):
        return ring(c, piece, at, s_s.at[piece], r_s.at[piece], c=twin)

    def from_twin(piece, at):
        return ring(twin, piece, at, s_s.at[piece], r_s.at[piece], c=twin)

    to_right = lambda at: ring(c, y, at, s_r, r_l, y=right)
    to_left = lambda at: ring(c, y, at, s_l, r_r, y=left)
    from_left = lambda at: ring(c, left, at, s_r, r_l, y=left)
    from_right = lambda at: ring(c, right, at, s_l, r_r, y=right)
    pass_right = lambda at: ring(c, left, at, s_fr, r_fl, y=right)
    pass_left = lambda at: ring(c, right, at, s_fl, r_fr, y=left)
    far_left = lambda at: ring(c, far, at, s_fr, r_fl, y=left)
    far_right = lambda at: ring(c, far, at, s_fl, r_fr, y=right)

    def share(at):
        to_right(at).start()
        to_left(at).start()
        to_twin(y, at).start()

    def step1(i):
        at = (z + nth_near(i, Z)) % Z
        part = kv.at[c, y, :, at]
        remote(part, part, s_g.at[at], r_g.at[at], z=at).wait_recv()
        share(at)

    def step2(i):
        at = (z + nth_near(i, Z)) % Z
        from_left(at).wait_recv()

        @pl.when(at % 2 == 0)
        def _():
            pass_right(at).start()

        to_twin(left, at).start()
        from_right(at).wait_recv()

        @pl.when(at % 2 == 1)
        def _():
            pass_left(at).start()

        to_twin(right, at).start()

    def step3(i):
        at = (z + nth_near(i, Z)) % Z

        @pl.when(at % 2 == 0)
        def _():
            far_left(at).wait_recv()

        @pl.when(at % 2 == 1)
        def _():
            far_right(at).wait_recv()

        to_twin(far, at).start()

    share(z)
    my_len = qlen[z]

    def key_marks(i):
        piece, j = i // bpq, i % bpq
        var = vb[inv[z * bpq + j], piece]
        place = lane1 + (j * Y * slot + piece * slot)
        rows = pl.ds(pl.multiple_of(j * slot, slot), slot)
        kfs[piece, rows, :] = features(marks(var, jnp.where(place >= my_len, 1.0, 0.0), None), ktab[...])

    def query_marks(at):
        qfs[at] = features(marks(hv[at], 1.0, None), qtab[...])

    def steps12(i):
        step1(i)

        @pl.when(i < 3)
        def _():
            each(2 * bpq * i, 2 * bpq * (i - 1), key_marks)
            each(Z // 2 * i, Z // 2 * (i - 1), query_marks)

        @pl.when(i > 2)
        def _():
            own_part(early + i - 3)

        @pl.when(i > 2)
        def _():
            step2(i - 3)

    each(Z, 1, steps12)

    def build(n, piece):
        def one(j):
            k = kv[0, piece, j].reshape(slot, cols)
            v = kv[1, piece, j].reshape(slot, cols)
            rows = pl.ds(pl.multiple_of(j * slot, slot), slot)
            kf = kfs[piece, rows, :]
            for pair in range(pairs):
                tile = slice(pair * 128, pair * 128 + 128)
                for odd in range(2):
                    mine = (half >= DH) if odd else (half < DH)
                    ka[2 * pair + odd, n, rows, :] = jnp.where(mine, k[:, tile], kf)
                    vx[2 * pair + odd, n, rows, :] = jnp.where(mine, v[:, tile], jnp.ones_like(kf))

        each(bpq, 0, one)

    def take_q(i):
        at = (z + nth_near(i, Z)) % Z
        qf = qfs[at]
        q = qh[at]
        rows = pl.ds(pl.multiple_of(i * slot, slot), slot)
        for pair in range(pairs):
            tile = slice(pair * 128, pair * 128 + 128)
            for odd in range(2):
                mine = (half >= DH) if odd else (half < DH)
                qa[2 * pair + odd, rows, :] = jnp.where(mine, q[:, tile], qf[:, tile])

    def wait_q(i):
        at = (z + nth_near(i, Z)) % Z

        @pl.when(i == 0)
        def _():
            own_q.wait()

        @pl.when(i > 0)
        def _():
            line_q(at, at).wait_recv()

        take_q(i)

    side = Z // 2 * slot

    def attend(n, group):
        rows = pl.ds(pl.multiple_of(group * side, side), side)

        def score(h):
            return lax.dot_general(qa[h, rows, :], ka[h, n], (((1,), (1,)), ((), ())), preferred_element_type=F32)

        def weigh(h, s):
            old = mx[h, rows, :][:, :1]
            m = jnp.maximum(old, jnp.max(s, axis=1, keepdims=True))
            o = jnp.dot(jnp.exp(s - m).astype(BF16), vx[h, n], preferred_element_type=F32)
            acc[h, rows, :] = acc[h, rows, :] * jnp.exp(old - m) + o
            mx[h, rows, :] = jnp.broadcast_to(m, (side, 128))

        s = score(0)
        for h in range(heads):
            later = score(h + 1) if h + 1 < heads else None
            weigh(h, s)
            s = later

    def twins(piece):
        each(Z, 0, lambda at: from_twin(piece, at).wait_recv())

    def line_o(to, at):
        return (remote(oh.at[to], ro.at[at], s_o.at[to], r_o.at[at], z=to),
                remote(sth.at[to], rst.at[at], s_t.at[to], r_t.at[at], z=to))

    def settle(i):
        at = (z + nth_near(i, Z)) % Z
        rows = pl.ds(pl.multiple_of(i * slot, slot), slot)
        stats = jnp.zeros((slot, 128), F32)
        for pair in range(pairs):
            outs = []
            for odd in range(2):
                mine = (half >= DH) if odd else (half < DH)
                head = 2 * pair + odd
                total = acc[head, rows, :]
                turned = pltpu.roll(total, DH, 1)
                l = jnp.where(mine, turned, total)
                outs.append(total / l)
                stats = jnp.where(half == head, mx[head, rows, :], jnp.where(half == 4 + head, l, stats))
            oh[at, :, pair * 128:pair * 128 + 128] = jnp.where(half < DH, outs[0], outs[1]).astype(BF16)
        sth[at] = jnp.transpose(stats)[:8]

    own_o = pltpu.make_async_copy(oh.at[z], ro.at[z], here.at[2])
    own_t = pltpu.make_async_copy(sth.at[z], rst.at[z], here.at[3])

    def settle_send(i):
        settle(i)
        at = (z + nth_near(i, Z)) % Z

        @pl.when(i == 0)
        def _():
            own_o.start()
            own_t.start()

        @pl.when(i > 0)
        def _():
            for copy in line_o(at, z):
                copy.start()

    mid_row = slot // 2
    keep = lambda at: pltpu.make_async_copy(att.at[at], attg.at[x, at], mine_sem.at[at])

    def xring(src, who, at, send, recv, dev):
        return remote(src, attg.at[who, at], send.at[at], recv.at[at], x=dev)

    def xpass(who, at, piece, send, recv, dev):
        part = attg.at[who, at, pl.ds(piece * mid_row, mid_row)]
        return remote(part, part, send.at[at], recv.at[at], x=dev)

    xto_right = lambda at: xring(att.at[at], x, at, x_r, y_l, xright)
    xto_left = lambda at: xring(att.at[at], x, at, x_l, y_r, xleft)
    xfrom_left = lambda at: xring(att.at[at], xleft, at, x_r, y_l, xleft)
    xfrom_right = lambda at: xring(att.at[at], xright, at, x_l, y_r, xright)
    xpass_right = lambda at: xpass(xleft, at, 0, x_fr, y_fl, xright)
    xpass_left = lambda at: xpass(xright, at, 1, x_fl, y_fr, xleft)
    xfar_left = lambda at: xpass(xfar, at, 0, x_fr, y_fl, xleft)
    xfar_right = lambda at: xpass(xfar, at, 1, x_fl, y_fr, xright)

    def join(at):
        far_m, far_l = rst[at][0:4], rst[at][4:8]
        own_m, own_l = sts[at][0:4], sts[at][4:8]
        m = jnp.maximum(far_m, own_m)
        a = far_l * jnp.exp(far_m - m)
        b = own_l * jnp.exp(own_m - m)
        share = a / (a + b)
        wide = lax.dot_general(
            jnp.concatenate([share, jnp.zeros_like(share)], axis=0), widen, (((0,), (0,)), ((), ())),
            preferred_element_type=F32, precision=lax.Precision.HIGHEST)
        value = os[at] + wide * (ro[at].astype(F32) - os[at])
        att[at] = value.astype(BF16)
        keep(at).start()
        xto_right(at).start()
        xto_left(at).start()

    def home(i):
        return (z + Z - nth_near(i, Z)) % Z

    def arrive(i):
        at = home(i)

        @pl.when(i == 0)
        def _():
            own_o.wait()
            own_t.wait()

        @pl.when(i > 0)
        def _():
            for copy in line_o(at, at):
                copy.wait_recv()

        join(at)

    def forward(i):
        at = home(i)
        xfrom_left(at).wait_recv()
        xpass_right(at).start()
        xfrom_right(at).wait_recv()
        xpass_left(at).start()

    hz = Z // 2

    def main(t):
        group, n = t // Y, t % Y
        piece = jnp.where(n == 0, y, jnp.where(n == 1, left, jnp.where(n == 2, right, far)))

        @pl.when(n == 0)
        def _():
            rows = pl.ds(pl.multiple_of(group * side, side), side)
            for h in range(heads):
                acc[h, rows, :] = jnp.zeros((side, 128), F32)
                mx[h, rows, :] = jnp.full((side, 128), -3e38, F32)
            each(hz, 0, lambda i: wait_q(group * hz + i))

        @pl.when(t < Y)
        def _():
            twins(piece)
            build(n, piece)

        @pl.when(t == 0)
        def _():
            each(Z, Z - 3, step2)

        attend(n, group)

        @pl.when(t == 1)
        def _():
            each(Z, 0, step3)

        @pl.when(t == Y - 1)
        def _():
            each(hz, 0, settle_send)

        @pl.when(t == Y)
        def _():
            arrive(0)

        @pl.when(t == Y + 1)
        def _():
            each(hz, 1, arrive)

        @pl.when(t == Y + 2)
        def _():
            forward(0)

    each(2 * Y, 0, main)
    each(Z, hz, settle_send)
    each(hz, 1, forward)

    def late(i):
        arrive(i)

        @pl.when(i > Z // 2)
        def _():
            forward(i - 1)

    each(Z, Z // 2, late)
    forward(Z - 1)

    def finish(at):
        xfar_left(at).wait_recv()
        xfar_right(at).wait_recv()
        keep(at).wait()
        for copy in (xto_right(at), xto_left(at), xpass_right(at), xpass_left(at), to_right(at), to_left(at)):
            copy.wait_send()

        @pl.when(at % 2 == 0)
        def _():
            pass_right(at).wait_send()

        @pl.when(at % 2 == 1)
        def _():
            pass_left(at).wait_send()

        for piece in range(Y):
            to_twin(piece, at).wait_send()

    each(Z, 0, finish)
    w_keep.wait()
    w_pass(xfar, 0, 4, 6, xleft).wait_recv()
    w_pass(xfar, 1, 5, 7, xright).wait_recv()
    for copy in (w_whole(x, 0, 2, xright), w_whole(x, 1, 3, xleft),
                 w_pass(xleft, 0, 4, 6, xright), w_pass(xright, 1, 5, 7, xleft)):
        copy.wait_send()

    def end_line(i):
        at = (z + i) % Z
        for copy in line_b(at, at) + line_o(at, at) + (line_q(at, at), line_g(at, at)):
            copy.wait_send()

    each(Z, 1, end_line)

    def end_cluster(i):
        to = (w + i) % W
        remote(abuf.at[to], abuf.at[to], s_a.at[to], r_a.at[to], y=to // C, c=to % C).wait_send()
        remote(cvar, va.at[to], s_va.at[to], r_va.at[to], y=to // C, c=to % C).wait_send()

    each(W, 1, end_cluster)


def out_kernel(dq, ids, att_ref, next_ref, w_ref, x_ref, seg_ref, gain_ref, read_ref, upd_ref, pool_ref, y_ref):
    step = pl.program_id(0)
    parts, slot, cols = att_ref.shape[0], att_ref.shape[2], att_ref.shape[3]
    rows = [jnp.concatenate([ref[p, 0] for p in range(parts)], axis=1) for ref in (att_ref, next_ref)]
    y = jnp.dot(jnp.concatenate(rows, axis=0), w_ref[...], preferred_element_type=F32)
    y_ref[...] = y
    upd_ref[...] = y_ref[:, pl.ds(pl.multiple_of(ids[1] * cols, cols), cols)]
    hidden = x_ref[...].astype(F32) + y
    square = jnp.sum(hidden * hidden, axis=1, keepdims=True)
    weighted = jnp.sum(hidden * (gain_ref[...] * read_ref[...]), axis=1, keepdims=True)
    score = weighted * lax.rsqrt(square / y.shape[1] + 1e-06)
    row = lax.broadcasted_iota(jnp.int32, (8, slot), 0)
    for n in range(2):
        first = (ids[0] * pl.num_programs(0) * 2 + step * 2 + n) * 2
        member = jnp.where((row < 2) & (seg_ref[n] - first == row), 1.0, 0.0)
        own = jnp.broadcast_to(score[n * slot:n * slot + slot], (slot, 128))
        sums = jnp.dot(member, own, preferred_element_type=F32, precision=lax.Precision.HIGHEST)
        count = jnp.maximum(jnp.sum(member, axis=1, keepdims=True), 1.0)
        mean = sums / count
        for k in range(2):
            pool_ref[step * 4 + n * 2 + k] = mean[k, 0]


def body(sizes, doc_x, doc_seg, doc_query, doc_var, query_len, block_perm, cache_k, cache_v, cache_var,
         w_query, w_key, w_value, w_out, var_bias, norm_gain, readout):
    X, Y, Z, C = sizes
    W = Y * C
    tokens, cols = doc_x.shape[0], w_query.shape[1]
    features = doc_x.shape[1]
    heads = cols // DH
    slot = tokens // Z
    crows = cache_k.shape[0]
    blocks = Y * Z * C
    bpq = blocks // Z
    piece = crows // (Y * Z)
    part_keys = bpq * slot
    i32 = jnp.int32
    dma = pltpu.SemaphoreType.DMA

    half_size = DH // 2
    frequency = 10000.0 ** (-np.arange(half_size) / half_size)
    frequency = np.tile(frequency.astype(np.float32), 128 // half_size)
    turns = np.arange(slot)[:, None] * frequency.astype(np.float64)[None, :]
    seg = doc_seg.reshape(Z, 1, slot)

    vm = lambda *shape: pltpu.VMEM(shape, BF16)
    vf = lambda *shape: pltpu.VMEM(shape, F32)
    vi = lambda *shape: pltpu.VMEM(shape, i32)
    smem = pl.BlockSpec(memory_space=pltpu.SMEM)
    vmem = pl.BlockSpec(memory_space=pltpu.VMEM)
    hbm = pl.BlockSpec(memory_space=ANY)
    attended, w_all, ids = pl.pallas_call(
        functools.partial(attention_kernel, sizes),
        in_specs=[smem] * 4 + [vmem] * 5 + [hbm] * 8,
        out_specs=[hbm] * 2 + [smem],
        out_shape=[
            jax.ShapeDtypeStruct((X, Z, slot, cols), BF16),
            jax.ShapeDtypeStruct((X, cols, features), BF16),
            jax.ShapeDtypeStruct((2,), i32),
        ],
        scratch_shapes=[
            pltpu.SMEM((blocks,), i32), vm(Z, slot, features), vm(features, cols), vm(features, cols), vm(features, cols),
            pltpu.SMEM((Z,), i32),
            vm(W, Z, piece, cols), vm(Z * W, piece, cols), vm(Z * bpq, piece, cols),
            vi(W, Y, 1, slot), vi(Z * W, Y, 1, slot),
            vm(C, Y, bpq, Z, piece, cols),
            vm(Z, slot, cols), vm(Z, slot, cols), vi(Z, 1, slot), vi(Z, 1, slot),
            vf(Z, slot, 128), vf(Z, slot, 128), vm(16, cols), vm(16, 128),
            vf(Z, slot, cols), vf(Z, 8, slot), vm(Y, part_keys, 128), vm(Z, slot, cols),
            vm(heads, Y, part_keys, 128), vm(heads, Y, part_keys, 128), vm(heads, tokens, 128),
            vf(heads, tokens, 128), vf(heads, tokens, 128),
            vm(Z, slot, cols), vf(Z, 8, slot), vm(Z, slot, cols), vf(Z, 8, slot), vm(Z, slot, cols),
            dma((4,)),
        ] + [dma((W,))] * 4 + [dma((Z,))] * 10 + [dma((Z,))] * 8 + [dma((Y, Z))] * 2
        + [dma((Z,))] * 4 + [dma((Z,))] * 9 + [dma((5,)), dma((9,))],
        compiler_params=pltpu.CompilerParams(
            collective_id=0, has_side_effects=True, vmem_limit_bytes=56 << 20),
        name="attention",
    )(block_perm, doc_query, query_len, var_bias, seg, doc_var.reshape(Z, 1, slot),
      jnp.asarray(np.cos(turns), F32), jnp.asarray(np.sin(turns), F32), jnp.asarray(frequency)[None, :],
      doc_x.reshape(Z, slot, features), w_query, w_key, w_value,
      cache_k.reshape(Y, Z, piece, cols), cache_v.reshape(Y, Z, piece, cols), cache_var.reshape(Y, 1, slot), w_out)

    full = lambda *shape: pl.BlockSpec(shape, lambda i, *_: (0,) * len(shape))
    update, pooled = pl.pallas_call(
        out_kernel,
        grid_spec=pltpu.PrefetchScalarGridSpec(
            num_scalar_prefetch=2,
            grid=(Z // 2,),
            in_specs=[
                pl.BlockSpec((X, 1, slot, cols), lambda i, d, n: (0, d[n[0] * 2 * Z + 4 * i], 0, 0)),
                pl.BlockSpec((X, 1, slot, cols), lambda i, d, n: (0, d[n[0] * 2 * Z + 4 * i + 2], 0, 0)),
                full(X * cols, features),
                pl.BlockSpec((2 * slot, features), lambda i, d, n: (i, 0)),
                pl.BlockSpec((2, 1, slot), lambda i, d, n: (i, 0, 0)),
                full(1, features),
                full(1, features),
            ],
            out_specs=[
                pl.BlockSpec((2 * slot, cols), lambda i, d, n: (i, 0)),
                smem,
            ],
            scratch_shapes=[pltpu.VMEM((2 * slot, features), F32)],
        ),
        out_shape=[
            jax.ShapeDtypeStruct((tokens, cols), F32),
            jax.ShapeDtypeStruct((2 * Z,), F32),
        ],
        compiler_params=pltpu.CompilerParams(vmem_limit_bytes=60 << 20),
        name="out_part",
    )(doc_query, ids, attended, attended, w_all.reshape(X * cols, features), doc_x, seg, norm_gain.reshape(1, features),
      readout.reshape(1, features))
    return update, pooled


def solution(mesh):
    heads = mesh.shape["head"]
    cores = 2
    across = 4
    along = mesh.shape["blk"] // (across * cores)
    sizes = (heads, across, along, cores)
    split = Mesh(mesh.devices.reshape(sizes), ("x", "y", "z", "c"))
    return jax.shard_map(
        functools.partial(body, sizes),
        mesh=split,
        in_specs=(
            P(BLK, None), P(BLK), P(), P(BLK), P(), P(),
            P(BLK, "x"), P(BLK, "x"), P(BLK),
            P(None, "x"), P(None, "x"), P(None, "x"), P("x", None), P(None, "x"),
            P(), P(),
        ),
        out_specs=(P(BLK, "x"), P(BLK)),
        check_vma=False,
    )
```

```python
import functools

import jax
import jax.numpy as jnp
import numpy as np
from jax import lax
from jax.experimental import pallas as pl
from jax.experimental.pallas import tpu as pltpu
from jax.sharding import Mesh, PartitionSpec as P

DH = 64
F32 = jnp.float32
BF16 = jnp.bfloat16
NEG = -1e30
ANY = pl.ANY
BLK = ("y", "z", "c")


def remote(src, dst, send_sem, recv_sem, **device):
    return pltpu.make_async_remote_copy(
        src_ref=src,
        dst_ref=dst,
        send_sem=send_sem,
        recv_sem=recv_sem,
        device_id=device,
        device_id_type=pl.DeviceIdType.MESH,
    )


def each(count, first, step):
    def run(i, carry):
        step(i)
        return carry

    lax.fori_loop(first, count, run, 0)


def nth_near(i, Z):
    return lax.rem(jnp.where(i % 2 == 1, (i + 1) // 2, Z - i // 2), Z)


def attention_kernel(
    sizes, perm, dq, qlen, bias, seg_ref, var_ref, tcos_ref, tsin_ref, freq_ref, x_in, wq_in, wk_in, wv_in, gain_ref, read_ref, ck, cv, cvar, w_in, upd, pool,
    attg, w_all, ytmp, yown, yout, means, inv, xv, wq, wk, wv, order, abuf, bbuf, gbuf, va, vb, kv, qrot, qh, dv, hv, cosv, sinv, qtab, ktab,
    os, sts, kfs, qfs, ka, vx, qa, acc, mx, oh, sth, ro, rst,
    s_x, s_a, r_a, s_va, r_va, s_b, r_b, s_vb, r_vb, s_g, r_g, s_q, r_q, s_dv, r_dv,
    s_r, s_l, r_l, r_r, s_fr, s_fl, r_fl, r_fr, s_s, r_s,
    s_o, r_o, s_t, r_t, x_r, x_l, y_l, y_r, x_fr, x_fl, y_fl, y_fr, here, w_sem, out_sem,
):
    X, Y, Z, C = sizes
    x, y, z, c = lax.axis_index("x"), lax.axis_index("y"), lax.axis_index("z"), lax.axis_index("c")
    W = Y * C
    w = y * C + c
    bpq = W
    blk = (y * Z + z) * C + c
    slot, cols = qrot.shape[1], qrot.shape[2]
    heads = cols // DH
    pairs = cols // 128
    part_keys = bpq * slot
    barrier = pltpu.get_barrier_semaphore()

    loads = [pltpu.make_async_copy(s, d, s_x.at[n]) for n, (s, d) in
             enumerate(((x_in, xv), (wq_in, wq), (wk_in, wk), (wv_in, wv)))]
    for load in loads:
        load.start()

    def greet(**device):
        pl.semaphore_signal(barrier, inc=1, device_id=device, device_id_type=pl.DeviceIdType.MESH)

    each(W, 1, lambda i: greet(y=(w + i) % W // C, c=(w + i) % W % C))
    each(Z, 1, lambda i: greet(z=(z + i) % Z))
    for side in ((x + 1) % X, (x + X - 1) % X):
        greet(x=side)

    slot_query = [dq[blk * 2 * Z + 2 * j] for j in range(Z)]
    for query in range(Z):
        at = jnp.int32(0)
        for j in range(Z):
            at = jnp.where(slot_query[j] == query, j, at)
        order[query] = at
    lane2 = lax.broadcasted_iota(jnp.int32, (16, cols), 1)
    row2 = lax.broadcasted_iota(jnp.int32, (16, cols), 0)
    feat2 = lane2 % DH
    lane_head = 2 * (lane2 // 128) + (1 - lane2 % 128 // DH)
    delta = jnp.zeros((16, cols), F32)
    for h in range(heads):
        delta = jnp.where(lane_head == h, bias[0, h] - bias[1, h], delta)
    hi = delta.astype(BF16).astype(F32)
    mid = (delta - hi).astype(BF16).astype(F32)
    low = delta - hi - mid
    value = jnp.where(feat2 < 8, hi, jnp.where(feat2 < 16, mid, low))
    value = jnp.where((feat2 < 24) & (feat2 % 8 == row2), value, 0.0)
    qtab[...] = jnp.where((row2 >= 8) & (row2 < 11) & (feat2 == row2 + 16), 1.0, value).astype(BF16)
    lane1, row1 = lane2[:, :128], row2[:, :128]
    feat1 = lane1 % DH
    value = jnp.where((feat1 < 24) & (feat1 % 8 == row1), 1.0, 0.0)
    hit = (((row1 == 8) & (feat1 == 24)) | ((row1 == 9) & (feat1 == 26)) | ((row1 == 10) & (feat1 == 25)))
    ktab[...] = jnp.where(hit, NEG, value).astype(BF16)

    def features(rows, table):
        return lax.dot_general(rows.astype(BF16), table, (((0,), (0,)), ((), ())),
                               preferred_element_type=F32).astype(BF16)

    def marks(var, eight, seg):
        same = jnp.where((row1 < 8) & (var == row1), 1.0, 0.0)
        rows = jnp.where(row1 == 8, eight, same)
        if seg is not None:
            rows = jnp.where(((row1 == 9) & (seg == 0)) | ((row1 == 10) & (seg == 1)), 1.0, rows)
        return rows

    pl.semaphore_wait(barrier, W - 1 + Z - 1 + 2)

    for step in range(1, Y):
        to = (y + step) % Y
        for kind in range(C):
            remote((ck, cv)[kind].at[to], abuf.at[w], s_a.at[to * C + kind], r_a.at[w], y=to, c=kind).start()
            remote(cvar, va.at[w], s_va.at[to * C + kind], r_va.at[w], y=to, c=kind).start()
    for kind in range(C):
        src = (ck, cv)[kind].at[y]

        @pl.when(kind != c)
        def _():
            remote(src, abuf.at[w], s_a.at[y * C + kind], r_a.at[w], c=kind).start()
            remote(cvar, va.at[w], s_va.at[y * C + kind], r_va.at[w], c=kind).start()

        @pl.when(kind == c)
        def _():
            pltpu.make_async_copy(src, abuf.at[w], here.at[0]).start()

    own_var = pltpu.make_async_copy(cvar, va.at[w], here.at[1])
    own_var.start()

    xright, xleft, xfar = (x + 1) % X, (x + X - 1) % X, (x + 2) % X
    w_half = w_in.shape[0] // 2
    w_keep = pltpu.make_async_copy(w_in, w_all.at[x], w_sem.at[8])

    def w_whole(who, send, recv, dev):
        return remote(w_in, w_all.at[who], w_sem.at[send], w_sem.at[recv], x=dev)

    def w_pass(who, piece, send, recv, dev):
        part = w_all.at[who, pl.ds(piece * w_half, w_half)]
        return remote(part, part, w_sem.at[send], w_sem.at[recv], x=dev)

    w_keep.start()
    w_whole(x, 0, 2, xright).start()
    w_whole(x, 1, 3, xleft).start()

    lane = lax.broadcasted_iota(jnp.int32, (slot, cols), 1)
    half = lax.broadcasted_iota(jnp.int32, (slot, 128), 1)
    first_lanes = (lane % DH) < DH // 2
    first_half = (half % DH) < DH // 2
    ones_row = jnp.where(row1 == 10, 1.0, 0.0).astype(BF16)

    def segment(at):
        return seg_ref[at] - (blk * 2 * Z + 2 * at)

    def turn(a, query):
        other = jnp.where(first_lanes, pltpu.roll(a, cols - DH // 2, 1), pltpu.roll(a, DH // 2, 1))
        cosine = jnp.concatenate([cosv[query]] * pairs, axis=1)
        sine = jnp.concatenate([sinv[query]] * pairs, axis=1)
        return a * cosine + other * sine

    loads[0].wait()
    loads[1].wait()

    def project_q(query):
        at = order[query]
        seg = segment(at)
        length = qlen[query].astype(F32)
        count = jnp.sum(jnp.where(seg == 0, 1.0, 0.0), axis=1, keepdims=True)
        base0 = freq_ref[...] * length
        base1 = freq_ref[...] * (length - count)
        second = features(marks(var_ref[at], 1.0, seg), ones_row).astype(F32) > 0.5
        cos_a = jnp.where(second, jnp.cos(base1), jnp.cos(base0))
        sin_a = jnp.where(second, jnp.sin(base1), jnp.sin(base0))
        cosv[query] = cos_a * tcos_ref[...] - sin_a * tsin_ref[...]
        sine = sin_a * tcos_ref[...] + cos_a * tsin_ref[...]
        sinv[query] = jnp.where(first_half, -sine, sine)
        a = jnp.dot(xv[at], wq[...], preferred_element_type=F32)
        qrot[query] = (turn(a, query) * 0.125).astype(BF16)
        dv[query] = var_ref[at]

    each(Z, 0, project_q)

    def line_q(to, at):
        return remote(qrot.at[to], qh.at[at], s_q.at[to], r_q.at[at], z=to)

    def send_q(i):
        line_q((z + nth_near(i, Z)) % Z, z).start()

    each(Z // 2, 1, send_q)
    own_q = pltpu.make_async_copy(qrot.at[z], qh.at[z], here.at[4])
    own_q.start()

    pltpu.make_async_copy(ck.at[y], abuf.at[w], here.at[0]).wait()
    own_var.wait()

    def wait_a(i):
        src = (w + i) % W
        remote(abuf.at[src], abuf.at[src], s_a.at[src], r_a.at[src], y=src // C, c=src % C).wait_recv()
        remote(va.at[src], va.at[src], s_va.at[src], r_va.at[src], y=src // C, c=src % C).wait_recv()

    each(W, 1, wait_a)

    def line_b(to, at):
        return (remote(abuf.at[:, to], bbuf.at[pl.ds(at * W, W)], s_b.at[to], r_b.at[at], z=to),
                remote(va, vb.at[pl.ds(at * W, W)], s_vb.at[to], r_vb.at[at], z=to),
                remote(dv.at[to], hv.at[at], s_dv.at[to], r_dv.at[at], z=to))

    def send_b(i):
        for copy in line_b((z + nth_near(i, Z)) % Z, z):
            copy.start()

    each(Z, 1, send_b)
    own_b = pltpu.make_async_copy(abuf.at[:, z], bbuf.at[pl.ds(z * W, W)], here.at[2])
    own_vb = pltpu.make_async_copy(va, vb.at[pl.ds(z * W, W)], here.at[3])
    own_dv = pltpu.make_async_copy(dv.at[z], hv.at[z], here.at[1])
    own_b.start()
    own_vb.start()
    own_dv.start()

    loads[2].wait()
    loads[3].wait()
    wide8 = lax.broadcasted_iota(jnp.int32, (8, cols), 1)
    deep8 = lax.broadcasted_iota(jnp.int32, (8, cols), 0)
    widen = jnp.where(wide8 // DH == deep8, 1.0, 0.0).astype(F32)

    def own_part(query):
        at = order[query]
        xs = xv[at]
        k = turn(jnp.dot(xs, wk[...], preferred_element_type=F32), query).astype(BF16)
        v = jnp.dot(xs, wv[...], preferred_element_type=F32).astype(BF16)
        seg = segment(at)
        qf = features(marks(var_ref[at], 1.0, seg), qtab[...])
        kf = features(marks(var_ref[at], 0.0, seg), ktab[...])
        q = qrot[query]
        stats = jnp.zeros((slot, 128), F32)
        for pair in range(pairs):
            tile = slice(pair * 128, pair * 128 + 128)
            outs = []
            for odd in range(2):
                mine = (half >= DH) if odd else (half < DH)
                qs = jnp.where(mine, q[:, tile], qf[:, tile])
                ks = jnp.where(mine, k[:, tile], kf)
                s = lax.dot_general(qs, ks, (((1,), (1,)), ((), ())), preferred_element_type=F32)
                m = jnp.max(s, axis=1, keepdims=True)
                p = jnp.exp(s - m)
                l = jnp.sum(p, axis=1, keepdims=True)
                outs.append(jnp.dot(p.astype(BF16), v[:, tile], preferred_element_type=F32) / l)
                head = 2 * pair + odd
                stats = jnp.where(half == head, m, jnp.where(half == 4 + head, l, stats))
            os[query, :, tile] = jnp.where(half < DH, outs[0], outs[1])
        sts[query] = jnp.transpose(stats)[:8]

    early = Z // 2 - 1
    each(early, 0, own_part)

    def find(k):
        at = jnp.int32(0)
        for e in range(Z * W):
            at = jnp.where(perm[e] == k, e // C % Z * W + e // (Z * C) * C + e % C, at)
        inv[k] = at

    each(Z * W, 0, find)
    w_whole(xleft, 0, 2, xleft).wait_recv()
    w_pass(xleft, 0, 4, 6, xright).start()
    w_whole(xright, 1, 3, xright).wait_recv()
    w_pass(xright, 1, 5, 7, xleft).start()

    own_b.wait()
    own_vb.wait()
    own_dv.wait()

    def wait_b(i):
        src = (z + i) % Z
        part = bbuf.at[pl.ds(src * W, W)]
        remote(part, part, s_b.at[src], r_b.at[src], z=src).wait_recv()
        part = vb.at[pl.ds(src * W, W)]
        remote(part, part, s_vb.at[src], r_vb.at[src], z=src).wait_recv()
        remote(hv.at[src], hv.at[src], s_dv.at[src], r_dv.at[src], z=src).wait_recv()

    each(Z, 1, wait_b)

    def pick(i):
        gbuf[i] = bbuf[inv[i]]

    each(Z * bpq, 0, pick)

    def line_g(to, at):
        return remote(gbuf.at[pl.ds(to * bpq, bpq)], kv.at[c, y, :, at], s_g.at[to], r_g.at[at], z=to)

    own_g = pltpu.make_async_copy(gbuf.at[pl.ds(z * bpq, bpq)], kv.at[c, y, :, z], here.at[2])
    own_g.start()
    each(Z, 1, lambda i: line_g((z + nth_near(i, Z)) % Z, z).start())

    each(Z, Z // 2, send_q)
    own_g.wait()

    right, left, far, twin = (y + 1) % Y, (y + Y - 1) % Y, (y + 2) % Y, 1 - c

    def ring(kind, piece, at, send, recv, **device):
        part = kv.at[kind, piece, :, at]
        return remote(part, part, send.at[at], recv.at[at], **device)

    def to_twin(piece, at):
        return ring(c, piece, at, s_s.at[piece], r_s.at[piece], c=twin)

    def from_twin(piece, at):
        return ring(twin, piece, at, s_s.at[piece], r_s.at[piece], c=twin)

    to_right = lambda at: ring(c, y, at, s_r, r_l, y=right)
    to_left = lambda at: ring(c, y, at, s_l, r_r, y=left)
    from_left = lambda at: ring(c, left, at, s_r, r_l, y=left)
    from_right = lambda at: ring(c, right, at, s_l, r_r, y=right)
    pass_right = lambda at: ring(c, left, at, s_fr, r_fl, y=right)
    pass_left = lambda at: ring(c, right, at, s_fl, r_fr, y=left)
    far_left = lambda at: ring(c, far, at, s_fr, r_fl, y=left)
    far_right = lambda at: ring(c, far, at, s_fl, r_fr, y=right)

    def share(at):
        to_right(at).start()
        to_left(at).start()
        to_twin(y, at).start()

    def step1(i):
        at = (z + nth_near(i, Z)) % Z
        part = kv.at[c, y, :, at]
        remote(part, part, s_g.at[at], r_g.at[at], z=at).wait_recv()
        share(at)

    def step2(i):
        at = (z + nth_near(i, Z)) % Z
        from_left(at).wait_recv()

        @pl.when(at % 2 == 0)
        def _():
            pass_right(at).start()

        to_twin(left, at).start()
        from_right(at).wait_recv()

        @pl.when(at % 2 == 1)
        def _():
            pass_left(at).start()

        to_twin(right, at).start()

    def step3(i):
        at = (z + nth_near(i, Z)) % Z

        @pl.when(at % 2 == 0)
        def _():
            far_left(at).wait_recv()

        @pl.when(at % 2 == 1)
        def _():
            far_right(at).wait_recv()

        to_twin(far, at).start()

    share(z)
    my_len = qlen[z]

    def key_marks(i):
        piece, j = i // bpq, i % bpq
        var = vb[inv[z * bpq + j], piece]
        place = lane1 + (j * Y * slot + piece * slot)
        rows = pl.ds(pl.multiple_of(j * slot, slot), slot)
        kfs[piece, rows, :] = features(marks(var, jnp.where(place >= my_len, 1.0, 0.0), None), ktab[...])

    def query_marks(at):
        qfs[at] = features(marks(hv[at], 1.0, None), qtab[...])

    def steps12(i):
        step1(i)

        @pl.when(i < 3)
        def _():
            each(2 * bpq * i, 2 * bpq * (i - 1), key_marks)
            each(Z // 2 * i, Z // 2 * (i - 1), query_marks)

        @pl.when(i > 2)
        def _():
            own_part(early + i - 3)

        @pl.when(i > 2)
        def _():
            step2(i - 3)

    each(Z, 1, steps12)

    def build(n, piece):
        def one(j):
            k = kv[0, piece, j].reshape(slot, cols)
            v = kv[1, piece, j].reshape(slot, cols)
            rows = pl.ds(pl.multiple_of(j * slot, slot), slot)
            kf = kfs[piece, rows, :]
            for pair in range(pairs):
                tile = slice(pair * 128, pair * 128 + 128)
                for odd in range(2):
                    mine = (half >= DH) if odd else (half < DH)
                    ka[2 * pair + odd, n, rows, :] = jnp.where(mine, k[:, tile], kf)
                    vx[2 * pair + odd, n, rows, :] = jnp.where(mine, v[:, tile], jnp.ones_like(kf))

        each(bpq, 0, one)

    def take_q(i):
        at = (z + nth_near(i, Z)) % Z
        qf = qfs[at]
        q = qh[at]
        rows = pl.ds(pl.multiple_of(i * slot, slot), slot)
        for pair in range(pairs):
            tile = slice(pair * 128, pair * 128 + 128)
            for odd in range(2):
                mine = (half >= DH) if odd else (half < DH)
                qa[2 * pair + odd, rows, :] = jnp.where(mine, q[:, tile], qf[:, tile])

    def wait_q(i):
        at = (z + nth_near(i, Z)) % Z

        @pl.when(i == 0)
        def _():
            own_q.wait()

        @pl.when(i > 0)
        def _():
            line_q(at, at).wait_recv()

        take_q(i)

    side = Z // 2 * slot

    def attend(n, group):
        rows = pl.ds(pl.multiple_of(group * side, side), side)

        def score(h):
            return lax.dot_general(qa[h, rows, :], ka[h, n], (((1,), (1,)), ((), ())), preferred_element_type=F32)

        def weigh(h, s):
            old = mx[h, rows, :][:, :1]
            m = jnp.maximum(old, jnp.max(s, axis=1, keepdims=True))
            o = jnp.dot(jnp.exp(s - m).astype(BF16), vx[h, n], preferred_element_type=F32)
            acc[h, rows, :] = acc[h, rows, :] * jnp.exp(old - m) + o
            mx[h, rows, :] = jnp.broadcast_to(m, (side, 128))

        s = score(0)
        for h in range(heads):
            later = score(h + 1) if h + 1 < heads else None
            weigh(h, s)
            s = later

    def twins(piece):
        each(Z, 0, lambda at: from_twin(piece, at).wait_recv())

    def line_o(to, at):
        return (remote(oh.at[to], ro.at[at], s_o.at[to], r_o.at[at], z=to),
                remote(sth.at[to], rst.at[at], s_t.at[to], r_t.at[at], z=to))

    def settle(i):
        at = (z + nth_near(i, Z)) % Z
        rows = pl.ds(pl.multiple_of(i * slot, slot), slot)
        stats = jnp.zeros((slot, 128), F32)
        for pair in range(pairs):
            outs = []
            for odd in range(2):
                mine = (half >= DH) if odd else (half < DH)
                head = 2 * pair + odd
                total = acc[head, rows, :]
                turned = pltpu.roll(total, DH, 1)
                l = jnp.where(mine, turned, total)
                outs.append(total / l)
                stats = jnp.where(half == head, mx[head, rows, :], jnp.where(half == 4 + head, l, stats))
            oh[at, :, pair * 128:pair * 128 + 128] = jnp.where(half < DH, outs[0], outs[1]).astype(BF16)
        sth[at] = jnp.transpose(stats)[:8]

    own_o = pltpu.make_async_copy(oh.at[z], ro.at[z], here.at[2])
    own_t = pltpu.make_async_copy(sth.at[z], rst.at[z], here.at[3])

    def settle_send(i):
        settle(i)
        at = (z + nth_near(i, Z)) % Z

        @pl.when(i == 0)
        def _():
            own_o.start()
            own_t.start()

        @pl.when(i > 0)
        def _():
            for copy in line_o(at, z):
                copy.start()

    mid_row = slot // 2

    def xring(who, at, send, recv, dev):
        part = attg.at[who, at]
        return remote(part, part, send.at[at], recv.at[at], x=dev)

    def xpass(who, at, piece, send, recv, dev):
        part = attg.at[who, at, pl.ds(piece * mid_row, mid_row)]
        return remote(part, part, send.at[at], recv.at[at], x=dev)

    xto_right = lambda at: xring(x, at, x_r, y_l, xright)
    xto_left = lambda at: xring(x, at, x_l, y_r, xleft)
    xfrom_left = lambda at: xring(xleft, at, x_r, y_l, xleft)
    xfrom_right = lambda at: xring(xright, at, x_l, y_r, xright)
    xpass_right = lambda at: xpass(xleft, at, 0, x_fr, y_fl, xright)
    xpass_left = lambda at: xpass(xright, at, 1, x_fl, y_fr, xleft)
    xfar_left = lambda at: xpass(xfar, at, 0, x_fr, y_fl, xleft)
    xfar_right = lambda at: xpass(xfar, at, 1, x_fl, y_fr, xright)

    def join(at):
        far_m, far_l = rst[at][0:4], rst[at][4:8]
        own_m, own_l = sts[at][0:4], sts[at][4:8]
        m = jnp.maximum(far_m, own_m)
        a = far_l * jnp.exp(far_m - m)
        b = own_l * jnp.exp(own_m - m)
        share = a / (a + b)
        wide = lax.dot_general(
            jnp.concatenate([share, jnp.zeros_like(share)], axis=0), widen, (((0,), (0,)), ((), ())),
            preferred_element_type=F32, precision=lax.Precision.HIGHEST)
        value = os[at] + wide * (ro[at].astype(F32) - os[at])
        attg[x, at] = value.astype(BF16)
        xto_right(at).start()
        xto_left(at).start()

    def home(i):
        return (z + Z - nth_near(i, Z)) % Z

    def arrive(i):
        at = home(i)

        @pl.when(i == 0)
        def _():
            own_o.wait()
            own_t.wait()

        @pl.when(i > 0)
        def _():
            for copy in line_o(at, at):
                copy.wait_recv()

        join(at)

    def forward(i):
        at = home(i)
        xfrom_left(at).wait_recv()
        xpass_right(at).start()
        xfrom_right(at).wait_recv()
        xpass_left(at).start()

    hz = Z // 2

    def main(t):
        group, n = t // Y, t % Y
        piece = jnp.where(n == 0, y, jnp.where(n == 1, left, jnp.where(n == 2, right, far)))

        @pl.when(n == 0)
        def _():
            rows = pl.ds(pl.multiple_of(group * side, side), side)
            for h in range(heads):
                acc[h, rows, :] = jnp.zeros((side, 128), F32)
                mx[h, rows, :] = jnp.full((side, 128), -3e38, F32)
            each(hz, 0, lambda i: wait_q(group * hz + i))

        @pl.when(t < Y)
        def _():
            twins(piece)
            build(n, piece)

        @pl.when(t == 0)
        def _():
            each(Z, Z - 3, step2)

        attend(n, group)

        @pl.when(t == 1)
        def _():
            each(Z, 0, step3)

        @pl.when(t == Y - 1)
        def _():
            each(hz, 0, settle_send)

        @pl.when(t == Y)
        def _():
            arrive(0)

        @pl.when(t == Y + 1)
        def _():
            each(hz, 1, arrive)

        @pl.when(t == Y + 2)
        def _():
            forward(0)

    each(2 * Y, 0, main)
    each(Z, hz, settle_send)
    each(hz, 1, forward)

    w_keep.wait()
    w_pass(xfar, 0, 4, 6, xleft).wait_recv()
    w_pass(xfar, 1, 5, 7, xright).wait_recv()
    width = xv.shape[2]
    row8 = lax.broadcasted_iota(jnp.int32, (8, slot), 0)

    def collect(i):
        at = home(i)
        xfar_left(at).wait_recv()
        xfar_right(at).wait_recv()
        place = order[at]
        rows = jnp.concatenate([attg[p, at] for p in range(X)], axis=1)
        value = jnp.dot(rows, w_all[...].reshape(X * cols, width), preferred_element_type=F32)
        ytmp[...] = value
        yown[at] = ytmp[:, pl.ds(pl.multiple_of(x * cols, cols), cols)]
        hidden = xv[place].astype(F32) + value
        square = jnp.sum(hidden * hidden, axis=1, keepdims=True)
        weighted = jnp.sum(hidden * (gain_ref[...] * read_ref[...]), axis=1, keepdims=True)
        score = weighted * lax.rsqrt(square / width + 1e-06)
        member = jnp.where((row8 < 2) & (segment(place) == row8), 1.0, 0.0)
        sums = jnp.dot(member, jnp.broadcast_to(score, (slot, 128)),
                       preferred_element_type=F32, precision=lax.Precision.HIGHEST)
        means[at] = sums / jnp.maximum(jnp.sum(member, axis=1, keepdims=True), 1.0)

    def late(i):
        collect(i - hz)
        arrive(i)

        @pl.when(i > Z // 2)
        def _():
            forward(i - 1)

    each(Z, hz, late)
    forward(Z - 1)
    each(Z, hz, collect)
    outs = []
    lane8 = lax.broadcasted_iota(jnp.int32, (8, 128), 1)
    pooled = jnp.zeros((8, 128), F32)
    for j in range(Z):
        query = slot_query[j]
        yout[j] = yown[query]
        outs.append(pltpu.make_async_copy(yout.at[j], upd.at[j], out_sem.at[j]))
        outs[j].start()
        mean = means[query]
        for k in range(2):
            pooled = jnp.where(lane8 == 2 * j + k, jnp.broadcast_to(mean[k:k + 1], (8, 128)), pooled)
    pool[...] = pooled

    def finish(at):
        for copy in (xto_right(at), xto_left(at), xpass_right(at), xpass_left(at), to_right(at), to_left(at)):
            copy.wait_send()

        @pl.when(at % 2 == 0)
        def _():
            pass_right(at).wait_send()

        @pl.when(at % 2 == 1)
        def _():
            pass_left(at).wait_send()

        for piece in range(Y):
            to_twin(piece, at).wait_send()

    each(Z, 0, finish)
    for copy in (w_whole(x, 0, 2, xright), w_whole(x, 1, 3, xleft),
                 w_pass(xleft, 0, 4, 6, xright), w_pass(xright, 1, 5, 7, xleft)):
        copy.wait_send()

    def end_line(i):
        at = (z + i) % Z
        for copy in line_b(at, at) + line_o(at, at) + (line_q(at, at), line_g(at, at)):
            copy.wait_send()

    each(Z, 1, end_line)

    def end_cluster(i):
        to = (w + i) % W
        remote(abuf.at[to], abuf.at[to], s_a.at[to], r_a.at[to], y=to // C, c=to % C).wait_send()
        remote(cvar, va.at[to], s_va.at[to], r_va.at[to], y=to // C, c=to % C).wait_send()

    each(W, 1, end_cluster)
    for copy in outs:
        copy.wait()


def body(sizes, doc_x, doc_seg, doc_query, doc_var, query_len, block_perm, cache_k, cache_v, cache_var,
         w_query, w_key, w_value, w_out, var_bias, norm_gain, readout):
    X, Y, Z, C = sizes
    W = Y * C
    tokens, cols = doc_x.shape[0], w_query.shape[1]
    features = doc_x.shape[1]
    heads = cols // DH
    slot = tokens // Z
    crows = cache_k.shape[0]
    blocks = Y * Z * C
    bpq = blocks // Z
    piece = crows // (Y * Z)
    part_keys = bpq * slot
    i32 = jnp.int32
    dma = pltpu.SemaphoreType.DMA

    half_size = DH // 2
    frequency = 10000.0 ** (-np.arange(half_size) / half_size)
    frequency = np.tile(frequency.astype(np.float32), 128 // half_size)
    turns = np.arange(slot)[:, None] * frequency.astype(np.float64)[None, :]
    seg = doc_seg.reshape(Z, 1, slot)

    vm = lambda *shape: pltpu.VMEM(shape, BF16)
    vf = lambda *shape: pltpu.VMEM(shape, F32)
    vi = lambda *shape: pltpu.VMEM(shape, i32)
    smem = pl.BlockSpec(memory_space=pltpu.SMEM)
    vmem = pl.BlockSpec(memory_space=pltpu.VMEM)
    hbm = pl.BlockSpec(memory_space=ANY)
    update, pooled = pl.pallas_call(
        functools.partial(attention_kernel, sizes),
        in_specs=[smem] * 4 + [vmem] * 5 + [hbm] * 4 + [vmem] * 2 + [hbm] * 4,
        out_specs=[hbm, vmem],
        out_shape=[
            jax.ShapeDtypeStruct((Z, slot, cols), F32),
            jax.ShapeDtypeStruct((8, 128), F32),
        ],
        scratch_shapes=[
            vm(X, Z, slot, cols), vm(X, cols, features), vf(slot, features), vf(Z, slot, cols), vf(Z, slot, cols),
            vf(Z, 8, 128),
            pltpu.SMEM((blocks,), i32), vm(Z, slot, features), vm(features, cols), vm(features, cols), vm(features, cols),
            pltpu.SMEM((Z,), i32),
            vm(W, Z, piece, cols), vm(Z * W, piece, cols), vm(Z * bpq, piece, cols),
            vi(W, Y, 1, slot), vi(Z * W, Y, 1, slot),
            vm(C, Y, bpq, Z, piece, cols),
            vm(Z, slot, cols), vm(Z, slot, cols), vi(Z, 1, slot), vi(Z, 1, slot),
            vf(Z, slot, 128), vf(Z, slot, 128), vm(16, cols), vm(16, 128),
            vf(Z, slot, cols), vf(Z, 8, slot), vm(Y, part_keys, 128), vm(Z, slot, cols),
            vm(heads, Y, part_keys, 128), vm(heads, Y, part_keys, 128), vm(heads, tokens, 128),
            vf(heads, tokens, 128), vf(heads, tokens, 128),
            vm(Z, slot, cols), vf(Z, 8, slot), vm(Z, slot, cols), vf(Z, 8, slot),
            dma((4,)),
        ] + [dma((W,))] * 4 + [dma((Z,))] * 10 + [dma((Z,))] * 8 + [dma((Y, Z))] * 2
        + [dma((Z,))] * 4 + [dma((Z,))] * 8 + [dma((5,)), dma((9,)), dma((Z,))],
        compiler_params=pltpu.CompilerParams(
            collective_id=0, has_side_effects=True, vmem_limit_bytes=56 << 20),
        name="attention",
    )(block_perm, doc_query, query_len, var_bias, seg, doc_var.reshape(Z, 1, slot),
      jnp.asarray(np.cos(turns), F32), jnp.asarray(np.sin(turns), F32), jnp.asarray(frequency)[None, :],
      doc_x.reshape(Z, slot, features), w_query, w_key, w_value,
      norm_gain.reshape(1, features), readout.reshape(1, features),
      cache_k.reshape(Y, Z, piece, cols), cache_v.reshape(Y, Z, piece, cols), cache_var.reshape(Y, 1, slot), w_out)

    return update.reshape(tokens, cols), pooled[0, :2 * Z]


def solution(mesh):
    heads = mesh.shape["head"]
    cores = 2
    across = 4
    along = mesh.shape["blk"] // (across * cores)
    sizes = (heads, across, along, cores)
    split = Mesh(mesh.devices.reshape(sizes), ("x", "y", "z", "c"))
    return jax.shard_map(
        functools.partial(body, sizes),
        mesh=split,
        in_specs=(
            P(BLK, None), P(BLK), P(), P(BLK), P(), P(),
            P(BLK, "x"), P(BLK, "x"), P(BLK),
            P(None, "x"), P(None, "x"), P(None, "x"), P("x", None), P(None, "x"),
            P(), P(),
        ),
        out_specs=(P(BLK, "x"), P(BLK)),
        check_vma=False,
    )
```

```python
import functools

import jax
import jax.numpy as jnp
import numpy as np
from jax import lax
from jax.experimental import pallas as pl
from jax.experimental.pallas import tpu as pltpu
from jax.sharding import Mesh, PartitionSpec as P

DH = 64
F32 = jnp.float32
BF16 = jnp.bfloat16
NEG = -1e30
ANY = pl.ANY
BLK = ("y", "z", "c")


def remote(src, dst, send_sem, recv_sem, **device):
    return pltpu.make_async_remote_copy(
        src_ref=src,
        dst_ref=dst,
        send_sem=send_sem,
        recv_sem=recv_sem,
        device_id=device,
        device_id_type=pl.DeviceIdType.MESH,
    )


def each(count, first, step):
    def run(i, carry):
        step(i)
        return carry

    lax.fori_loop(first, count, run, 0)


def nth_near(i, Z):
    return lax.rem(jnp.where(i % 2 == 1, (i + 1) // 2, Z - i // 2), Z)


def attention_kernel(
    sizes, perm, dq, qlen, bias, seg_ref, var_ref, tcos_ref, tsin_ref, freq_ref, x_in, wq_in, wk_in, wv_in, gain_ref, read_ref, ck, cv, cvar, w_in, upd, means,
    attg, w_all, ytmp, yown, inv, xv, wq, wk, wv, order, abuf, bbuf, gbuf, va, vb, kv, qrot, qh, dv, hv, cosv, sinv, qtab, ktab,
    os, sts, kfs, qfs, ka, vx, qa, acc, mx, oh, sth, ro, rst,
    s_x, s_a, r_a, s_va, r_va, s_b, r_b, s_vb, r_vb, s_g, r_g, s_q, r_q, s_dv, r_dv,
    s_r, s_l, r_l, r_r, s_fr, s_fl, r_fl, r_fr, s_s, r_s,
    s_o, r_o, s_t, r_t, x_r, x_l, y_l, y_r, x_fr, x_fl, y_fl, y_fr, here, w_sem, out_sem,
):
    X, Y, Z, C = sizes
    x, y, z, c = lax.axis_index("x"), lax.axis_index("y"), lax.axis_index("z"), lax.axis_index("c")
    W = Y * C
    w = y * C + c
    bpq = W
    blk = (y * Z + z) * C + c
    slot, cols = qrot.shape[1], qrot.shape[2]
    heads = cols // DH
    pairs = cols // 128
    part_keys = bpq * slot
    barrier = pltpu.get_barrier_semaphore()

    loads = [pltpu.make_async_copy(s, d, s_x.at[n]) for n, (s, d) in
             enumerate(((x_in, xv), (wq_in, wq), (wk_in, wk), (wv_in, wv)))]
    for load in loads:
        load.start()

    def greet(**device):
        pl.semaphore_signal(barrier, inc=1, device_id=device, device_id_type=pl.DeviceIdType.MESH)

    each(W, 1, lambda i: greet(y=(w + i) % W // C, c=(w + i) % W % C))
    each(Z, 1, lambda i: greet(z=(z + i) % Z))
    for side in ((x + 1) % X, (x + X - 1) % X):
        greet(x=side)

    slot_query = [dq[blk * 2 * Z + 2 * j] for j in range(Z)]
    for query in range(Z):
        at = jnp.int32(0)
        for j in range(Z):
            at = jnp.where(slot_query[j] == query, j, at)
        order[query] = at
    lane2 = lax.broadcasted_iota(jnp.int32, (16, cols), 1)
    row2 = lax.broadcasted_iota(jnp.int32, (16, cols), 0)
    feat2 = lane2 % DH
    lane_head = 2 * (lane2 // 128) + (1 - lane2 % 128 // DH)
    delta = jnp.zeros((16, cols), F32)
    for h in range(heads):
        delta = jnp.where(lane_head == h, bias[0, h] - bias[1, h], delta)
    hi = delta.astype(BF16).astype(F32)
    mid = (delta - hi).astype(BF16).astype(F32)
    low = delta - hi - mid
    value = jnp.where(feat2 < 8, hi, jnp.where(feat2 < 16, mid, low))
    value = jnp.where((feat2 < 24) & (feat2 % 8 == row2), value, 0.0)
    qtab[...] = jnp.where((row2 >= 8) & (row2 < 11) & (feat2 == row2 + 16), 1.0, value).astype(BF16)
    lane1, row1 = lane2[:, :128], row2[:, :128]
    feat1 = lane1 % DH
    value = jnp.where((feat1 < 24) & (feat1 % 8 == row1), 1.0, 0.0)
    hit = (((row1 == 8) & (feat1 == 24)) | ((row1 == 9) & (feat1 == 26)) | ((row1 == 10) & (feat1 == 25)))
    ktab[...] = jnp.where(hit, NEG, value).astype(BF16)

    def features(rows, table):
        return lax.dot_general(rows.astype(BF16), table, (((0,), (0,)), ((), ())),
                               preferred_element_type=F32).astype(BF16)

    def marks(var, eight, seg):
        same = jnp.where((row1 < 8) & (var == row1), 1.0, 0.0)
        rows = jnp.where(row1 == 8, eight, same)
        if seg is not None:
            rows = jnp.where(((row1 == 9) & (seg == 0)) | ((row1 == 10) & (seg == 1)), 1.0, rows)
        return rows

    pl.semaphore_wait(barrier, W - 1 + Z - 1 + 2)

    for step in range(1, Y):
        to = (y + step) % Y
        for kind in range(C):
            remote((ck, cv)[kind].at[to], abuf.at[w], s_a.at[to * C + kind], r_a.at[w], y=to, c=kind).start()
            remote(cvar, va.at[w], s_va.at[to * C + kind], r_va.at[w], y=to, c=kind).start()
    for kind in range(C):
        src = (ck, cv)[kind].at[y]

        @pl.when(kind != c)
        def _():
            remote(src, abuf.at[w], s_a.at[y * C + kind], r_a.at[w], c=kind).start()
            remote(cvar, va.at[w], s_va.at[y * C + kind], r_va.at[w], c=kind).start()

        @pl.when(kind == c)
        def _():
            pltpu.make_async_copy(src, abuf.at[w], here.at[0]).start()

    own_var = pltpu.make_async_copy(cvar, va.at[w], here.at[1])
    own_var.start()

    xright, xleft, xfar = (x + 1) % X, (x + X - 1) % X, (x + 2) % X
    w_half = w_in.shape[0] // 2
    w_keep = pltpu.make_async_copy(w_in, w_all.at[x], w_sem.at[8])

    def w_whole(who, send, recv, dev):
        return remote(w_in, w_all.at[who], w_sem.at[send], w_sem.at[recv], x=dev)

    def w_pass(who, piece, send, recv, dev):
        part = w_all.at[who, pl.ds(piece * w_half, w_half)]
        return remote(part, part, w_sem.at[send], w_sem.at[recv], x=dev)

    w_keep.start()
    w_whole(x, 0, 2, xright).start()
    w_whole(x, 1, 3, xleft).start()

    lane = lax.broadcasted_iota(jnp.int32, (slot, cols), 1)
    half = lax.broadcasted_iota(jnp.int32, (slot, 128), 1)
    first_lanes = (lane % DH) < DH // 2
    first_half = (half % DH) < DH // 2
    ones_row = jnp.where(row1 == 10, 1.0, 0.0).astype(BF16)

    def segment(at):
        return seg_ref[at] - (blk * 2 * Z + 2 * at)

    def turn(a, query):
        other = jnp.where(first_lanes, pltpu.roll(a, cols - DH // 2, 1), pltpu.roll(a, DH // 2, 1))
        cosine = jnp.concatenate([cosv[query]] * pairs, axis=1)
        sine = jnp.concatenate([sinv[query]] * pairs, axis=1)
        return a * cosine + other * sine

    loads[0].wait()
    loads[1].wait()

    def project_q(query):
        at = order[query]
        seg = segment(at)
        length = qlen[query].astype(F32)
        count = jnp.sum(jnp.where(seg == 0, 1.0, 0.0), axis=1, keepdims=True)
        base0 = freq_ref[...] * length
        base1 = freq_ref[...] * (length - count)
        second = features(marks(var_ref[at], 1.0, seg), ones_row).astype(F32) > 0.5
        cos_a = jnp.where(second, jnp.cos(base1), jnp.cos(base0))
        sin_a = jnp.where(second, jnp.sin(base1), jnp.sin(base0))
        cosv[query] = cos_a * tcos_ref[...] - sin_a * tsin_ref[...]
        sine = sin_a * tcos_ref[...] + cos_a * tsin_ref[...]
        sinv[query] = jnp.where(first_half, -sine, sine)
        a = jnp.dot(xv[at], wq[...], preferred_element_type=F32)
        qrot[query] = (turn(a, query) * 0.125).astype(BF16)
        dv[query] = var_ref[at]

    each(Z, 0, project_q)

    def line_q(to, at):
        return remote(qrot.at[to], qh.at[at], s_q.at[to], r_q.at[at], z=to)

    def send_q(i):
        line_q((z + nth_near(i, Z)) % Z, z).start()

    each(Z // 2, 1, send_q)
    own_q = pltpu.make_async_copy(qrot.at[z], qh.at[z], here.at[4])
    own_q.start()

    pltpu.make_async_copy(ck.at[y], abuf.at[w], here.at[0]).wait()
    own_var.wait()

    def wait_a(i):
        src = (w + i) % W
        remote(abuf.at[src], abuf.at[src], s_a.at[src], r_a.at[src], y=src // C, c=src % C).wait_recv()
        remote(va.at[src], va.at[src], s_va.at[src], r_va.at[src], y=src // C, c=src % C).wait_recv()

    each(W, 1, wait_a)

    def line_b(to, at):
        return (remote(abuf.at[:, to], bbuf.at[pl.ds(at * W, W)], s_b.at[to], r_b.at[at], z=to),
                remote(va, vb.at[pl.ds(at * W, W)], s_vb.at[to], r_vb.at[at], z=to),
                remote(dv.at[to], hv.at[at], s_dv.at[to], r_dv.at[at], z=to))

    def send_b(i):
        for copy in line_b((z + nth_near(i, Z)) % Z, z):
            copy.start()

    each(Z, 1, send_b)
    own_b = pltpu.make_async_copy(abuf.at[:, z], bbuf.at[pl.ds(z * W, W)], here.at[2])
    own_vb = pltpu.make_async_copy(va, vb.at[pl.ds(z * W, W)], here.at[3])
    own_dv = pltpu.make_async_copy(dv.at[z], hv.at[z], here.at[1])
    own_b.start()
    own_vb.start()
    own_dv.start()

    loads[2].wait()
    loads[3].wait()
    wide8 = lax.broadcasted_iota(jnp.int32, (8, cols), 1)
    deep8 = lax.broadcasted_iota(jnp.int32, (8, cols), 0)
    widen = jnp.where(wide8 // DH == deep8, 1.0, 0.0).astype(F32)

    def own_part(query):
        at = order[query]
        xs = xv[at]
        k = turn(jnp.dot(xs, wk[...], preferred_element_type=F32), query).astype(BF16)
        v = jnp.dot(xs, wv[...], preferred_element_type=F32).astype(BF16)
        seg = segment(at)
        qf = features(marks(var_ref[at], 1.0, seg), qtab[...])
        kf = features(marks(var_ref[at], 0.0, seg), ktab[...])
        q = qrot[query]
        stats = jnp.zeros((slot, 128), F32)
        for pair in range(pairs):
            tile = slice(pair * 128, pair * 128 + 128)
            outs = []
            for odd in range(2):
                mine = (half >= DH) if odd else (half < DH)
                qs = jnp.where(mine, q[:, tile], qf[:, tile])
                ks = jnp.where(mine, k[:, tile], kf)
                s = lax.dot_general(qs, ks, (((1,), (1,)), ((), ())), preferred_element_type=F32)
                m = jnp.max(s, axis=1, keepdims=True)
                p = jnp.exp(s - m)
                l = jnp.sum(p, axis=1, keepdims=True)
                outs.append(jnp.dot(p.astype(BF16), v[:, tile], preferred_element_type=F32) / l)
                head = 2 * pair + odd
                stats = jnp.where(half == head, m, jnp.where(half == 4 + head, l, stats))
            os[query, :, tile] = jnp.where(half < DH, outs[0], outs[1])
        sts[query] = jnp.transpose(stats)[:8]

    early = Z // 2 - 1
    each(early, 0, own_part)

    def find(k):
        at = jnp.int32(0)
        for e in range(Z * W):
            at = jnp.where(perm[e] == k, e // C % Z * W + e // (Z * C) * C + e % C, at)
        inv[k] = at

    each(Z * W, 0, find)
    w_whole(xleft, 0, 2, xleft).wait_recv()
    w_pass(xleft, 0, 4, 6, xright).start()
    w_whole(xright, 1, 3, xright).wait_recv()
    w_pass(xright, 1, 5, 7, xleft).start()

    own_b.wait()
    own_vb.wait()
    own_dv.wait()

    def wait_b(i):
        src = (z + i) % Z
        part = bbuf.at[pl.ds(src * W, W)]
        remote(part, part, s_b.at[src], r_b.at[src], z=src).wait_recv()
        part = vb.at[pl.ds(src * W, W)]
        remote(part, part, s_vb.at[src], r_vb.at[src], z=src).wait_recv()
        remote(hv.at[src], hv.at[src], s_dv.at[src], r_dv.at[src], z=src).wait_recv()

    each(Z, 1, wait_b)

    def pick(i):
        gbuf[i] = bbuf[inv[i]]

    each(Z * bpq, 0, pick)

    def line_g(to, at):
        return remote(gbuf.at[pl.ds(to * bpq, bpq)], kv.at[c, y, :, at], s_g.at[to], r_g.at[at], z=to)

    own_g = pltpu.make_async_copy(gbuf.at[pl.ds(z * bpq, bpq)], kv.at[c, y, :, z], here.at[2])
    own_g.start()
    each(Z, 1, lambda i: line_g((z + nth_near(i, Z)) % Z, z).start())

    each(Z, Z // 2, send_q)
    own_g.wait()

    right, left, far, twin = (y + 1) % Y, (y + Y - 1) % Y, (y + 2) % Y, 1 - c

    def ring(kind, piece, at, send, recv, **device):
        part = kv.at[kind, piece, :, at]
        return remote(part, part, send.at[at], recv.at[at], **device)

    def to_twin(piece, at):
        return ring(c, piece, at, s_s.at[piece], r_s.at[piece], c=twin)

    def from_twin(piece, at):
        return ring(twin, piece, at, s_s.at[piece], r_s.at[piece], c=twin)

    to_right = lambda at: ring(c, y, at, s_r, r_l, y=right)
    to_left = lambda at: ring(c, y, at, s_l, r_r, y=left)
    from_left = lambda at: ring(c, left, at, s_r, r_l, y=left)
    from_right = lambda at: ring(c, right, at, s_l, r_r, y=right)
    pass_right = lambda at: ring(c, left, at, s_fr, r_fl, y=right)
    pass_left = lambda at: ring(c, right, at, s_fl, r_fr, y=left)
    far_left = lambda at: ring(c, far, at, s_fr, r_fl, y=left)
    far_right = lambda at: ring(c, far, at, s_fl, r_fr, y=right)

    def share(at):
        to_right(at).start()
        to_left(at).start()
        to_twin(y, at).start()

    def step1(i):
        at = (z + nth_near(i, Z)) % Z
        part = kv.at[c, y, :, at]
        remote(part, part, s_g.at[at], r_g.at[at], z=at).wait_recv()
        share(at)

    def step2(i):
        at = (z + nth_near(i, Z)) % Z
        from_left(at).wait_recv()

        @pl.when(at % 2 == 0)
        def _():
            pass_right(at).start()

        to_twin(left, at).start()
        from_right(at).wait_recv()

        @pl.when(at % 2 == 1)
        def _():
            pass_left(at).start()

        to_twin(right, at).start()

    def step3(i):
        at = (z + nth_near(i, Z)) % Z

        @pl.when(at % 2 == 0)
        def _():
            far_left(at).wait_recv()

        @pl.when(at % 2 == 1)
        def _():
            far_right(at).wait_recv()

        to_twin(far, at).start()

    share(z)
    my_len = qlen[z]

    def key_marks(i):
        piece, j = i // bpq, i % bpq
        var = vb[inv[z * bpq + j], piece]
        place = lane1 + (j * Y * slot + piece * slot)
        rows = pl.ds(pl.multiple_of(j * slot, slot), slot)
        kfs[piece, rows, :] = features(marks(var, jnp.where(place >= my_len, 1.0, 0.0), None), ktab[...])

    def query_marks(at):
        qfs[at] = features(marks(hv[at], 1.0, None), qtab[...])

    def steps12(i):
        step1(i)

        @pl.when(i < 3)
        def _():
            each(2 * bpq * i, 2 * bpq * (i - 1), key_marks)
            each(Z // 2 * i, Z // 2 * (i - 1), query_marks)

        @pl.when(i > 2)
        def _():
            own_part(early + i - 3)

        @pl.when(i > 2)
        def _():
            step2(i - 3)

    each(Z, 1, steps12)

    def build(n, piece):
        def one(j):
            k = kv[0, piece, j].reshape(slot, cols)
            v = kv[1, piece, j].reshape(slot, cols)
            rows = pl.ds(pl.multiple_of(j * slot, slot), slot)
            kf = kfs[piece, rows, :]
            for pair in range(pairs):
                tile = slice(pair * 128, pair * 128 + 128)
                for odd in range(2):
                    mine = (half >= DH) if odd else (half < DH)
                    ka[2 * pair + odd, n, rows, :] = jnp.where(mine, k[:, tile], kf)
                    vx[2 * pair + odd, n, rows, :] = jnp.where(mine, v[:, tile], jnp.ones_like(kf))

        each(bpq, 0, one)

    def take_q(i):
        at = (z + nth_near(i, Z)) % Z
        qf = qfs[at]
        q = qh[at]
        rows = pl.ds(pl.multiple_of(i * slot, slot), slot)
        for pair in range(pairs):
            tile = slice(pair * 128, pair * 128 + 128)
            for odd in range(2):
                mine = (half >= DH) if odd else (half < DH)
                qa[2 * pair + odd, rows, :] = jnp.where(mine, q[:, tile], qf[:, tile])

    def wait_q(i):
        at = (z + nth_near(i, Z)) % Z

        @pl.when(i == 0)
        def _():
            own_q.wait()

        @pl.when(i > 0)
        def _():
            line_q(at, at).wait_recv()

        take_q(i)

    side = Z // 2 * slot

    def attend(n, group):
        rows = pl.ds(pl.multiple_of(group * side, side), side)

        def score(h):
            return lax.dot_general(qa[h, rows, :], ka[h, n], (((1,), (1,)), ((), ())), preferred_element_type=F32)

        def weigh(h, s):
            old = mx[h, rows, :][:, :1]
            m = jnp.maximum(old, jnp.max(s, axis=1, keepdims=True))
            o = jnp.dot(jnp.exp(s - m).astype(BF16), vx[h, n], preferred_element_type=F32)
            acc[h, rows, :] = acc[h, rows, :] * jnp.exp(old - m) + o
            mx[h, rows, :] = jnp.broadcast_to(m, (side, 128))

        s = score(0)
        for h in range(heads):
            later = score(h + 1) if h + 1 < heads else None
            weigh(h, s)
            s = later

    def twins(piece):
        each(Z, 0, lambda at: from_twin(piece, at).wait_recv())

    def line_o(to, at):
        return (remote(oh.at[to], ro.at[at], s_o.at[to], r_o.at[at], z=to),
                remote(sth.at[to], rst.at[at], s_t.at[to], r_t.at[at], z=to))

    def settle(i):
        at = (z + nth_near(i, Z)) % Z
        rows = pl.ds(pl.multiple_of(i * slot, slot), slot)
        stats = jnp.zeros((slot, 128), F32)
        for pair in range(pairs):
            outs = []
            for odd in range(2):
                mine = (half >= DH) if odd else (half < DH)
                head = 2 * pair + odd
                total = acc[head, rows, :]
                turned = pltpu.roll(total, DH, 1)
                l = jnp.where(mine, turned, total)
                outs.append(total / l)
                stats = jnp.where(half == head, mx[head, rows, :], jnp.where(half == 4 + head, l, stats))
            oh[at, :, pair * 128:pair * 128 + 128] = jnp.where(half < DH, outs[0], outs[1]).astype(BF16)
        sth[at] = jnp.transpose(stats)[:8]

    own_o = pltpu.make_async_copy(oh.at[z], ro.at[z], here.at[2])
    own_t = pltpu.make_async_copy(sth.at[z], rst.at[z], here.at[3])

    def settle_send(i):
        settle(i)
        at = (z + nth_near(i, Z)) % Z

        @pl.when(i == 0)
        def _():
            own_o.start()
            own_t.start()

        @pl.when(i > 0)
        def _():
            for copy in line_o(at, z):
                copy.start()

    mid_row = slot // 2

    def xring(who, at, send, recv, dev):
        part = attg.at[who, at]
        return remote(part, part, send.at[at], recv.at[at], x=dev)

    def xpass(who, at, piece, send, recv, dev):
        part = attg.at[who, at, pl.ds(piece * mid_row, mid_row)]
        return remote(part, part, send.at[at], recv.at[at], x=dev)

    xto_right = lambda at: xring(x, at, x_r, y_l, xright)
    xto_left = lambda at: xring(x, at, x_l, y_r, xleft)
    xfrom_left = lambda at: xring(xleft, at, x_r, y_l, xleft)
    xfrom_right = lambda at: xring(xright, at, x_l, y_r, xright)
    xpass_right = lambda at: xpass(xleft, at, 0, x_fr, y_fl, xright)
    xpass_left = lambda at: xpass(xright, at, 1, x_fl, y_fr, xleft)
    xfar_left = lambda at: xpass(xfar, at, 0, x_fr, y_fl, xleft)
    xfar_right = lambda at: xpass(xfar, at, 1, x_fl, y_fr, xright)

    def join(at):
        far_m, far_l = rst[at][0:4], rst[at][4:8]
        own_m, own_l = sts[at][0:4], sts[at][4:8]
        m = jnp.maximum(far_m, own_m)
        a = far_l * jnp.exp(far_m - m)
        b = own_l * jnp.exp(own_m - m)
        share = a / (a + b)
        wide = lax.dot_general(
            jnp.concatenate([share, jnp.zeros_like(share)], axis=0), widen, (((0,), (0,)), ((), ())),
            preferred_element_type=F32, precision=lax.Precision.HIGHEST)
        value = os[at] + wide * (ro[at].astype(F32) - os[at])
        attg[x, at] = value.astype(BF16)
        xto_right(at).start()
        xto_left(at).start()

    def home(i):
        return (z + Z - nth_near(i, Z)) % Z

    def arrive(i):
        at = home(i)

        @pl.when(i == 0)
        def _():
            own_o.wait()
            own_t.wait()

        @pl.when(i > 0)
        def _():
            for copy in line_o(at, at):
                copy.wait_recv()

        join(at)

    def forward(i):
        at = home(i)
        xfrom_left(at).wait_recv()
        xpass_right(at).start()
        xfrom_right(at).wait_recv()
        xpass_left(at).start()

    hz = Z // 2

    def main(t):
        group, n = t // Y, t % Y
        piece = jnp.where(n == 0, y, jnp.where(n == 1, left, jnp.where(n == 2, right, far)))

        @pl.when(n == 0)
        def _():
            rows = pl.ds(pl.multiple_of(group * side, side), side)
            for h in range(heads):
                acc[h, rows, :] = jnp.zeros((side, 128), F32)
                mx[h, rows, :] = jnp.full((side, 128), -3e38, F32)
            each(hz, 0, lambda i: wait_q(group * hz + i))

        @pl.when(t < Y)
        def _():
            twins(piece)
            build(n, piece)

        @pl.when(t == 0)
        def _():
            each(Z, Z - 3, step2)

        attend(n, group)

        @pl.when(t == 1)
        def _():
            each(Z, 0, step3)

        @pl.when(t == Y - 1)
        def _():
            each(hz, 0, settle_send)

        @pl.when(t == Y)
        def _():
            arrive(0)

        @pl.when(t == Y + 1)
        def _():
            each(hz, 1, arrive)

        @pl.when(t == Y + 2)
        def _():
            forward(0)

    each(2 * Y, 0, main)
    each(Z, hz, settle_send)
    each(hz, 1, forward)

    w_keep.wait()
    w_pass(xfar, 0, 4, 6, xleft).wait_recv()
    w_pass(xfar, 1, 5, 7, xright).wait_recv()
    width = xv.shape[2]
    row8 = lax.broadcasted_iota(jnp.int32, (8, slot), 0)

    give = lambda at: pltpu.make_async_copy(yown.at[at], upd.at[at], out_sem.at[at])

    def collect(i):
        at = home(i)
        xfar_left(at).wait_recv()
        xfar_right(at).wait_recv()
        place = order[at]
        rows = jnp.concatenate([attg[p, at] for p in range(X)], axis=1)
        value = jnp.dot(rows, w_all[...].reshape(X * cols, width), preferred_element_type=F32)
        ytmp[...] = value
        yown[at] = ytmp[:, pl.ds(pl.multiple_of(x * cols, cols), cols)]
        give(at).start()
        hidden = xv[place].astype(F32) + value
        square = jnp.sum(hidden * hidden, axis=1, keepdims=True)
        weighted = jnp.sum(hidden * (gain_ref[...] * read_ref[...]), axis=1, keepdims=True)
        score = weighted * lax.rsqrt(square / width + 1e-06)
        member = jnp.where((row8 < 2) & (segment(place) == row8), 1.0, 0.0)
        sums = jnp.dot(member, jnp.broadcast_to(score, (slot, 128)),
                       preferred_element_type=F32, precision=lax.Precision.HIGHEST)
        means[at] = sums / jnp.maximum(jnp.sum(member, axis=1, keepdims=True), 1.0)

    def late(i):
        collect(i - hz)
        arrive(i)

        @pl.when(i > Z // 2)
        def _():
            forward(i - 1)

    each(Z, hz, late)
    forward(Z - 1)
    each(Z, hz, collect)

    def finish(at):
        for copy in (xto_right(at), xto_left(at), xpass_right(at), xpass_left(at), to_right(at), to_left(at)):
            copy.wait_send()

        @pl.when(at % 2 == 0)
        def _():
            pass_right(at).wait_send()

        @pl.when(at % 2 == 1)
        def _():
            pass_left(at).wait_send()

        for piece in range(Y):
            to_twin(piece, at).wait_send()

    each(Z, 0, finish)
    for copy in (w_whole(x, 0, 2, xright), w_whole(x, 1, 3, xleft),
                 w_pass(xleft, 0, 4, 6, xright), w_pass(xright, 1, 5, 7, xleft)):
        copy.wait_send()

    def end_line(i):
        at = (z + i) % Z
        for copy in line_b(at, at) + line_o(at, at) + (line_q(at, at), line_g(at, at)):
            copy.wait_send()

    each(Z, 1, end_line)

    def end_cluster(i):
        to = (w + i) % W
        remote(abuf.at[to], abuf.at[to], s_a.at[to], r_a.at[to], y=to // C, c=to % C).wait_send()
        remote(cvar, va.at[to], s_va.at[to], r_va.at[to], y=to // C, c=to % C).wait_send()

    each(W, 1, end_cluster)
    each(Z, 0, lambda at: give(at).wait())


def order_kernel(sizes, dq, by_query, means, upd, pool, sem):
    X, Y, Z, C = sizes
    blk = (lax.axis_index("y") * Z + lax.axis_index("z")) * C + lax.axis_index("c")
    copies = []
    for j in range(Z):
        query = dq[blk * 2 * Z + 2 * j]
        copies.append(pltpu.make_async_copy(by_query.at[query], upd.at[j], sem.at[j]))
        copies[j].start()
    for j in range(Z):
        mean = means[dq[blk * 2 * Z + 2 * j]]
        for k in range(2):
            pool[2 * j + k] = mean[k, 0]
    for copy in copies:
        copy.wait()


def body(sizes, doc_x, doc_seg, doc_query, doc_var, query_len, block_perm, cache_k, cache_v, cache_var,
         w_query, w_key, w_value, w_out, var_bias, norm_gain, readout):
    X, Y, Z, C = sizes
    W = Y * C
    tokens, cols = doc_x.shape[0], w_query.shape[1]
    features = doc_x.shape[1]
    heads = cols // DH
    slot = tokens // Z
    crows = cache_k.shape[0]
    blocks = Y * Z * C
    bpq = blocks // Z
    piece = crows // (Y * Z)
    part_keys = bpq * slot
    i32 = jnp.int32
    dma = pltpu.SemaphoreType.DMA

    half_size = DH // 2
    frequency = 10000.0 ** (-np.arange(half_size) / half_size)
    frequency = np.tile(frequency.astype(np.float32), 128 // half_size)
    turns = np.arange(slot)[:, None] * frequency.astype(np.float64)[None, :]
    seg = doc_seg.reshape(Z, 1, slot)

    vm = lambda *shape: pltpu.VMEM(shape, BF16)
    vf = lambda *shape: pltpu.VMEM(shape, F32)
    vi = lambda *shape: pltpu.VMEM(shape, i32)
    smem = pl.BlockSpec(memory_space=pltpu.SMEM)
    vmem = pl.BlockSpec(memory_space=pltpu.VMEM)
    hbm = pl.BlockSpec(memory_space=ANY)
    by_query, means = pl.pallas_call(
        functools.partial(attention_kernel, sizes),
        in_specs=[smem] * 4 + [vmem] * 5 + [hbm] * 4 + [vmem] * 2 + [hbm] * 4,
        out_specs=[hbm, vmem],
        out_shape=[
            jax.ShapeDtypeStruct((Z, slot, cols), F32),
            jax.ShapeDtypeStruct((Z, 8, 128), F32),
        ],
        scratch_shapes=[
            vm(X, Z, slot, cols), vm(X, cols, features), vf(slot, features), vf(Z, slot, cols),
            pltpu.SMEM((blocks,), i32), vm(Z, slot, features), vm(features, cols), vm(features, cols), vm(features, cols),
            pltpu.SMEM((Z,), i32),
            vm(W, Z, piece, cols), vm(Z * W, piece, cols), vm(Z * bpq, piece, cols),
            vi(W, Y, 1, slot), vi(Z * W, Y, 1, slot),
            vm(C, Y, bpq, Z, piece, cols),
            vm(Z, slot, cols), vm(Z, slot, cols), vi(Z, 1, slot), vi(Z, 1, slot),
            vf(Z, slot, 128), vf(Z, slot, 128), vm(16, cols), vm(16, 128),
            vf(Z, slot, cols), vf(Z, 8, slot), vm(Y, part_keys, 128), vm(Z, slot, cols),
            vm(heads, Y, part_keys, 128), vm(heads, Y, part_keys, 128), vm(heads, tokens, 128),
            vf(heads, tokens, 128), vf(heads, tokens, 128),
            vm(Z, slot, cols), vf(Z, 8, slot), vm(Z, slot, cols), vf(Z, 8, slot),
            dma((4,)),
        ] + [dma((W,))] * 4 + [dma((Z,))] * 10 + [dma((Z,))] * 8 + [dma((Y, Z))] * 2
        + [dma((Z,))] * 4 + [dma((Z,))] * 8 + [dma((5,)), dma((9,)), dma((Z,))],
        compiler_params=pltpu.CompilerParams(
            collective_id=0, has_side_effects=True, vmem_limit_bytes=56 << 20),
        name="attention",
    )(block_perm, doc_query, query_len, var_bias, seg, doc_var.reshape(Z, 1, slot),
      jnp.asarray(np.cos(turns), F32), jnp.asarray(np.sin(turns), F32), jnp.asarray(frequency)[None, :],
      doc_x.reshape(Z, slot, features), w_query, w_key, w_value,
      norm_gain.reshape(1, features), readout.reshape(1, features),
      cache_k.reshape(Y, Z, piece, cols), cache_v.reshape(Y, Z, piece, cols), cache_var.reshape(Y, 1, slot), w_out)

    update, pooled = pl.pallas_call(
        functools.partial(order_kernel, sizes),
        in_specs=[smem, hbm, vmem],
        out_specs=[hbm, smem],
        out_shape=[
            jax.ShapeDtypeStruct((Z, slot, cols), F32),
            jax.ShapeDtypeStruct((2 * Z,), F32),
        ],
        scratch_shapes=[dma((Z,))],
        compiler_params=pltpu.CompilerParams(vmem_limit_bytes=60 << 20),
        name="slot_order",
    )(doc_query, by_query, means)
    return update.reshape(tokens, cols), pooled


def solution(mesh):
    heads = mesh.shape["head"]
    cores = 2
    across = 4
    along = mesh.shape["blk"] // (across * cores)
    sizes = (heads, across, along, cores)
    split = Mesh(mesh.devices.reshape(sizes), ("x", "y", "z", "c"))
    return jax.shard_map(
        functools.partial(body, sizes),
        mesh=split,
        in_specs=(
            P(BLK, None), P(BLK), P(), P(BLK), P(), P(),
            P(BLK, "x"), P(BLK, "x"), P(BLK),
            P(None, "x"), P(None, "x"), P(None, "x"), P("x", None), P(None, "x"),
            P(), P(),
        ),
        out_specs=(P(BLK, "x"), P(BLK)),
        check_vma=False,
    )
```

```python
import functools

import jax
import jax.numpy as jnp
import numpy as np
from jax import lax
from jax.experimental import pallas as pl
from jax.experimental.pallas import tpu as pltpu
from jax.sharding import Mesh, PartitionSpec as P

DH = 64
F32 = jnp.float32
BF16 = jnp.bfloat16
NEG = -1e30
ANY = pl.ANY
BLK = ("y", "z", "c")


def remote(src, dst, send_sem, recv_sem, **device):
    return pltpu.make_async_remote_copy(
        src_ref=src,
        dst_ref=dst,
        send_sem=send_sem,
        recv_sem=recv_sem,
        device_id=device,
        device_id_type=pl.DeviceIdType.MESH,
    )


def each(count, first, step):
    def run(i, carry):
        step(i)
        return carry

    lax.fori_loop(first, count, run, 0)


def nth_near(i, Z):
    return lax.rem(jnp.where(i % 2 == 1, (i + 1) // 2, Z - i // 2), Z)


def attention_kernel(
    sizes, perm, dq, qlen, bias, seg_ref, var_ref, tcos_ref, tsin_ref, freq_ref, x_in, wq_in, wk_in, wv_in, gain_ref, read_ref, ck, cv, cvar, w_in, upd, means,
    attg, w_all, ytmp, yown, inv, xv, wq, wk, wv, order, abuf, bbuf, gbuf, va, vb, kv, qrot, qh, dv, hv, cosv, sinv, qtab, ktab,
    os, sts, kfs, qfs, ka, vx, qa, acc, mx, oh, sth, ro, rst,
    s_x, s_a, r_a, s_va, r_va, s_b, r_b, s_vb, r_vb, s_g, r_g, s_q, r_q, s_dv, r_dv,
    s_r, s_l, r_l, r_r, s_fr, s_fl, r_fl, r_fr, s_s, r_s,
    s_o, r_o, s_t, r_t, x_r, x_l, y_l, y_r, x_fr, x_fl, y_fl, y_fr, here, w_sem, out_sem,
):
    X, Y, Z, C = sizes
    x, y, z, c = lax.axis_index("x"), lax.axis_index("y"), lax.axis_index("z"), lax.axis_index("c")
    W = Y * C
    w = y * C + c
    bpq = W
    blk = (y * Z + z) * C + c
    slot, cols = qrot.shape[1], qrot.shape[2]
    heads = cols // DH
    pairs = cols // 128
    part_keys = bpq * slot
    barrier = pltpu.get_barrier_semaphore()

    loads = [pltpu.make_async_copy(s, d, s_x.at[n]) for n, (s, d) in
             enumerate(((x_in, xv), (wq_in, wq), (wk_in, wk), (wv_in, wv)))]
    for load in loads:
        load.start()

    def greet(**device):
        pl.semaphore_signal(barrier, inc=1, device_id=device, device_id_type=pl.DeviceIdType.MESH)

    each(W, 1, lambda i: greet(y=(w + i) % W // C, c=(w + i) % W % C))
    each(Z, 1, lambda i: greet(z=(z + i) % Z))
    for side in ((x + 1) % X, (x + X - 1) % X):
        greet(x=side)

    slot_query = [dq[blk * 2 * Z + 2 * j] for j in range(Z)]
    for query in range(Z):
        at = jnp.int32(0)
        for j in range(Z):
            at = jnp.where(slot_query[j] == query, j, at)
        order[query] = at
    lane2 = lax.broadcasted_iota(jnp.int32, (16, cols), 1)
    row2 = lax.broadcasted_iota(jnp.int32, (16, cols), 0)
    feat2 = lane2 % DH
    lane_head = 2 * (lane2 // 128) + (1 - lane2 % 128 // DH)
    delta = jnp.zeros((16, cols), F32)
    for h in range(heads):
        delta = jnp.where(lane_head == h, bias[0, h] - bias[1, h], delta)
    hi = delta.astype(BF16).astype(F32)
    mid = (delta - hi).astype(BF16).astype(F32)
    low = delta - hi - mid
    value = jnp.where(feat2 < 8, hi, jnp.where(feat2 < 16, mid, low))
    value = jnp.where((feat2 < 24) & (feat2 % 8 == row2), value, 0.0)
    qtab[...] = jnp.where((row2 >= 8) & (row2 < 11) & (feat2 == row2 + 16), 1.0, value).astype(BF16)
    lane1, row1 = lane2[:, :128], row2[:, :128]
    feat1 = lane1 % DH
    value = jnp.where((feat1 < 24) & (feat1 % 8 == row1), 1.0, 0.0)
    hit = (((row1 == 8) & (feat1 == 24)) | ((row1 == 9) & (feat1 == 26)) | ((row1 == 10) & (feat1 == 25)))
    ktab[...] = jnp.where(hit, NEG, value).astype(BF16)

    def features(rows, table):
        return lax.dot_general(rows.astype(BF16), table, (((0,), (0,)), ((), ())),
                               preferred_element_type=F32).astype(BF16)

    def marks(var, eight, seg):
        same = jnp.where((row1 < 8) & (var == row1), 1.0, 0.0)
        rows = jnp.where(row1 == 8, eight, same)
        if seg is not None:
            rows = jnp.where(((row1 == 9) & (seg == 0)) | ((row1 == 10) & (seg == 1)), 1.0, rows)
        return rows

    pl.semaphore_wait(barrier, W - 1 + Z - 1 + 2)

    for step in range(1, Y):
        to = (y + step) % Y
        for kind in range(C):
            remote((ck, cv)[kind].at[to], abuf.at[w], s_a.at[to * C + kind], r_a.at[w], y=to, c=kind).start()
            remote(cvar, va.at[w], s_va.at[to * C + kind], r_va.at[w], y=to, c=kind).start()
    for kind in range(C):
        src = (ck, cv)[kind].at[y]

        @pl.when(kind != c)
        def _():
            remote(src, abuf.at[w], s_a.at[y * C + kind], r_a.at[w], c=kind).start()
            remote(cvar, va.at[w], s_va.at[y * C + kind], r_va.at[w], c=kind).start()

        @pl.when(kind == c)
        def _():
            pltpu.make_async_copy(src, abuf.at[w], here.at[0]).start()

    own_var = pltpu.make_async_copy(cvar, va.at[w], here.at[1])
    own_var.start()

    xright, xleft, xfar = (x + 1) % X, (x + X - 1) % X, (x + 2) % X
    w_half = w_in.shape[0] // 2
    w_keep = pltpu.make_async_copy(w_in, w_all.at[x], w_sem.at[8])

    def w_whole(who, send, recv, dev):
        return remote(w_in, w_all.at[who], w_sem.at[send], w_sem.at[recv], x=dev)

    def w_pass(who, piece, send, recv, dev):
        part = w_all.at[who, pl.ds(piece * w_half, w_half)]
        return remote(part, part, w_sem.at[send], w_sem.at[recv], x=dev)

    w_keep.start()
    w_whole(x, 0, 2, xright).start()
    w_whole(x, 1, 3, xleft).start()

    lane = lax.broadcasted_iota(jnp.int32, (slot, cols), 1)
    half = lax.broadcasted_iota(jnp.int32, (slot, 128), 1)
    first_lanes = (lane % DH) < DH // 2
    first_half = (half % DH) < DH // 2
    ones_row = jnp.where(row1 == 10, 1.0, 0.0).astype(BF16)

    def segment(at):
        return seg_ref[at] - (blk * 2 * Z + 2 * at)

    def turn(a, query):
        other = jnp.where(first_lanes, pltpu.roll(a, cols - DH // 2, 1), pltpu.roll(a, DH // 2, 1))
        cosine = jnp.concatenate([cosv[query]] * pairs, axis=1)
        sine = jnp.concatenate([sinv[query]] * pairs, axis=1)
        return a * cosine + other * sine

    loads[0].wait()
    loads[1].wait()

    def project_q(query):
        at = order[query]
        seg = segment(at)
        length = qlen[query].astype(F32)
        count = jnp.sum(jnp.where(seg == 0, 1.0, 0.0), axis=1, keepdims=True)
        base0 = freq_ref[...] * length
        base1 = freq_ref[...] * (length - count)
        second = features(marks(var_ref[at], 1.0, seg), ones_row).astype(F32) > 0.5
        cos_a = jnp.where(second, jnp.cos(base1), jnp.cos(base0))
        sin_a = jnp.where(second, jnp.sin(base1), jnp.sin(base0))
        cosv[query] = cos_a * tcos_ref[...] - sin_a * tsin_ref[...]
        sine = sin_a * tcos_ref[...] + cos_a * tsin_ref[...]
        sinv[query] = jnp.where(first_half, -sine, sine)
        a = jnp.dot(xv[at], wq[...], preferred_element_type=F32)
        qrot[query] = (turn(a, query) * 0.125).astype(BF16)
        dv[query] = var_ref[at]

    each(Z, 0, project_q)

    def line_q(to, at):
        return remote(qrot.at[to], qh.at[at], s_q.at[to], r_q.at[at], z=to)

    def send_q(i):
        line_q((z + nth_near(i, Z)) % Z, z).start()

    each(Z // 2, 1, send_q)
    own_q = pltpu.make_async_copy(qrot.at[z], qh.at[z], here.at[4])
    own_q.start()

    pltpu.make_async_copy(ck.at[y], abuf.at[w], here.at[0]).wait()
    own_var.wait()

    def wait_a(i):
        src = (w + i) % W
        remote(abuf.at[src], abuf.at[src], s_a.at[src], r_a.at[src], y=src // C, c=src % C).wait_recv()
        remote(va.at[src], va.at[src], s_va.at[src], r_va.at[src], y=src // C, c=src % C).wait_recv()

    each(W, 1, wait_a)

    def line_b(to, at):
        return (remote(abuf.at[:, to], bbuf.at[pl.ds(at * W, W)], s_b.at[to], r_b.at[at], z=to),
                remote(va, vb.at[pl.ds(at * W, W)], s_vb.at[to], r_vb.at[at], z=to),
                remote(dv.at[to], hv.at[at], s_dv.at[to], r_dv.at[at], z=to))

    def send_b(i):
        for copy in line_b((z + nth_near(i, Z)) % Z, z):
            copy.start()

    each(Z, 1, send_b)
    own_b = pltpu.make_async_copy(abuf.at[:, z], bbuf.at[pl.ds(z * W, W)], here.at[2])
    own_vb = pltpu.make_async_copy(va, vb.at[pl.ds(z * W, W)], here.at[3])
    own_dv = pltpu.make_async_copy(dv.at[z], hv.at[z], here.at[1])
    own_b.start()
    own_vb.start()
    own_dv.start()

    loads[2].wait()
    loads[3].wait()
    wide8 = lax.broadcasted_iota(jnp.int32, (8, cols), 1)
    deep8 = lax.broadcasted_iota(jnp.int32, (8, cols), 0)
    widen = jnp.where(wide8 // DH == deep8, 1.0, 0.0).astype(F32)

    def own_part(query):
        at = order[query]
        xs = xv[at]
        k = turn(jnp.dot(xs, wk[...], preferred_element_type=F32), query).astype(BF16)
        v = jnp.dot(xs, wv[...], preferred_element_type=F32).astype(BF16)
        seg = segment(at)
        qf = features(marks(var_ref[at], 1.0, seg), qtab[...])
        kf = features(marks(var_ref[at], 0.0, seg), ktab[...])
        q = qrot[query]
        stats = jnp.zeros((slot, 128), F32)
        for pair in range(pairs):
            tile = slice(pair * 128, pair * 128 + 128)
            outs = []
            for odd in range(2):
                mine = (half >= DH) if odd else (half < DH)
                qs = jnp.where(mine, q[:, tile], qf[:, tile])
                ks = jnp.where(mine, k[:, tile], kf)
                s = lax.dot_general(qs, ks, (((1,), (1,)), ((), ())), preferred_element_type=F32)
                m = jnp.max(s, axis=1, keepdims=True)
                p = jnp.exp(s - m)
                l = jnp.sum(p, axis=1, keepdims=True)
                outs.append(jnp.dot(p.astype(BF16), v[:, tile], preferred_element_type=F32) / l)
                head = 2 * pair + odd
                stats = jnp.where(half == head, m, jnp.where(half == 4 + head, l, stats))
            os[query, :, tile] = jnp.where(half < DH, outs[0], outs[1])
        sts[query] = jnp.transpose(stats)[:8]

    early = Z // 2 - 1
    each(early, 0, own_part)

    def find(k):
        at = jnp.int32(0)
        for e in range(Z * W):
            at = jnp.where(perm[e] == k, e // C % Z * W + e // (Z * C) * C + e % C, at)
        inv[k] = at

    each(Z * W, 0, find)
    w_whole(xleft, 0, 2, xleft).wait_recv()
    w_pass(xleft, 0, 4, 6, xright).start()
    w_whole(xright, 1, 3, xright).wait_recv()
    w_pass(xright, 1, 5, 7, xleft).start()

    own_b.wait()
    own_vb.wait()
    own_dv.wait()

    def wait_b(i):
        src = (z + i) % Z
        part = bbuf.at[pl.ds(src * W, W)]
        remote(part, part, s_b.at[src], r_b.at[src], z=src).wait_recv()
        part = vb.at[pl.ds(src * W, W)]
        remote(part, part, s_vb.at[src], r_vb.at[src], z=src).wait_recv()
        remote(hv.at[src], hv.at[src], s_dv.at[src], r_dv.at[src], z=src).wait_recv()

    each(Z, 1, wait_b)

    def pick(i):
        gbuf[i] = bbuf[inv[i]]

    each(Z * bpq, 0, pick)

    def line_g(to, at):
        return remote(gbuf.at[pl.ds(to * bpq, bpq)], kv.at[c, y, :, at], s_g.at[to], r_g.at[at], z=to)

    own_g = pltpu.make_async_copy(gbuf.at[pl.ds(z * bpq, bpq)], kv.at[c, y, :, z], here.at[2])
    own_g.start()
    each(Z, 1, lambda i: line_g((z + nth_near(i, Z)) % Z, z).start())

    each(Z, Z // 2, send_q)
    own_g.wait()

    right, left, far, twin = (y + 1) % Y, (y + Y - 1) % Y, (y + 2) % Y, 1 - c

    def ring(kind, piece, at, send, recv, **device):
        part = kv.at[kind, piece, :, at]
        return remote(part, part, send.at[at], recv.at[at], **device)

    def to_twin(piece, at):
        return ring(c, piece, at, s_s.at[piece], r_s.at[piece], c=twin)

    def from_twin(piece, at):
        return ring(twin, piece, at, s_s.at[piece], r_s.at[piece], c=twin)

    to_right = lambda at: ring(c, y, at, s_r, r_l, y=right)
    to_left = lambda at: ring(c, y, at, s_l, r_r, y=left)
    from_left = lambda at: ring(c, left, at, s_r, r_l, y=left)
    from_right = lambda at: ring(c, right, at, s_l, r_r, y=right)
    pass_right = lambda at: ring(c, left, at, s_fr, r_fl, y=right)
    pass_left = lambda at: ring(c, right, at, s_fl, r_fr, y=left)
    far_left = lambda at: ring(c, far, at, s_fr, r_fl, y=left)
    far_right = lambda at: ring(c, far, at, s_fl, r_fr, y=right)

    def share(at):
        to_right(at).start()
        to_left(at).start()
        to_twin(y, at).start()

    def step1(i):
        at = (z + nth_near(i, Z)) % Z
        part = kv.at[c, y, :, at]
        remote(part, part, s_g.at[at], r_g.at[at], z=at).wait_recv()
        share(at)

    def step2(i):
        at = (z + nth_near(i, Z)) % Z
        from_left(at).wait_recv()

        @pl.when(at % 2 == 0)
        def _():
            pass_right(at).start()

        to_twin(left, at).start()
        from_right(at).wait_recv()

        @pl.when(at % 2 == 1)
        def _():
            pass_left(at).start()

        to_twin(right, at).start()

    def step3(i):
        at = (z + nth_near(i, Z)) % Z

        @pl.when(at % 2 == 0)
        def _():
            far_left(at).wait_recv()

        @pl.when(at % 2 == 1)
        def _():
            far_right(at).wait_recv()

        to_twin(far, at).start()

    share(z)
    my_len = qlen[z]

    def key_marks(i):
        piece, j = i // bpq, i % bpq
        var = vb[inv[z * bpq + j], piece]
        place = lane1 + (j * Y * slot + piece * slot)
        rows = pl.ds(pl.multiple_of(j * slot, slot), slot)
        kfs[piece, rows, :] = features(marks(var, jnp.where(place >= my_len, 1.0, 0.0), None), ktab[...])

    def query_marks(at):
        qfs[at] = features(marks(hv[at], 1.0, None), qtab[...])

    def steps12(i):
        step1(i)

        @pl.when(i < 3)
        def _():
            each(2 * bpq * i, 2 * bpq * (i - 1), key_marks)
            each(Z // 2 * i, Z // 2 * (i - 1), query_marks)

        @pl.when(i > 2)
        def _():
            own_part(early + i - 3)

        @pl.when(i > 2)
        def _():
            step2(i - 3)

    each(Z, 1, steps12)

    def build(n, piece):
        def one(j):
            k = kv[0, piece, j].reshape(slot, cols)
            v = kv[1, piece, j].reshape(slot, cols)
            rows = pl.ds(pl.multiple_of(j * slot, slot), slot)
            kf = kfs[piece, rows, :]
            for pair in range(pairs):
                tile = slice(pair * 128, pair * 128 + 128)
                for odd in range(2):
                    mine = (half >= DH) if odd else (half < DH)
                    ka[2 * pair + odd, n, rows, :] = jnp.where(mine, k[:, tile], kf)
                    vx[2 * pair + odd, n, rows, :] = jnp.where(mine, v[:, tile], jnp.ones_like(kf))

        each(bpq, 0, one)

    def take_q(i):
        at = (z + nth_near(i, Z)) % Z
        qf = qfs[at]
        q = qh[at]
        rows = pl.ds(pl.multiple_of(i * slot, slot), slot)
        for pair in range(pairs):
            tile = slice(pair * 128, pair * 128 + 128)
            for odd in range(2):
                mine = (half >= DH) if odd else (half < DH)
                qa[2 * pair + odd, rows, :] = jnp.where(mine, q[:, tile], qf[:, tile])

    def wait_q(i):
        at = (z + nth_near(i, Z)) % Z

        @pl.when(i == 0)
        def _():
            own_q.wait()

        @pl.when(i > 0)
        def _():
            line_q(at, at).wait_recv()

        take_q(i)

    side = Z // 2 * slot

    def attend(n, group):
        rows = pl.ds(pl.multiple_of(group * side, side), side)

        def score(h):
            return lax.dot_general(qa[h, rows, :], ka[h, n], (((1,), (1,)), ((), ())), preferred_element_type=F32)

        def weigh(h, s):
            old = mx[h, rows, :][:, :1]
            m = jnp.maximum(old, jnp.max(s, axis=1, keepdims=True))
            o = jnp.dot(jnp.exp(s - m).astype(BF16), vx[h, n], preferred_element_type=F32)
            acc[h, rows, :] = acc[h, rows, :] * jnp.exp(old - m) + o
            mx[h, rows, :] = jnp.broadcast_to(m, (side, 128))

        s = score(0)
        for h in range(heads):
            later = score(h + 1) if h + 1 < heads else None
            weigh(h, s)
            s = later

    def twins(piece):
        each(Z, 0, lambda at: from_twin(piece, at).wait_recv())

    def line_o(to, at):
        return (remote(oh.at[to], ro.at[at], s_o.at[to], r_o.at[at], z=to),
                remote(sth.at[to], rst.at[at], s_t.at[to], r_t.at[at], z=to))

    def settle(i):
        at = (z + nth_near(i, Z)) % Z
        rows = pl.ds(pl.multiple_of(i * slot, slot), slot)
        stats = jnp.zeros((slot, 128), F32)
        for pair in range(pairs):
            outs = []
            for odd in range(2):
                mine = (half >= DH) if odd else (half < DH)
                head = 2 * pair + odd
                total = acc[head, rows, :]
                turned = pltpu.roll(total, DH, 1)
                l = jnp.where(mine, turned, total)
                outs.append(total / l)
                stats = jnp.where(half == head, mx[head, rows, :], jnp.where(half == 4 + head, l, stats))
            oh[at, :, pair * 128:pair * 128 + 128] = jnp.where(half < DH, outs[0], outs[1]).astype(BF16)
        sth[at] = jnp.transpose(stats)[:8]

    own_o = pltpu.make_async_copy(oh.at[z], ro.at[z], here.at[2])
    own_t = pltpu.make_async_copy(sth.at[z], rst.at[z], here.at[3])

    def settle_send(i):
        settle(i)
        at = (z + nth_near(i, Z)) % Z

        @pl.when(i == 0)
        def _():
            own_o.start()
            own_t.start()

        @pl.when(i > 0)
        def _():
            for copy in line_o(at, z):
                copy.start()

    mid_row = slot // 2

    def xring(who, at, send, recv, dev):
        part = attg.at[who, at]
        return remote(part, part, send.at[at], recv.at[at], x=dev)

    def xpass(who, at, piece, send, recv, dev):
        part = attg.at[who, at, pl.ds(piece * mid_row, mid_row)]
        return remote(part, part, send.at[at], recv.at[at], x=dev)

    xto_right = lambda at: xring(x, at, x_r, y_l, xright)
    xto_left = lambda at: xring(x, at, x_l, y_r, xleft)
    xfrom_left = lambda at: xring(xleft, at, x_r, y_l, xleft)
    xfrom_right = lambda at: xring(xright, at, x_l, y_r, xright)
    xpass_right = lambda at: xpass(xleft, at, 0, x_fr, y_fl, xright)
    xpass_left = lambda at: xpass(xright, at, 1, x_fl, y_fr, xleft)
    xfar_left = lambda at: xpass(xfar, at, 0, x_fr, y_fl, xleft)
    xfar_right = lambda at: xpass(xfar, at, 1, x_fl, y_fr, xright)

    def join(at):
        far_m, far_l = rst[at][0:4], rst[at][4:8]
        own_m, own_l = sts[at][0:4], sts[at][4:8]
        m = jnp.maximum(far_m, own_m)
        a = far_l * jnp.exp(far_m - m)
        b = own_l * jnp.exp(own_m - m)
        share = a / (a + b)
        wide = lax.dot_general(
            jnp.concatenate([share, jnp.zeros_like(share)], axis=0), widen, (((0,), (0,)), ((), ())),
            preferred_element_type=F32, precision=lax.Precision.HIGHEST)
        value = os[at] + wide * (ro[at].astype(F32) - os[at])
        attg[x, at] = value.astype(BF16)
        xto_right(at).start()
        xto_left(at).start()

    def home(i):
        return (z + Z - nth_near(i, Z)) % Z

    def arrive(i):
        at = home(i)

        @pl.when(i == 0)
        def _():
            own_o.wait()
            own_t.wait()

        @pl.when(i > 0)
        def _():
            for copy in line_o(at, at):
                copy.wait_recv()

        join(at)

    def forward(i):
        at = home(i)
        xfrom_left(at).wait_recv()
        xpass_right(at).start()
        xfrom_right(at).wait_recv()
        xpass_left(at).start()

    hz = Z // 2

    def main(t):
        group, n = t // Y, t % Y
        piece = jnp.where(n == 0, y, jnp.where(n == 1, left, jnp.where(n == 2, right, far)))

        @pl.when(n == 0)
        def _():
            rows = pl.ds(pl.multiple_of(group * side, side), side)
            for h in range(heads):
                acc[h, rows, :] = jnp.zeros((side, 128), F32)
                mx[h, rows, :] = jnp.full((side, 128), -3e38, F32)
            each(hz, 0, lambda i: wait_q(group * hz + i))

        @pl.when(t < Y)
        def _():
            twins(piece)
            build(n, piece)

        @pl.when(t == 0)
        def _():
            each(Z, Z - 3, step2)

        attend(n, group)

        @pl.when(t == 1)
        def _():
            each(Z, 0, step3)

        @pl.when(t == Y - 1)
        def _():
            each(hz, 0, settle_send)

        @pl.when(t == Y)
        def _():
            arrive(0)

        @pl.when(t == Y + 1)
        def _():
            each(hz, 1, arrive)

        @pl.when(t == Y + 2)
        def _():
            forward(0)

    each(2 * Y, 0, main)
    each(Z, hz, settle_send)
    each(hz, 1, forward)

    w_keep.wait()
    w_pass(xfar, 0, 4, 6, xleft).wait_recv()
    w_pass(xfar, 1, 5, 7, xright).wait_recv()
    width = xv.shape[2]
    row8 = lax.broadcasted_iota(jnp.int32, (8, slot), 0)

    give = lambda at: pltpu.make_async_copy(yown.at[at], upd.at[at], out_sem.at[at])

    def collect(i):
        at = home(i)
        xfar_left(at).wait_recv()
        xfar_right(at).wait_recv()
        place = order[at]
        rows = jnp.concatenate([attg[p, at] for p in range(X)], axis=1)
        value = jnp.dot(rows, w_all[...].reshape(X * cols, width), preferred_element_type=F32)
        ytmp[...] = value
        yown[at] = ytmp[:, pl.ds(pl.multiple_of(x * cols, cols), cols)]
        give(at).start()
        hidden = xv[place].astype(F32) + value
        square = jnp.sum(hidden * hidden, axis=1, keepdims=True)
        weighted = jnp.sum(hidden * (gain_ref[...] * read_ref[...]), axis=1, keepdims=True)
        score = weighted * lax.rsqrt(square / width + 1e-06)
        member = jnp.where((row8 < 2) & (segment(place) == row8), 1.0, 0.0)
        sums = jnp.dot(member, jnp.broadcast_to(score, (slot, 128)),
                       preferred_element_type=F32, precision=lax.Precision.HIGHEST)
        means[at] = sums / jnp.maximum(jnp.sum(member, axis=1, keepdims=True), 1.0)

    def late(i):
        collect(i - hz)
        arrive(i)

        @pl.when(i > Z // 2)
        def _():
            forward(i - 1)

    each(Z, hz, late)
    forward(Z - 1)
    each(Z, hz, collect)

    def finish(at):
        for copy in (xto_right(at), xto_left(at), xpass_right(at), xpass_left(at), to_right(at), to_left(at)):
            copy.wait_send()

        @pl.when(at % 2 == 0)
        def _():
            pass_right(at).wait_send()

        @pl.when(at % 2 == 1)
        def _():
            pass_left(at).wait_send()

        for piece in range(Y):
            to_twin(piece, at).wait_send()

    each(Z, 0, finish)
    for copy in (w_whole(x, 0, 2, xright), w_whole(x, 1, 3, xleft),
                 w_pass(xleft, 0, 4, 6, xright), w_pass(xright, 1, 5, 7, xleft)):
        copy.wait_send()

    def end_line(i):
        at = (z + i) % Z
        for copy in line_b(at, at) + line_o(at, at) + (line_q(at, at), line_g(at, at)):
            copy.wait_send()

    each(Z, 1, end_line)

    def end_cluster(i):
        to = (w + i) % W
        remote(abuf.at[to], abuf.at[to], s_a.at[to], r_a.at[to], y=to // C, c=to % C).wait_send()
        remote(cvar, va.at[to], s_va.at[to], r_va.at[to], y=to // C, c=to % C).wait_send()

    each(W, 1, end_cluster)
    each(Z, 0, lambda at: give(at).wait())


def order_kernel(sizes, dq, by_query, means, upd, pool, staged, sem):
    X, Y, Z, C = sizes
    blk = (lax.axis_index("y") * Z + lax.axis_index("z")) * C + lax.axis_index("c")
    copies = []
    for j in range(Z):
        query = dq[blk * 2 * Z + 2 * j]
        staged[j] = by_query[query]
        copies.append(pltpu.make_async_copy(staged.at[j], upd.at[j], sem.at[j]))
        copies[j].start()
    for j in range(Z):
        mean = means[dq[blk * 2 * Z + 2 * j]]
        for k in range(2):
            pool[2 * j + k] = mean[k, 0]
    for copy in copies:
        copy.wait()


def body(sizes, doc_x, doc_seg, doc_query, doc_var, query_len, block_perm, cache_k, cache_v, cache_var,
         w_query, w_key, w_value, w_out, var_bias, norm_gain, readout):
    X, Y, Z, C = sizes
    W = Y * C
    tokens, cols = doc_x.shape[0], w_query.shape[1]
    features = doc_x.shape[1]
    heads = cols // DH
    slot = tokens // Z
    crows = cache_k.shape[0]
    blocks = Y * Z * C
    bpq = blocks // Z
    piece = crows // (Y * Z)
    part_keys = bpq * slot
    i32 = jnp.int32
    dma = pltpu.SemaphoreType.DMA

    half_size = DH // 2
    frequency = 10000.0 ** (-np.arange(half_size) / half_size)
    frequency = np.tile(frequency.astype(np.float32), 128 // half_size)
    turns = np.arange(slot)[:, None] * frequency.astype(np.float64)[None, :]
    seg = doc_seg.reshape(Z, 1, slot)

    vm = lambda *shape: pltpu.VMEM(shape, BF16)
    vf = lambda *shape: pltpu.VMEM(shape, F32)
    vi = lambda *shape: pltpu.VMEM(shape, i32)
    smem = pl.BlockSpec(memory_space=pltpu.SMEM)
    vmem = pl.BlockSpec(memory_space=pltpu.VMEM)
    hbm = pl.BlockSpec(memory_space=ANY)
    by_query, means = pl.pallas_call(
        functools.partial(attention_kernel, sizes),
        in_specs=[smem] * 4 + [vmem] * 5 + [hbm] * 4 + [vmem] * 2 + [hbm] * 4,
        out_specs=[hbm, vmem],
        out_shape=[
            jax.ShapeDtypeStruct((Z, slot, cols), F32),
            jax.ShapeDtypeStruct((Z, 8, 128), F32),
        ],
        scratch_shapes=[
            vm(X, Z, slot, cols), vm(X, cols, features), vf(slot, features), vf(Z, slot, cols),
            pltpu.SMEM((blocks,), i32), vm(Z, slot, features), vm(features, cols), vm(features, cols), vm(features, cols),
            pltpu.SMEM((Z,), i32),
            vm(W, Z, piece, cols), vm(Z * W, piece, cols), vm(Z * bpq, piece, cols),
            vi(W, Y, 1, slot), vi(Z * W, Y, 1, slot),
            vm(C, Y, bpq, Z, piece, cols),
            vm(Z, slot, cols), vm(Z, slot, cols), vi(Z, 1, slot), vi(Z, 1, slot),
            vf(Z, slot, 128), vf(Z, slot, 128), vm(16, cols), vm(16, 128),
            vf(Z, slot, cols), vf(Z, 8, slot), vm(Y, part_keys, 128), vm(Z, slot, cols),
            vm(heads, Y, part_keys, 128), vm(heads, Y, part_keys, 128), vm(heads, tokens, 128),
            vf(heads, tokens, 128), vf(heads, tokens, 128),
            vm(Z, slot, cols), vf(Z, 8, slot), vm(Z, slot, cols), vf(Z, 8, slot),
            dma((4,)),
        ] + [dma((W,))] * 4 + [dma((Z,))] * 10 + [dma((Z,))] * 8 + [dma((Y, Z))] * 2
        + [dma((Z,))] * 4 + [dma((Z,))] * 8 + [dma((5,)), dma((9,)), dma((Z,))],
        compiler_params=pltpu.CompilerParams(
            collective_id=0, has_side_effects=True, vmem_limit_bytes=56 << 20),
        name="attention",
    )(block_perm, doc_query, query_len, var_bias, seg, doc_var.reshape(Z, 1, slot),
      jnp.asarray(np.cos(turns), F32), jnp.asarray(np.sin(turns), F32), jnp.asarray(frequency)[None, :],
      doc_x.reshape(Z, slot, features), w_query, w_key, w_value,
      norm_gain.reshape(1, features), readout.reshape(1, features),
      cache_k.reshape(Y, Z, piece, cols), cache_v.reshape(Y, Z, piece, cols), cache_var.reshape(Y, 1, slot), w_out)

    update, pooled = pl.pallas_call(
        functools.partial(order_kernel, sizes),
        in_specs=[smem, vmem, vmem],
        out_specs=[hbm, smem],
        out_shape=[
            jax.ShapeDtypeStruct((Z, slot, cols), F32),
            jax.ShapeDtypeStruct((2 * Z,), F32),
        ],
        scratch_shapes=[vf(Z, slot, cols), dma((Z,))],
        compiler_params=pltpu.CompilerParams(vmem_limit_bytes=60 << 20),
        name="slot_order",
    )(doc_query, by_query, means)
    return update.reshape(tokens, cols), pooled


def solution(mesh):
    heads = mesh.shape["head"]
    cores = 2
    across = 4
    along = mesh.shape["blk"] // (across * cores)
    sizes = (heads, across, along, cores)
    split = Mesh(mesh.devices.reshape(sizes), ("x", "y", "z", "c"))
    return jax.shard_map(
        functools.partial(body, sizes),
        mesh=split,
        in_specs=(
            P(BLK, None), P(BLK), P(), P(BLK), P(), P(),
            P(BLK, "x"), P(BLK, "x"), P(BLK),
            P(None, "x"), P(None, "x"), P(None, "x"), P("x", None), P(None, "x"),
            P(), P(),
        ),
        out_specs=(P(BLK, "x"), P(BLK)),
        check_vma=False,
    )
```
